32 devices in a mesh: groups: 2 (over x), wide: 8 (over z, y), narrow: 2 (over core).
Axes of the slice: x: 2, y: 2, z: 4, core: 2. Of those that a mesh axis runs over, the one named last changes fastest.
Arguments:
- features: bfloat16 [64, 16, 128, 256], P(('groups', 'wide'), 'narrow'), parts along dimension 0, may hold values from -6 to 6
- tile_ids: int32 [64, 16, 3], P(('groups', 'wide'), 'narrow'), parts along dimension 0, may hold values from 0 to 15
- tiles: bfloat16 [16, 128, 128], replicated, may hold values from -0.25 to 0.25
- w_first: bfloat16 [256, 256], replicated, may hold values from -0.375 to 0.375
- w_second: bfloat16 [256, 256], replicated, may hold values from -0.375 to 0.375
- readout: bfloat16 [256], replicated, may hold values from -0.375 to 0.375
- target: float32 [64, 16, 128], P(('groups', 'wide'), 'narrow'), parts along dimension 0, may hold values from -6 to 6
Outputs:
- pred: float32 [64, 16, 128], P(('groups', 'wide'), 'narrow'), parts along dimension 0
- grad_first: float32 [512, 256], P(('groups', 'wide', 'narrow')), parts along dimension 0
- grad_second: float32 [512, 256], P(('groups', 'wide', 'narrow')), parts along dimension 0
- grad_readout: float32 [512], P('groups'), parts along dimension 0
The draws below stay inside these ranges and needn't reach their ends.
There are 2 independent parts, one for each index of `groups`. The reference program is written for one: setup_inputs(seed, part) draws one part's arguments, and reference() takes and returns one part's arrays. A program takes and returns all parts, laid end to end along the dimension named above; an argument that names none is the same for every part. Nothing has to cross between parts.
All inputs are finite; a program needn't handle non-finite values.
Results may differ from the reference program's by a relative error of at most 0.0049.
Values may be sent and summed in bfloat16 or wider, within the bound.
No kernel may reach another device: no remote copies, remote signals or barrier semaphores. Data moves between devices by JAX's collectives and lax.ppermute only.
A program may use at most 128 MiB of HBM per device.

```python
import jax
import jax.numpy as jnp

H = 256
BLOCK = 128
TILES = 16
NBX = 32
NBY = 16
NODES = 65536


def plant(entries, key, least, largest):
    shape = entries.shape
    spot = [jax.random.randint(jax.random.fold_in(key, axis), (), 0, shape[axis]) for axis in range(len(shape))]
    entries = entries.at[tuple(spot)].set(least)
    longest = shape.index(max(shape))
    spot[longest] = (spot[longest] + 1) % shape[longest]
    return entries.at[tuple(spot)].set(largest)


def shard_levels(rng, dims, shards, least, largest):
    factor_of, own = 1.0, jax.random.fold_in(rng, 6)
    for dim, parts in shards:
        steps = jnp.exp(jax.random.uniform(jax.random.fold_in(own, dim), (parts,), jnp.float32, least / len(shards), largest / len(shards)))
        factor_of = factor_of * jnp.repeat(steps, dims[dim] // parts).reshape([-1 if axis == dim else 1 for axis in range(len(dims))])
    return factor_of


def noise(own_key, dims, width, most, cuts=(), kind=jnp.bfloat16):
    values = width * jax.random.normal(own_key, dims, jnp.float32)
    if cuts:
        values = values * shard_levels(own_key, dims, cuts, -0.22, 0.18)
    return jnp.clip(values, -most, most).astype(kind)


def setup_inputs(seed: int = 0, part: int = 0) -> dict:
    key_of = jax.random.split(jax.random.key(seed), 8)
    part_keys = jax.random.split(jax.random.fold_in(key_of[7], part), 8)
    return {
        "features": noise(part_keys[0], (NBX, NBY, BLOCK, H), 1.0, 6.0, ((0, 8), (1, 2))),
        "tile_ids": plant(jax.random.randint(part_keys[1], (NBX, NBY, 3), 0, TILES), jax.random.fold_in(part_keys[1], 1), 0, TILES - 1).astype(jnp.int32),
        "tiles": noise(key_of[2], (TILES, BLOCK, BLOCK), (5 * BLOCK) ** -0.5, 0.25),
        "w_first": noise(key_of[3], (H, H), H ** -0.5, 0.375),
        "w_second": noise(key_of[4], (H, H), H ** -0.5, 0.375),
        "readout": noise(key_of[5], (H,), H ** -0.5, 0.375),
        "target": noise(part_keys[6], (NBX, NBY, BLOCK), 1.0, 6.0, ((0, 8), (1, 2)), jnp.float32),
    }


def operate(padded, ids_pad, tiles):
    nx = padded.shape[0] - 2
    ny = padded.shape[1] - 2
    centre_ids = ids_pad[1:1 + nx, 1:1 + ny]
    west_ids = ids_pad[0:nx, 1:1 + ny, 1]
    south_ids = ids_pad[1:1 + nx, 0:ny, 2]
    table = tiles.astype(jnp.float32)
    field = padded.astype(jnp.float32)
    centre = field[1:-1, 1:-1]
    selfs = jnp.take(table, centre_ids[..., 0], axis=0)
    total = jnp.einsum('xynm,xymh->xynh', selfs, centre) + jnp.einsum('xymn,xymh->xynh', selfs, centre)
    east = jnp.take(table, centre_ids[..., 1], axis=0)
    total = total + jnp.einsum('xynm,xymh->xynh', east, field[2:, 1:-1])
    west = jnp.take(table, west_ids, axis=0)
    total = total + jnp.einsum('xymn,xymh->xynh', west, field[:-2, 1:-1])
    north = jnp.take(table, centre_ids[..., 2], axis=0)
    total = total + jnp.einsum('xynm,xymh->xynh', north, field[1:-1, 2:])
    south = jnp.take(table, south_ids, axis=0)
    total = total + jnp.einsum('xymn,xymh->xynh', south, field[1:-1, :-2])
    return total

def padfield(field):
    return jnp.pad(field, ((1, 1), (1, 1), (0, 0), (0, 0)))

def reference(features, tile_ids, tiles, w_first, w_second, readout, target):
    ids_pad = jnp.pad(tile_ids, ((1, 1), (1, 1), (0, 0)))
    m_one = operate(padfield(features), ids_pad, tiles).astype(jnp.bfloat16)
    z_one = jnp.einsum('xynh,hk->xynk', m_one.astype(jnp.float32), w_first.astype(jnp.float32))
    x_one = (features.astype(jnp.float32) + jnp.tanh(z_one)).astype(jnp.bfloat16)
    m_two = operate(padfield(x_one), ids_pad, tiles).astype(jnp.bfloat16)
    z_two = jnp.einsum('xynh,hk->xynk', m_two.astype(jnp.float32), w_second.astype(jnp.float32))
    x_two = (x_one.astype(jnp.float32) + jnp.tanh(z_two)).astype(jnp.bfloat16)
    readf = readout.astype(jnp.float32)
    pred = jnp.einsum('xynh,h->xyn', x_two.astype(jnp.float32), readf)
    scale = jnp.sqrt(jnp.float32(H) / jnp.float32(NODES))
    grad_pred = (pred - target) * scale
    grad_readout = jnp.einsum('xynh,xyn->h', x_two.astype(jnp.float32), grad_pred)
    grad_x_two = grad_pred[..., None] * readf
    tanh_two = jnp.tanh(z_two)
    grad_z_two = (grad_x_two * (1.0 - tanh_two * tanh_two)).astype(jnp.bfloat16)
    grad_second = jnp.dot(m_two.reshape(-1, H).T, grad_z_two.reshape(-1, H), preferred_element_type=jnp.float32)
    grad_m_two = jnp.einsum('xynk,hk->xynh', grad_z_two.astype(jnp.float32), w_second.astype(jnp.float32)).astype(jnp.bfloat16)
    grad_x_one = grad_x_two + operate(padfield(grad_m_two), ids_pad, tiles)
    tanh_one = jnp.tanh(z_one)
    grad_z_one = (grad_x_one * (1.0 - tanh_one * tanh_one)).astype(jnp.bfloat16)
    grad_first = jnp.dot(m_one.reshape(-1, H).T, grad_z_one.reshape(-1, H), preferred_element_type=jnp.float32)
    return (pred, grad_first, grad_second, grad_readout)
```

```python
import functools

import jax
import jax.numpy as jnp
import numpy as np
from jax import lax
from jax.experimental import pallas as pl
from jax.experimental.pallas import tpu as pltpu
from jax.sharding import PartitionSpec as P

F32 = jnp.float32
BF16 = jnp.bfloat16
AXES = ("wide", "narrow")
VMEM_LIMIT = 40 * 1024 * 1024
ANY = pl.BlockSpec(memory_space=pl.ANY)
VMEM = pl.BlockSpec(memory_space=pltpu.VMEM)
SMEM = pl.BlockSpec(memory_space=pltpu.SMEM)

SELF, EAST, WEST, NORTH, SOUTH, FLAGS = 0, 1, 2, 3, 4, 5


def routes(wide):
    depth = wide // 2

    def at(z, y, c):
        return (2 * z + y) * 2 + c

    every = [(z, y, c) for z in range(depth) for y in range(2) for c in range(2)]
    swap = [(at(z, c, y), at(z, y, c)) for z, y, c in every if y != c]
    first_side = [(at(z, c, 1 - y), at(z, y, c)) for z, y, c in every]
    inner = [(at(z, y, 1 - c), at(z, y, c)) for z, y, c in every]
    outer = [(at(z - 1, y, 1), at(z, y, 0)) for z, y, c in every if c == 0 and z > 0]
    outer += [(at(z + 1, y, 0), at(z, y, 1)) for z, y, c in every if c == 1 and z + 1 < depth]
    side = [(at(z, 1 - y, c), at(z, y, c)) for z, y, c in every]
    above = [(at(z, 0, y), at(z, y, 1)) for z, y, c in every if c == 1]
    above += [(at(z - 1, 1, y), at(z, y, 0)) for z, y, c in every if c == 0 and z > 0]
    left = [(at(z, c, 0), at(z, y, c)) for z, y, c in every if y == 1]
    return swap, first_side, inner, outer, side, above, left


def block_product(table, field, tiles, turned, row, col, rows, cols):
    at = row * cols + col
    step = rows * cols
    own = table[SELF * step + at]
    lhs = jnp.concatenate(
        [
            tiles[own],
            turned[own],
            tiles[table[EAST * step + at]],
            turned[table[WEST * step + at]],
            tiles[table[NORTH * step + at]],
            turned[table[SOUTH * step + at]],
        ],
        axis=1,
    )
    centre = field[row + 1, col + 1]
    rhs = jnp.concatenate(
        [
            centre,
            centre,
            field[row + 2, col + 1],
            field[row, col + 1],
            field[row + 1, col + 2],
            field[row + 1, col],
        ],
        axis=0,
    )
    return lax.dot_general(lhs, rhs, (((1,), (0,)), ((), ())), preferred_element_type=F32)


def rim_copies(table, field, inner, outer, side, sems, rows, cols):
    base = FLAGS * rows * cols
    low, right = table[base + 1], table[base + 2]
    bottom, end = rows + 1, cols + 1
    zero_col = jnp.where(right == 0, 0, end)
    side_col = jnp.where(right == 0, end, 0)
    for row in range(1, rows + 1):
        field[row, zero_col] = jnp.zeros(field.shape[2:], field.dtype)
    return [
        pltpu.make_async_copy(inner, field.at[jnp.where(low == 0, bottom, 0), pl.ds(1, cols)], sems.at[0]),
        pltpu.make_async_copy(outer, field.at[jnp.where(low == 0, 0, bottom), pl.ds(1, cols)], sems.at[1]),
        pltpu.make_async_copy(side, field.at[pl.ds(1, rows), side_col], sems.at[2]),
    ]


def edge_copies(table, done, inner, outer, side, sems, rows, cols):
    base = FLAGS * rows * cols
    low, right = table[base + 1], table[base + 2]
    return [
        pltpu.make_async_copy(done.at[jnp.where(low == 0, rows - 1, 0)], inner, sems.at[3]),
        pltpu.make_async_copy(done.at[jnp.where(low == 0, 0, rows - 1)], outer, sems.at[4]),
        pltpu.make_async_copy(done.at[:, jnp.where(right == 0, cols - 1, 0)], side, sems.at[5]),
    ]


def first_kernel(rows, cols, table, own, ends, middle, inner, outer, side, tiles, turned, weight,
                 x_out, m_out, inner_out, outer_out, side_out, field, x_new, m_new, sems):
    nodes, width = own.shape[2], own.shape[3]
    moving = table[FLAGS * rows * cols]
    inside = pl.ds(1, cols)
    copies = rim_copies(table, field, inner, outer, side, sems, rows, cols)
    for copy in copies:
        copy.start()

    @pl.when(moving == 0)
    def _():
        copy = pltpu.make_async_copy(own, field.at[pl.ds(1, rows), inside], sems.at[6])
        copy.start()
        copy.wait()

    @pl.when(moving != 0)
    def _():
        parts = [
            pltpu.make_async_copy(ends.at[0], field.at[1, inside], sems.at[6]),
            pltpu.make_async_copy(ends.at[1], field.at[rows, inside], sems.at[7]),
            pltpu.make_async_copy(middle, field.at[pl.ds(2, rows - 2), inside], sems.at[8]),
        ]
        for part in parts:
            part.start()
        for part in parts:
            part.wait()

    for copy in copies:
        copy.wait()

    def one_row(row, carry):
        for col in range(cols):
            m_new[row, col] = block_product(table, field, tiles, turned, row, col, rows, cols).astype(BF16)
        for col in range(0, cols, 2):
            m_part = m_new[row, pl.ds(col, 2)].reshape(2 * nodes, width)
            z = jnp.dot(m_part, weight[...], preferred_element_type=F32)
            base = field[row + 1, pl.ds(1 + col, 2)].reshape(2 * nodes, width)
            x_new[row, pl.ds(col, 2)] = (base.astype(F32) + jnp.tanh(z)).astype(BF16).reshape(2, nodes, width)
        return carry

    lax.fori_loop(0, rows, one_row, 0)
    outs = edge_copies(table, x_new, inner_out, outer_out, side_out, sems, rows, cols)
    outs += [
        pltpu.make_async_copy(x_new, x_out, sems.at[0]),
        pltpu.make_async_copy(m_new, m_out, sems.at[1]),
    ]
    for copy in outs:
        copy.start()
    for copy in outs:
        copy.wait()


def second_kernel(rows, cols, scale, table, x_own, inner, outer, side, tiles, turned, weight, readout,
                  spread, target, g_out, inner_out, outer_out, side_out, pred_out, second_out, readout_out,
                  field, g_new, m_row, gz_row, sems):
    nodes, width = x_own.shape[2], x_own.shape[3]
    copies = rim_copies(table, field, inner, outer, side, sems, rows, cols)
    copies.append(pltpu.make_async_copy(x_own, field.at[pl.ds(1, rows), pl.ds(1, cols)], sems.at[6]))
    for copy in copies:
        copy.start()
    for copy in copies:
        copy.wait()
    readf = readout[...]
    lanes = lax.broadcasted_iota(jnp.int32, (nodes, 128), 1)
    second_out[...] = jnp.zeros_like(second_out)
    readout_out[...] = jnp.zeros_like(readout_out)

    def one_row(row, carry):
        goal = target[row].T
        seen = jnp.zeros((nodes, 128), F32)
        for col in range(cols):
            m_row[col] = block_product(table, field, tiles, turned, row, col, rows, cols).astype(BF16)
        for col in range(cols):
            z = jnp.dot(m_row[col], weight[...], preferred_element_type=F32)
            t = jnp.tanh(z)
            x = (field[row + 1, col + 1].astype(F32) + t).astype(BF16)
            pred = jnp.dot(x, spread[...], preferred_element_type=F32)
            seen = jnp.where(lanes == col, pred, seen)
            gp = (pred[:, 0:1] - goal[:, col : col + 1]) * scale
            part = x.astype(F32) * gp
            readout_out[...] += part.reshape(nodes // 8, 8, width).sum(axis=0)
            gz = (gp * readf * (1.0 - t * t)).astype(BF16)
            gz_row[col] = gz
            g_new[row, col] = lax.dot_general(
                gz, weight[...], (((1,), (1,)), ((), ())), preferred_element_type=F32
            ).astype(BF16)
        second_out[...] += lax.dot_general(
            m_row[...].reshape(cols * nodes, width), gz_row[...].reshape(cols * nodes, width),
            (((0,), (0,)), ((), ())), preferred_element_type=F32,
        )
        pred_out[row] = seen.T[0:cols]
        return carry

    lax.fori_loop(0, rows, one_row, 0)
    outs = edge_copies(table, g_new, inner_out, outer_out, side_out, sems, rows, cols)
    outs.append(pltpu.make_async_copy(g_new, g_out, sems.at[0]))
    for copy in outs:
        copy.start()
    for copy in outs:
        copy.wait()


def third_kernel(rows, cols, scale, table, g_own, inner, outer, side, tiles, turned, m_own, weight, readout,
                 pred, target, first_out, field, m_in, gz_row, sems):
    nodes, width = g_own.shape[2], g_own.shape[3]
    copies = rim_copies(table, field, inner, outer, side, sems, rows, cols)
    copies.append(pltpu.make_async_copy(g_own, field.at[pl.ds(1, rows), pl.ds(1, cols)], sems.at[6]))
    copies.append(pltpu.make_async_copy(m_own, m_in, sems.at[7]))
    for copy in copies:
        copy.start()
    for copy in copies:
        copy.wait()
    readf = readout[...]
    first_out[...] = jnp.zeros_like(first_out)

    def one_row(row, carry):
        gp_all = ((pred[row] - target[row]) * scale).T
        for col in range(cols):
            gx = gp_all[:, col : col + 1] * readf
            gx = gx + block_product(table, field, tiles, turned, row, col, rows, cols)
            t = jnp.tanh(jnp.dot(m_in[row, col], weight[...], preferred_element_type=F32))
            gz_row[col] = (gx * (1.0 - t * t)).astype(BF16)
        first_out[...] += lax.dot_general(
            m_in[row].reshape(cols * nodes, width), gz_row[...].reshape(cols * nodes, width),
            (((0,), (0,)), ((), ())), preferred_element_type=F32,
        )
        return carry

    lax.fori_loop(0, rows, one_row, 0)


def sum_shares(slots, extra, count):
    place = lax.axis_index(AXES)
    bit = 1
    while bit < count:
        route = [(i, i ^ bit) for i in range(count)]
        mine = (place // bit) % 2
        pairs = slots.reshape(slots.shape[0] // 2, 2, *slots.shape[1:])
        keep = lax.dynamic_index_in_dim(pairs, mine, 1, keepdims=False)
        send = lax.dynamic_index_in_dim(pairs, 1 - mine, 1, keepdims=False)
        load = jnp.concatenate([send.reshape(-1, send.shape[-1]), extra], axis=0)
        got = lax.ppermute(load, AXES, route)
        cut = load.shape[0] - extra.shape[0]
        slots = keep + got[:cut].reshape(keep.shape)
        extra = extra + got[cut:]
        bit *= 2
    return slots[0], extra


def per_device(features, tile_ids, tiles, w_first, w_second, readout, target):
    rows, cols, nodes, width = features.shape
    wide, narrow = lax.axis_size("wide"), lax.axis_size("narrow")
    count = wide * narrow
    swap, first_side, inner_way, outer_way, side_way, above_way, left_way = routes(wide)
    y = lax.axis_index("wide") % 2
    c = lax.axis_index("narrow")
    moving = (y != c).astype(jnp.int32)
    scale = float(np.sqrt(np.float32(width) / np.float32(rows * cols * nodes * count)))

    def send(value, way):
        return lax.ppermute(value, AXES, way)

    def edges(inner, outer, side):
        return send(inner, inner_way), send(outer, outer_way), send(side, side_way)

    ends = send(jnp.concatenate([features[0:1], features[rows - 1 : rows]], axis=0), swap)
    side = send(jnp.where(c == 1, features[:, 0], features[:, cols - 1]), first_side)
    middle = send(features[1 : rows - 1], swap)
    ids_swap = send(tile_ids, swap)
    above_ids = send(tile_ids[rows - 1, :, 1], above_way)
    left_ids = send(tile_ids[:, cols - 1, 2], left_way)
    goal_swap = send(target, swap)

    ids = jnp.where(moving == 1, ids_swap, tile_ids)
    goal = jnp.where(moving == 1, goal_swap, target)
    west = jnp.concatenate([above_ids[None], ids[: rows - 1, :, 1]], axis=0)
    south = jnp.concatenate([left_ids[:, None], ids[:, : cols - 1, 2]], axis=1)
    table = jnp.concatenate(
        [
            jnp.stack([ids[:, :, 0], ids[:, :, 1], west, ids[:, :, 2], south]).reshape(-1),
            jnp.stack([moving, c, y]).astype(jnp.int32),
        ]
    )
    turned = jnp.swapaxes(tiles, 1, 2)
    readf = readout.astype(F32)[None]
    spread = jnp.broadcast_to(readout[:, None], (width, 128))

    top = jnp.where(moving == 1, ends[0], features[0])
    low = jnp.where(moving == 1, ends[1], features[rows - 1])
    inner = send(jnp.where(c == 0, low, top), inner_way)
    outer = send(jnp.where(c == 0, top, low), outer_way)

    patch = jax.ShapeDtypeStruct(features.shape, BF16)
    line = jax.ShapeDtypeStruct((cols, nodes, width), BF16)
    column = jax.ShapeDtypeStruct((rows, nodes, width), BF16)
    square = jax.ShapeDtypeStruct((width, width), F32)
    rim = pltpu.VMEM((rows + 2, cols + 2, nodes, width), BF16)
    whole = pltpu.VMEM(features.shape, BF16)
    strip = pltpu.VMEM((cols, nodes, width), BF16)
    sems = pltpu.SemaphoreType.DMA((9,))
    params = pltpu.CompilerParams(vmem_limit_bytes=VMEM_LIMIT)
    product = 2 * rows * cols * nodes * width * (6 * nodes)
    dense = 2 * rows * cols * nodes * width * width
    moved = features.size * 2

    x_one, m_one, inner_s, outer_s, side_s = pl.pallas_call(
        functools.partial(first_kernel, rows, cols),
        out_shape=(patch, patch, line, line, column),
        in_specs=[SMEM] + [ANY] * 6 + [VMEM] * 3,
        out_specs=(ANY,) * 5,
        scratch_shapes=[rim, whole, whole, sems],
        compiler_params=params,
        cost_estimate=pl.CostEstimate(flops=product + dense, bytes_accessed=4 * moved, transcendentals=features.size),
        name="layer_one",
    )(table, features, ends, middle, inner, outer, side, tiles, turned, w_first)

    inner, outer, side = edges(inner_s, outer_s, side_s)
    g_two, inner_s, outer_s, side_s, pred, second, readout_part = pl.pallas_call(
        functools.partial(second_kernel, rows, cols, scale),
        out_shape=(patch, line, line, column, jax.ShapeDtypeStruct(target.shape, F32), square,
                   jax.ShapeDtypeStruct((8, width), F32)),
        in_specs=[SMEM] + [ANY] * 4 + [VMEM] * 6,
        out_specs=(ANY,) * 4 + (VMEM,) * 3,
        scratch_shapes=[rim, whole, strip, strip, sems],
        compiler_params=params,
        cost_estimate=pl.CostEstimate(flops=product + 3 * dense, bytes_accessed=3 * moved, transcendentals=features.size),
        name="layer_two",
    )(table, x_one, inner, outer, side, tiles, turned, w_second, readf, spread, goal)

    inner, outer, side = edges(inner_s, outer_s, side_s)
    first = pl.pallas_call(
        functools.partial(third_kernel, rows, cols, scale),
        out_shape=square,
        in_specs=[SMEM] + [ANY] * 4 + [VMEM] * 2 + [ANY] + [VMEM] * 4,
        out_specs=VMEM,
        scratch_shapes=[rim, whole, strip, sems],
        compiler_params=params,
        cost_estimate=pl.CostEstimate(flops=product + 2 * dense, bytes_accessed=3 * moved, transcendentals=features.size),
        name="layer_one_back",
    )(table, g_two, inner, outer, side, tiles, turned, m_one, w_first, readf, pred, goal)

    share = width // count
    slots = jnp.concatenate([first.reshape(count, share, width), second.reshape(count, share, width)], axis=1)
    mine, extra = sum_shares(slots, readout_part, count)
    pred = jnp.where(moving == 1, send(pred, swap), pred)
    return pred, mine[:share], mine[share:], extra.sum(axis=0)


def solution(mesh):
    in_specs = (
        P(("groups", "wide"), "narrow", None, None),
        P(("groups", "wide"), "narrow", None),
        P(),
        P(),
        P(),
        P(),
        P(("groups", "wide"), "narrow", None),
    )
    out_specs = (
        P(("groups", "wide"), "narrow", None),
        P(("groups", "wide", "narrow"), None),
        P(("groups", "wide", "narrow"), None),
        P("groups"),
    )
    return jax.shard_map(
        per_device, mesh=mesh, in_specs=in_specs, out_specs=out_specs, check_vma=False
    )
```

```python
import functools

import jax
import jax.numpy as jnp
import numpy as np
from jax import lax
from jax.experimental import pallas as pl
from jax.experimental.pallas import tpu as pltpu
from jax.sharding import PartitionSpec as P

F32 = jnp.float32
BF16 = jnp.bfloat16
AXES = ("wide", "narrow")
VMEM_LIMIT = 20 * 1024 * 1024
BIG_VMEM = 60 * 1024 * 1024
ANY = pl.BlockSpec(memory_space=pl.ANY)
VMEM = pl.BlockSpec(memory_space=pltpu.VMEM)
HBM = pl.BlockSpec(memory_space=pltpu.HBM)
SMEM = pl.BlockSpec(memory_space=pltpu.SMEM)

SELF, EAST, WEST, NORTH, SOUTH, FLAGS = 0, 1, 2, 3, 4, 5


def routes(wide):
    depth = wide // 2

    def at(z, y, c):
        return (2 * z + y) * 2 + c

    every = [(z, y, c) for z in range(depth) for y in range(2) for c in range(2)]
    swap = [(at(z, c, y), at(z, y, c)) for z, y, c in every if y != c]
    first_side = [(at(z, c, 1 - y), at(z, y, c)) for z, y, c in every]
    inner = [(at(z, y, 1 - c), at(z, y, c)) for z, y, c in every]
    outer = [(at(z - 1, y, 1), at(z, y, 0)) for z, y, c in every if c == 0 and z > 0]
    outer += [(at(z + 1, y, 0), at(z, y, 1)) for z, y, c in every if c == 1 and z + 1 < depth]
    side = [(at(z, 1 - y, c), at(z, y, c)) for z, y, c in every]
    above = [(at(z, 0, y), at(z, y, 1)) for z, y, c in every if c == 1]
    above += [(at(z - 1, 1, y), at(z, y, 0)) for z, y, c in every if c == 0 and z > 0]
    left = [(at(z, c, 0), at(z, y, c)) for z, y, c in every if y == 1]
    return swap, first_side, inner, outer, side, above, left


def block_product(table, field, tiles, turned, row, col, rows, cols):
    at = row * cols + col
    step = rows * cols
    own = table[SELF * step + at]
    lhs = jnp.concatenate(
        [
            tiles[own],
            turned[own],
            tiles[table[EAST * step + at]],
            turned[table[WEST * step + at]],
            tiles[table[NORTH * step + at]],
            turned[table[SOUTH * step + at]],
        ],
        axis=1,
    )
    centre = field[row + 1, col + 1]
    rhs = jnp.concatenate(
        [
            centre,
            centre,
            field[row + 2, col + 1],
            field[row, col + 1],
            field[row + 1, col + 2],
            field[row + 1, col],
        ],
        axis=0,
    )
    return lax.dot_general(lhs, rhs, (((1,), (0,)), ((), ())), preferred_element_type=F32)


def rim_copies(table, field, inner, outer, side, sems, rows, cols):
    base = FLAGS * rows * cols
    low, right = table[base + 1], table[base + 2]
    bottom, end = rows + 1, cols + 1
    zero_col = jnp.where(right == 0, 0, end)
    side_col = jnp.where(right == 0, end, 0)
    for row in range(1, rows + 1):
        field[row, zero_col] = jnp.zeros(field.shape[2:], field.dtype)
    return [
        pltpu.make_async_copy(inner, field.at[jnp.where(low == 0, bottom, 0), pl.ds(1, cols)], sems.at[0]),
        pltpu.make_async_copy(outer, field.at[jnp.where(low == 0, 0, bottom), pl.ds(1, cols)], sems.at[1]),
        pltpu.make_async_copy(side, field.at[pl.ds(1, rows), side_col], sems.at[2]),
    ]


def edge_copies(table, done, inner, outer, side, sems, rows, cols):
    base = FLAGS * rows * cols
    low, right = table[base + 1], table[base + 2]
    return [
        pltpu.make_async_copy(done.at[jnp.where(low == 0, rows - 1, 0)], inner, sems.at[3]),
        pltpu.make_async_copy(done.at[jnp.where(low == 0, 0, rows - 1)], outer, sems.at[4]),
        pltpu.make_async_copy(done.at[:, jnp.where(right == 0, cols - 1, 0)], side, sems.at[5]),
    ]


def pack_kernel(rows, cols, flags, own, ends, side, sems):
    copies = [
        pltpu.make_async_copy(own.at[0], ends.at[0], sems.at[0]),
        pltpu.make_async_copy(own.at[rows - 1], ends.at[1], sems.at[1]),
        pltpu.make_async_copy(own.at[:, jnp.where(flags[1] == 1, 0, cols - 1)], side, sems.at[2]),
    ]
    for copy in copies:
        copy.start()
    for copy in copies:
        copy.wait()


def middle_kernel(rows, own, after, middle, sem):
    copy = pltpu.make_async_copy(own.at[pl.ds(1, rows - 2)], middle, sem)
    copy.start()
    copy.wait()


def turn_kernel(tiles, plain, turned, sem):
    copy = pltpu.make_async_copy(tiles, plain, sem)
    copy.start()
    copy.wait()

    def one_tile(tile, carry):
        turned[tile] = plain[tile].T
        return carry

    lax.fori_loop(0, tiles.shape[0], one_tile, 0)


def first_kernel(rows, cols, table, own, ends, middle, inner, outer, side, tiles, turned, weight,
                 x_out, m_out, inner_out, outer_out, side_out, field, x_new, m_new, sems):
    nodes, width = own.shape[2], own.shape[3]
    moving = table[FLAGS * rows * cols]
    inside = pl.ds(1, cols)
    copies = rim_copies(table, field, inner, outer, side, sems, rows, cols)
    for copy in copies:
        copy.start()

    @pl.when(moving == 0)
    def _():
        copy = pltpu.make_async_copy(own, field.at[pl.ds(1, rows), inside], sems.at[6])
        copy.start()
        copy.wait()

    @pl.when(moving != 0)
    def _():
        parts = [
            pltpu.make_async_copy(ends.at[0], field.at[1, inside], sems.at[6]),
            pltpu.make_async_copy(ends.at[1], field.at[rows, inside], sems.at[7]),
            pltpu.make_async_copy(middle, field.at[pl.ds(2, rows - 2), inside], sems.at[8]),
        ]
        for part in parts:
            part.start()
        for part in parts:
            part.wait()

    for copy in copies:
        copy.wait()

    def one_row(row, carry):
        for col in range(cols):
            m_new[row, col] = block_product(table, field, tiles, turned, row, col, rows, cols).astype(BF16)
        for col in range(0, cols, 2):
            m_part = m_new[row, pl.ds(col, 2)].reshape(2 * nodes, width)
            z = jnp.dot(m_part, weight[...], preferred_element_type=F32)
            base = field[row + 1, pl.ds(1 + col, 2)].reshape(2 * nodes, width)
            x_new[row, pl.ds(col, 2)] = (base.astype(F32) + jnp.tanh(z)).astype(BF16).reshape(2, nodes, width)
        return carry

    lax.fori_loop(0, rows, one_row, 0)
    outs = edge_copies(table, x_new, inner_out, outer_out, side_out, sems, rows, cols)
    outs += [
        pltpu.make_async_copy(x_new, x_out, sems.at[0]),
        pltpu.make_async_copy(m_new, m_out, sems.at[1]),
    ]
    for copy in outs:
        copy.start()
    for copy in outs:
        copy.wait()


def second_kernel(rows, cols, scale, table, x_own, inner, outer, side, tiles, turned, weight, readout,
                  spread, target, g_out, inner_out, outer_out, side_out, pred_out, second_out, readout_out,
                  field, g_new, m_row, gz_row, sems):
    nodes, width = x_own.shape[2], x_own.shape[3]
    copies = rim_copies(table, field, inner, outer, side, sems, rows, cols)
    copies.append(pltpu.make_async_copy(x_own, field.at[pl.ds(1, rows), pl.ds(1, cols)], sems.at[6]))
    for copy in copies:
        copy.start()
    for copy in copies:
        copy.wait()
    readf = readout[...]
    lanes = lax.broadcasted_iota(jnp.int32, (nodes, 128), 1)
    second_out[...] = jnp.zeros_like(second_out)
    readout_out[...] = jnp.zeros_like(readout_out)

    def one_row(row, carry):
        goal = target[row].T
        seen = jnp.zeros((nodes, 128), F32)
        for col in range(cols):
            m_row[col] = block_product(table, field, tiles, turned, row, col, rows, cols).astype(BF16)
        for col in range(cols):
            z = jnp.dot(m_row[col], weight[...], preferred_element_type=F32)
            t = jnp.tanh(z)
            x = (field[row + 1, col + 1].astype(F32) + t).astype(BF16)
            pred = jnp.dot(x, spread[...], preferred_element_type=F32)
            seen = jnp.where(lanes == col, pred, seen)
            gp = (pred[:, 0:1] - goal[:, col : col + 1]) * scale
            part = x.astype(F32) * gp
            readout_out[...] += part.reshape(nodes // 8, 8, width).sum(axis=0)
            gz = (gp * readf * (1.0 - t * t)).astype(BF16)
            gz_row[col] = gz
            g_new[row, col] = lax.dot_general(
                gz, weight[...], (((1,), (1,)), ((), ())), preferred_element_type=F32
            ).astype(BF16)
        second_out[...] += lax.dot_general(
            m_row[...].reshape(cols * nodes, width), gz_row[...].reshape(cols * nodes, width),
            (((0,), (0,)), ((), ())), preferred_element_type=F32,
        )
        pred_out[row] = seen.T[0:cols]
        return carry

    lax.fori_loop(0, rows, one_row, 0)
    outs = edge_copies(table, g_new, inner_out, outer_out, side_out, sems, rows, cols)
    outs.append(pltpu.make_async_copy(g_new, g_out, sems.at[0]))
    for copy in outs:
        copy.start()
    for copy in outs:
        copy.wait()


def spread_shares(parts, extra, digit, outs):
    size = parts.shape[1]
    for k, out in enumerate(outs):
        for group in range(parts.shape[0] // 4):
            out[group * size : (group + 1) * size] = parts[4 * group + jnp.bitwise_xor(digit, k)]
        out[out.shape[0] - 8 :] = extra


def fold_kernel(base, flags, keep, one, two, three, *refs):
    digit = lax.rem(flags[3] // base, 4)
    parts = refs[-1]
    count, size, width = parts.shape
    total = keep[...] + one[...] + two[...] + three[...]
    parts[...] = total[: count * size].reshape(count, size, width)
    spread_shares(parts, total[count * size :], digit, refs[:-1])


def last_fold_kernel(keep, one, two, three, first, second, readout):
    share = first.shape[0]
    total = keep[...] + one[...] + two[...] + three[...]
    first[...] = total[:share]
    second[...] = total[share : 2 * share]
    readout[...] = total[2 * share :].sum(axis=0, keepdims=True)


def third_kernel(rows, cols, scale, table, g_own, inner, outer, side, tiles, turned, m_own, weight, readout,
                 pred, target, second, extra, keep, one, two, three, first_out, parts, field, m_in, gz_row, sems):
    nodes, width = g_own.shape[2], g_own.shape[3]
    copies = rim_copies(table, field, inner, outer, side, sems, rows, cols)
    copies.append(pltpu.make_async_copy(g_own, field.at[pl.ds(1, rows), pl.ds(1, cols)], sems.at[6]))
    copies.append(pltpu.make_async_copy(m_own, m_in, sems.at[7]))
    for copy in copies:
        copy.start()
    for copy in copies:
        copy.wait()
    readf = readout[...]
    first_out[...] = jnp.zeros_like(first_out)

    def one_row(row, carry):
        gp_all = ((pred[row] - target[row]) * scale).T
        for col in range(cols):
            gx = gp_all[:, col : col + 1] * readf
            gx = gx + block_product(table, field, tiles, turned, row, col, rows, cols)
            t = jnp.tanh(jnp.dot(m_in[row, col], weight[...], preferred_element_type=F32))
            gz_row[col] = (gx * (1.0 - t * t)).astype(BF16)
        first_out[...] += lax.dot_general(
            m_in[row].reshape(cols * nodes, width), gz_row[...].reshape(cols * nodes, width),
            (((0,), (0,)), ((), ())), preferred_element_type=F32,
        )
        return carry

    lax.fori_loop(0, rows, one_row, 0)
    count, size, _ = parts.shape
    parts[:, : size // 2] = first_out[...].reshape(count, size // 2, width)
    parts[:, size // 2 :] = second[...].reshape(count, size // 2, width)
    digit = lax.rem(table[FLAGS * rows * cols + 3], 4)
    spread_shares(parts, extra[...], digit, (keep, one, two, three))


def shares_shape(groups, size, width):
    return (jax.ShapeDtypeStruct((groups * size + 8, width), F32),) * 4


def sum_shares(flags, outs, count, share, width, params):
    base, groups = 1, count // 4
    while True:
        got = [
            lax.ppermute(outs[k], AXES, [(i, i ^ (k * base)) for i in range(count)]) for k in (1, 2, 3)
        ]
        if groups == 1:
            break
        base *= 4
        outs = pl.pallas_call(
            functools.partial(fold_kernel, base),
            out_shape=shares_shape(groups // 4, 2 * share, width),
            in_specs=[SMEM] + [VMEM] * 4,
            out_specs=(VMEM,) * 4,
            scratch_shapes=[pltpu.VMEM((groups, 2 * share, width), F32)],
            compiler_params=params,
            name="fold",
        )(flags, outs[0], *got)
        groups //= 4
    small = jax.ShapeDtypeStruct((share, width), F32)
    return pl.pallas_call(
        last_fold_kernel,
        out_shape=(small, small, jax.ShapeDtypeStruct((1, width), F32)),
        in_specs=[VMEM] * 4,
        out_specs=(VMEM,) * 3,
        compiler_params=params,
        name="last_fold",
    )(outs[0], *got)


def per_device(features, tile_ids, tiles, w_first, w_second, readout, target):
    rows, cols, nodes, width = features.shape
    wide, narrow = lax.axis_size("wide"), lax.axis_size("narrow")
    count = wide * narrow
    swap, first_side, inner_way, outer_way, side_way, above_way, left_way = routes(wide)
    y = lax.axis_index("wide") % 2
    c = lax.axis_index("narrow")
    moving = (y != c).astype(jnp.int32)
    scale = float(np.sqrt(np.float32(width) / np.float32(rows * cols * nodes * count)))

    def send(value, way):
        return lax.ppermute(value, AXES, way)

    def edges(inner, outer, side):
        return send(inner, inner_way), send(outer, outer_way), send(side, side_way)

    params = pltpu.CompilerParams(vmem_limit_bytes=VMEM_LIMIT)
    patch = jax.ShapeDtypeStruct(features.shape, BF16)
    line = jax.ShapeDtypeStruct((cols, nodes, width), BF16)
    column = jax.ShapeDtypeStruct((rows, nodes, width), BF16)
    flags = jnp.stack([moving, c, y, lax.axis_index(AXES)]).astype(jnp.int32)
    ends_s, side_s = pl.pallas_call(
        functools.partial(pack_kernel, rows, cols),
        out_shape=(jax.ShapeDtypeStruct((2, cols, nodes, width), BF16), column),
        in_specs=[SMEM, HBM],
        out_specs=(HBM,) * 2,
        scratch_shapes=[pltpu.SemaphoreType.DMA((3,))],
        compiler_params=pltpu.CompilerParams(vmem_limit_bytes=BIG_VMEM),
        name="pack",
    )(flags, features)
    ends = send(ends_s, swap)
    side = send(side_s, first_side)
    middle_s = pl.pallas_call(
        functools.partial(middle_kernel, rows),
        out_shape=jax.ShapeDtypeStruct((rows - 2, cols, nodes, width), BF16),
        in_specs=[HBM, HBM],
        out_specs=HBM,
        scratch_shapes=[pltpu.SemaphoreType.DMA],
        compiler_params=params,
        name="pack_middle",
    )(features, side)
    middle = send(middle_s, swap)
    tile_ids, target, tiles, _ = lax.optimization_barrier((tile_ids, target, tiles, middle_s))
    ids_swap = send(tile_ids, swap)
    above_ids = send(tile_ids[rows - 1, :, 1], above_way)
    left_ids = send(tile_ids[:, cols - 1, 2], left_way)
    goal_swap = send(target, swap)

    ids = jnp.where(moving == 1, ids_swap, tile_ids)
    goal = jnp.where(moving == 1, goal_swap, target)
    west = jnp.concatenate([above_ids[None], ids[: rows - 1, :, 1]], axis=0)
    south = jnp.concatenate([left_ids[:, None], ids[:, : cols - 1, 2]], axis=1)
    table = jnp.concatenate(
        [
            jnp.stack([ids[:, :, 0], ids[:, :, 1], west, ids[:, :, 2], south]).reshape(-1),
            flags,
        ]
    )
    tiles, turned = pl.pallas_call(
        turn_kernel,
        out_shape=(jax.ShapeDtypeStruct(tiles.shape, BF16),) * 2,
        in_specs=[HBM],
        out_specs=(VMEM,) * 2,
        scratch_shapes=[pltpu.SemaphoreType.DMA],
        compiler_params=params,
        name="turn",
    )(tiles)
    readf = readout.astype(F32)[None]
    spread = jnp.broadcast_to(readout[:, None], (width, 128))

    top = jnp.where(moving == 1, ends[0], features[0])
    low = jnp.where(moving == 1, ends[1], features[rows - 1])
    inner = send(jnp.where(c == 0, low, top), inner_way)
    outer = send(jnp.where(c == 0, top, low), outer_way)

    square = jax.ShapeDtypeStruct((width, width), F32)
    rim = pltpu.VMEM((rows + 2, cols + 2, nodes, width), BF16)
    whole = pltpu.VMEM(features.shape, BF16)
    strip = pltpu.VMEM((cols, nodes, width), BF16)
    sems = pltpu.SemaphoreType.DMA((9,))
    product = 2 * rows * cols * nodes * width * (6 * nodes)
    dense = 2 * rows * cols * nodes * width * width
    moved = features.size * 2

    x_one, m_one, inner_s, outer_s, side_s = pl.pallas_call(
        functools.partial(first_kernel, rows, cols),
        out_shape=(patch, patch, line, line, column),
        in_specs=[SMEM] + [ANY] * 6 + [VMEM] * 3,
        out_specs=(ANY,) * 5,
        scratch_shapes=[rim, whole, whole, sems],
        compiler_params=params,
        cost_estimate=pl.CostEstimate(flops=product + dense, bytes_accessed=4 * moved, transcendentals=features.size),
        name="layer_one",
    )(table, features, ends, middle, inner, outer, side, tiles, turned, w_first)

    inner, outer, side = edges(inner_s, outer_s, side_s)
    g_two, inner_s, outer_s, side_s, pred, second, readout_part = pl.pallas_call(
        functools.partial(second_kernel, rows, cols, scale),
        out_shape=(patch, line, line, column, jax.ShapeDtypeStruct(target.shape, F32), square,
                   jax.ShapeDtypeStruct((8, width), F32)),
        in_specs=[SMEM] + [ANY] * 4 + [VMEM] * 6,
        out_specs=(ANY,) * 4 + (VMEM,) * 3,
        scratch_shapes=[rim, whole, strip, strip, sems],
        compiler_params=params,
        cost_estimate=pl.CostEstimate(flops=product + 3 * dense, bytes_accessed=3 * moved, transcendentals=features.size),
        name="layer_two",
    )(table, x_one, inner, outer, side, tiles, turned, w_second, readf, spread, goal)

    inner, outer, side = edges(inner_s, outer_s, side_s)
    pred_out = jnp.where(moving == 1, send(pred, swap), pred)
    pred_out, side = lax.optimization_barrier((pred_out, side))
    share = width // count
    outs = pl.pallas_call(
        functools.partial(third_kernel, rows, cols, scale),
        out_shape=shares_shape(count // 4, 2 * share, width),
        in_specs=[SMEM] + [ANY] * 4 + [VMEM] * 2 + [ANY] + [VMEM] * 6,
        out_specs=(VMEM,) * 4,
        scratch_shapes=[pltpu.VMEM((width, width), F32), pltpu.VMEM((count, 2 * share, width), F32), rim, whole, strip, sems],
        compiler_params=params,
        cost_estimate=pl.CostEstimate(flops=product + 2 * dense, bytes_accessed=3 * moved, transcendentals=features.size),
        name="layer_one_back",
    )(table, g_two, inner, outer, side, tiles, turned, m_one, w_first, readf, pred, goal, second, readout_part)
    first, second, extra = sum_shares(flags, outs, count, share, width, params)
    return pred_out, first, second, extra[0]


def solution(mesh):
    in_specs = (
        P(("groups", "wide"), "narrow", None, None),
        P(("groups", "wide"), "narrow", None),
        P(),
        P(),
        P(),
        P(),
        P(("groups", "wide"), "narrow", None),
    )
    out_specs = (
        P(("groups", "wide"), "narrow", None),
        P(("groups", "wide", "narrow"), None),
        P(("groups", "wide", "narrow"), None),
        P("groups"),
    )
    return jax.shard_map(
        per_device, mesh=mesh, in_specs=in_specs, out_specs=out_specs, check_vma=False
    )
```

```python
import functools

import jax
import jax.numpy as jnp
import numpy as np
from jax import lax
from jax.experimental import pallas as pl
from jax.experimental.pallas import tpu as pltpu
from jax.sharding import PartitionSpec as P

F32 = jnp.float32
BF16 = jnp.bfloat16
AXES = ("wide", "narrow")
VMEM_LIMIT = 16 * 1024 * 1024
ANY = pl.BlockSpec(memory_space=pl.ANY)
VMEM = pl.BlockSpec(memory_space=pltpu.VMEM)
SMEM = pl.BlockSpec(memory_space=pltpu.SMEM)

SELF, EAST, WEST, NORTH, SOUTH = 0, 1, 2, 3, 4
TAIL = 16


def routes(wide):
    depth = wide // 2

    def at(z, y, c):
        return (2 * z + y) * 2 + c

    every = [(z, y, c) for z in range(depth) for y in range(2) for c in range(2)]
    swap = [(at(z, c, y), at(z, y, c)) for z, y, c in every if y != c]
    first_side = [(at(z, c, 1 - y), at(z, y, c)) for z, y, c in every]
    inner = [(at(z, y, 1 - c), at(z, y, c)) for z, y, c in every]
    outer = [(at(z - 1, y, 1), at(z, y, 0)) for z, y, c in every if c == 0 and z > 0]
    outer += [(at(z + 1, y, 0), at(z, y, 1)) for z, y, c in every if c == 1 and z + 1 < depth]
    side = [(at(z, 1 - y, c), at(z, y, c)) for z, y, c in every]
    return swap, first_side, inner, outer, side


def place():
    half = lax.axis_index("narrow")
    side = lax.rem(lax.axis_index("wide"), 2)
    return half, side, half != side


def start_all(pairs, sems, first=0):
    copies = [pltpu.make_async_copy(a, b, sems.at[first + i]) for i, (a, b) in enumerate(pairs)]
    for copy in copies:
        copy.start()
    return copies


def wait_all(copies):
    for copy in copies:
        copy.wait()


def block_product(table, field, tiles, turned, row, col, nodes, rows, cols):
    at = row * cols + col
    step = rows * cols

    def block(r, c):
        return field[r, c * nodes : (c + 1) * nodes]

    lhs = jnp.concatenate(
        [
            tiles[table[SELF * step + at]],
            turned[table[SELF * step + at]],
            tiles[table[EAST * step + at]],
            turned[table[WEST * step + at]],
            tiles[table[NORTH * step + at]],
            turned[table[SOUTH * step + at]],
        ],
        axis=1,
    )
    centre = block(row + 1, col + 1)
    rhs = jnp.concatenate(
        [
            centre,
            centre,
            block(row + 2, col + 1),
            block(row, col + 1),
            block(row + 1, col + 2),
            block(row + 1, col),
        ],
        axis=0,
    )
    return jnp.dot(lhs, rhs, preferred_element_type=F32)


def rim_pairs(field, inner, outer, side, nodes, rows, cols):
    half, right, _ = place()
    zero_col = pl.multiple_of(jnp.where(right == 0, 0, (cols + 1) * nodes), nodes)
    side_col = pl.multiple_of(jnp.where(right == 0, (cols + 1) * nodes, 0), nodes)
    inside = pl.ds(nodes, cols * nodes)
    line = pl.ds(0, cols * nodes)
    for row in range(1, rows + 1):
        field[row, pl.ds(zero_col, nodes)] = jnp.zeros((nodes, field.shape[2]), field.dtype)
    pairs = [
        (inner.at[line], field.at[jnp.where(half == 0, rows + 1, 0), inside]),
        (outer.at[line], field.at[jnp.where(half == 0, 0, rows + 1), inside]),
    ]
    for row in range(rows):
        pairs.append((side.at[pl.ds(row * nodes, nodes)], field.at[row + 1, pl.ds(side_col, nodes)]))
    return pairs


def edge_pairs(done, inner, outer, side, nodes, rows, cols):
    half, right, _ = place()
    col = pl.multiple_of(jnp.where(right == 0, (cols - 1) * nodes, 0), nodes)
    pairs = [
        (done.at[jnp.where(half == 0, rows - 1, 0)], inner),
        (done.at[jnp.where(half == 0, 0, rows - 1)], outer),
    ]
    for row in range(rows):
        pairs.append((done.at[row, pl.ds(col, nodes)], side.at[pl.ds(row * nodes, nodes)]))
    return pairs


def pack_kernel(nodes, cols, ids, own, ends, side, numbers, ids_in, wide_ids, sems):
    rows, line = own.shape[0], own.shape[1]
    ids_copy = start_all([(ids, ids_in)], sems, 2 + rows)
    half, _, _ = place()
    col = pl.multiple_of(jnp.where(half == 1, 0, (cols - 1) * nodes), nodes)
    pairs = [(own.at[0], ends.at[pl.ds(0, line)]), (own.at[rows - 1], ends.at[pl.ds(line, line)])]
    for row in range(rows):
        pairs.append((own.at[row, pl.ds(col, nodes)], side.at[pl.ds(row * nodes, nodes)]))
    copies = start_all(pairs, sems)
    wait_all(ids_copy)
    wide_ids[...] = jnp.zeros_like(wide_ids)
    for kind in range(3):
        wide_ids[kind * rows : (kind + 1) * rows, 0:cols] = ids_in[kind].astype(F32)
    tail = wide_ids[...].astype(BF16)
    numbers[...] = tail
    ends[2 * line :] = tail
    side[rows * nodes :] = tail
    wait_all(copies)


def middle_kernel(own, after, middle, sems):
    wait_all(start_all([(own.at[pl.ds(1, own.shape[0] - 2)], middle)], sems))


def turn_kernel(tiles, turned, plain, sems):
    wait_all(start_all([(tiles, plain)], sems))

    def one_tile(tile, carry):
        turned[tile] = plain[tile].T
        return carry

    lax.fori_loop(0, tiles.shape[0], one_tile, 0)


def pick_kernel(numbers, own, ends, after, inner, outer, sems):
    rows, line = own.shape[0], own.shape[1]
    half, _, moved = place()
    whole = pl.ds(0, line)
    tail = pl.ds(line, TAIL)

    @pl.when(moved)
    def _():
        near = pl.multiple_of(jnp.where(half == 0, line, 0), line)
        far = pl.multiple_of(jnp.where(half == 0, 0, line), line)
        wait_all(start_all([
            (ends.at[pl.ds(near, line)], inner.at[whole]),
            (ends.at[pl.ds(far, line)], outer.at[whole]),
            (ends.at[pl.ds(2 * line, TAIL)], inner.at[tail]),
            (ends.at[pl.ds(2 * line, TAIL)], outer.at[tail]),
        ], sems))

    @pl.when(jnp.logical_not(moved))
    def _():
        copies = start_all([
            (own.at[jnp.where(half == 0, rows - 1, 0)], inner.at[whole]),
            (own.at[jnp.where(half == 0, 0, rows - 1)], outer.at[whole]),
        ], sems)
        inner[line:] = numbers[...]
        outer[line:] = numbers[...]
        wait_all(copies)


def first_kernel(nodes, cols, numbers, own, ends, middle, inner, outer, side, tiles_in, turned_in, weight_in,
                 table, x_out, m_out, inner_out, outer_out, side_out,
                 field, x_new, m_new, tiles, turned, weight, heads, heads_int, marks, sems):
    rows, line, width = own.shape
    step = rows * cols
    half, _, moved = place()
    inside = pl.ds(nodes, line)

    def main_pairs(flag):
        if flag:
            pairs = [
                (ends.at[pl.ds(2 * line, TAIL)], heads.at[0]),
                (ends.at[pl.ds(0, line)], field.at[1, inside]),
                (ends.at[pl.ds(line, line)], field.at[rows, inside]),
                (middle, field.at[pl.ds(2, rows - 2), inside]),
            ]
        else:
            pairs = [(numbers, heads.at[0]), (own, field.at[pl.ds(1, rows), inside])]
        return pairs

    def above_pairs(flag):
        return [((inner if flag else outer).at[pl.ds(line, TAIL)], heads.at[1])]

    def either(flag, build, first):
        @pl.when(flag)
        def _():
            start_all(build(True), sems, first)

        @pl.when(jnp.logical_not(flag))
        def _():
            start_all(build(False), sems, first)

    def either_wait(flag, build, first, low, high):
        def some(value):
            for i, (a, b) in list(enumerate(build(value)))[low:high]:
                pltpu.make_async_copy(a, b, sems.at[first + i]).wait()

        @pl.when(flag)
        def _():
            some(True)

        @pl.when(jnp.logical_not(flag))
        def _():
            some(False)

    either(moved, main_pairs, 0)
    either(half == 1, above_pairs, 4)
    left = start_all([(side.at[pl.ds(rows * nodes, TAIL)], heads.at[2])], sems, 5)
    rest = start_all(
        [(tiles_in, tiles), (turned_in, turned), (weight_in, weight)]
        + rim_pairs(field, inner, outer, side, nodes, rows, cols),
        sems,
        6,
    )
    either_wait(moved, main_pairs, 0, 0, 1)
    either_wait(half == 1, above_pairs, 4, 0, 1)
    wait_all(left)
    heads_int[...] = heads[:, :, 0:128].astype(F32).astype(jnp.int32)
    wait_all(start_all([(heads_int, marks)], sems, 5))

    def fill(at, carry):
        row, col = at // cols, lax.rem(at, cols)
        last = rows - 1
        up = jnp.where(row == 0, marks[1, rows + last, col], marks[0, rows + jnp.maximum(row - 1, 0), col])
        back = jnp.where(
            col == 0, marks[2, 2 * rows + row, cols - 1], marks[0, 2 * rows + row, jnp.maximum(col - 1, 0)]
        )
        table[SELF * step + at] = marks[0, row, col]
        table[EAST * step + at] = marks[0, rows + row, col]
        table[WEST * step + at] = up
        table[NORTH * step + at] = marks[0, 2 * rows + row, col]
        table[SOUTH * step + at] = back
        return carry

    lax.fori_loop(0, step, fill, 0)
    wait_all(rest)
    either_wait(moved, main_pairs, 0, 1, None)

    def one_row(row, carry):
        for col in range(cols):
            m_new[row, col * nodes : (col + 1) * nodes] = block_product(
                table, field, tiles, turned, row, col, nodes, rows, cols
            ).astype(BF16)
        for part in range(0, line, 2 * nodes):
            z = jnp.dot(m_new[row, part : part + 2 * nodes], weight[...], preferred_element_type=F32)
            base = field[row + 1, nodes + part : 3 * nodes + part]
            x_new[row, part : part + 2 * nodes] = (base.astype(F32) + jnp.tanh(z)).astype(BF16)
        return carry

    lax.fori_loop(0, rows, one_row, 0)
    wait_all(start_all(
        edge_pairs(x_new, inner_out, outer_out, side_out, nodes, rows, cols) + [(x_new, x_out), (m_new, m_out)], sems
    ))


def second_kernel(nodes, cols, scale, table, x_own, inner, outer, side, tiles_in, turned_in, weight_in, readout,
                  spread, target, target_swap, g_out, inner_out, outer_out, side_out, pred_out, second_out, readout_out, goals,
                  field, g_new, m_row, gz_row, tiles, turned, weight, sems):
    rows, line, width = x_own.shape
    wait_all(start_all(
        [(x_own, field.at[pl.ds(1, rows), pl.ds(nodes, line)]), (tiles_in, tiles), (turned_in, turned), (weight_in, weight)]
        + rim_pairs(field, inner, outer, side, nodes, rows, cols),
        sems,
    ))
    readf = readout[...]
    moved = place()[2]

    @pl.when(moved)
    def _():
        goals[...] = target_swap[...]

    @pl.when(jnp.logical_not(moved))
    def _():
        goals[...] = target[...]

    lanes = lax.broadcasted_iota(jnp.int32, (nodes, 128), 1)
    second_out[...] = jnp.zeros_like(second_out)
    readout_out[...] = jnp.zeros_like(readout_out)

    def one_row(row, carry):
        goal = goals[row].T
        seen = jnp.zeros((nodes, 128), F32)
        for col in range(cols):
            m_row[col * nodes : (col + 1) * nodes] = block_product(
                table, field, tiles, turned, row, col, nodes, rows, cols
            ).astype(BF16)
        for col in range(cols):
            here = slice(col * nodes, (col + 1) * nodes)
            z = jnp.dot(m_row[here], weight[...], preferred_element_type=F32)
            t = jnp.tanh(z)
            x = (field[row + 1, (col + 1) * nodes : (col + 2) * nodes].astype(F32) + t).astype(BF16)
            pred = jnp.dot(x, spread[...], preferred_element_type=F32)
            seen = jnp.where(lanes == col, pred, seen)
            gp = (pred[:, 0:1] - goal[:, col : col + 1]) * scale
            part = x.astype(F32) * gp
            readout_out[...] += part.reshape(nodes // 8, 8, width).sum(axis=0)
            gz = (gp * readf * (1.0 - t * t)).astype(BF16)
            gz_row[here] = gz
            g_new[row, here] = lax.dot_general(
                gz, weight[...], (((1,), (1,)), ((), ())), preferred_element_type=F32
            ).astype(BF16)
        second_out[...] += lax.dot_general(
            m_row[...], gz_row[...], (((0,), (0,)), ((), ())), preferred_element_type=F32
        )
        pred_out[row] = seen.T[0:cols]
        return carry

    lax.fori_loop(0, rows, one_row, 0)
    wait_all(start_all(
        edge_pairs(g_new, inner_out, outer_out, side_out, nodes, rows, cols) + [(g_new, g_out)], sems
    ))


def spread_shares(parts, extra, digit, outs):
    size = parts.shape[1]
    for k, out in enumerate(outs):
        for group in range(parts.shape[0] // 4):
            out[group * size : (group + 1) * size] = parts[4 * group + jnp.bitwise_xor(digit, k)]
        out[out.shape[0] - 8 :] = extra


def fold_kernel(base, keep, one, two, three, *refs):
    digit = lax.rem(lax.axis_index(AXES) // base, 4)
    parts = refs[-1]
    count, size, width = parts.shape
    total = keep[...] + one[...] + two[...] + three[...]
    parts[...] = total[: count * size].reshape(count, size, width)
    spread_shares(parts, total[count * size :], digit, refs[:-1])


def last_fold_kernel(keep, one, two, three, first, second, readout):
    share = first.shape[0]
    total = keep[...] + one[...] + two[...] + three[...]
    first[...] = total[:share]
    second[...] = total[share : 2 * share]
    readout[...] = total[2 * share :].sum(axis=0, keepdims=True)


def third_kernel(nodes, cols, scale, table, g_own, inner, outer, side, tiles_in, turned_in, m_own, weight_in, readout,
                 pred, pred_swap, target, second, extra, keep, one, two, three, pred_out,
                 first_out, parts, field, m_in, gz_row, tiles, turned, weight, sems):
    rows, line, width = g_own.shape
    wait_all(start_all(
        [
            (g_own, field.at[pl.ds(1, rows), pl.ds(nodes, line)]),
            (m_own, m_in),
            (tiles_in, tiles),
            (turned_in, turned),
            (weight_in, weight),
        ]
        + rim_pairs(field, inner, outer, side, nodes, rows, cols),
        sems,
    ))
    readf = readout[...]
    moved = place()[2]

    @pl.when(moved)
    def _():
        pred_out[...] = pred_swap[...]

    @pl.when(jnp.logical_not(moved))
    def _():
        pred_out[...] = pred[...]

    first_out[...] = jnp.zeros_like(first_out)

    def one_row(row, carry):
        gp_all = ((pred[row] - target[row]) * scale).T
        for col in range(cols):
            here = slice(col * nodes, (col + 1) * nodes)
            gx = gp_all[:, col : col + 1] * readf
            gx = gx + block_product(table, field, tiles, turned, row, col, nodes, rows, cols)
            t = jnp.tanh(jnp.dot(m_in[row, here], weight[...], preferred_element_type=F32))
            gz_row[here] = (gx * (1.0 - t * t)).astype(BF16)
        first_out[...] += lax.dot_general(
            m_in[row], gz_row[...], (((0,), (0,)), ((), ())), preferred_element_type=F32
        )
        return carry

    lax.fori_loop(0, rows, one_row, 0)
    count, size, _ = parts.shape
    parts[:, : size // 2] = first_out[...].reshape(count, size // 2, width)
    parts[:, size // 2 :] = second[...].reshape(count, size // 2, width)
    spread_shares(parts, extra[...], lax.rem(lax.axis_index(AXES), 4), (keep, one, two, three))


def shares_shape(groups, size, width):
    return (jax.ShapeDtypeStruct((groups * size + 8, width), F32),) * 4


def sum_shares(outs, count, share, width, params):
    base, groups = 1, count // 4
    while True:
        got = [
            lax.ppermute(outs[k], AXES, [(i, i ^ (k * base)) for i in range(count)]) for k in (1, 2, 3)
        ]
        if groups == 1:
            break
        base *= 4
        outs = pl.pallas_call(
            functools.partial(fold_kernel, base),
            out_shape=shares_shape(groups // 4, 2 * share, width),
            in_specs=[VMEM] * 4,
            out_specs=(VMEM,) * 4,
            scratch_shapes=[pltpu.VMEM((groups, 2 * share, width), F32)],
            compiler_params=params,
            name="fold",
        )(outs[0], *got)
        groups //= 4
    small = jax.ShapeDtypeStruct((share, width), F32)
    return pl.pallas_call(
        last_fold_kernel,
        out_shape=(small, small, jax.ShapeDtypeStruct((1, width), F32)),
        in_specs=[VMEM] * 4,
        out_specs=(VMEM,) * 3,
        compiler_params=params,
        name="last_fold",
    )(outs[0], *got)


def per_device(features, tile_ids, tiles, w_first, w_second, readout, target):
    rows, cols, nodes, width = features.shape
    wide, narrow = lax.axis_size("wide"), lax.axis_size("narrow")
    count = wide * narrow
    line, step = cols * nodes, rows * cols
    swap, first_side, inner_way, outer_way, side_way = routes(wide)
    scale = float(np.sqrt(np.float32(width) / np.float32(rows * line * count)))
    params = pltpu.CompilerParams(vmem_limit_bytes=VMEM_LIMIT)

    def send(value, way):
        return lax.ppermute(value, AXES, way)

    def edges(inner, outer, side):
        return send(inner, inner_way), send(outer, outer_way), send(side, side_way)

    def bf(*shape):
        return jax.ShapeDtypeStruct(shape, BF16)

    def sems(number):
        return pltpu.SemaphoreType.DMA((number,))

    features = features.reshape(rows, line, width)
    ends_s, side_s, numbers = pl.pallas_call(
        functools.partial(pack_kernel, nodes, cols),
        out_shape=(bf(2 * line + TAIL, width), bf(rows * nodes + TAIL, width), bf(TAIL, width)),
        in_specs=[ANY, ANY],
        out_specs=(VMEM,) * 3,
        scratch_shapes=[pltpu.VMEM((3, rows, cols), jnp.int32), pltpu.VMEM((TAIL, width), F32), sems(3 + rows)],
        compiler_params=params,
        name="pack",
    )(jnp.transpose(tile_ids, (2, 0, 1)), features)
    ends = send(ends_s, swap)
    side = send(side_s, first_side)
    middle_s = pl.pallas_call(
        middle_kernel,
        out_shape=bf(rows - 2, line, width),
        in_specs=[ANY, ANY],
        out_specs=VMEM,
        scratch_shapes=[sems(1)],
        compiler_params=params,
        name="pack_middle",
    )(features, side_s)
    middle = send(middle_s, swap)
    target, tiles, _ = lax.optimization_barrier((target, tiles, middle_s))
    goal_swap = send(target, swap)
    turned = pl.pallas_call(
        turn_kernel,
        out_shape=bf(*tiles.shape),
        in_specs=[ANY],
        out_specs=VMEM,
        scratch_shapes=[pltpu.VMEM(tiles.shape, BF16), sems(1)],
        compiler_params=params,
        name="turn",
    )(tiles)
    readf = readout.astype(F32)[None]
    spread = jnp.broadcast_to(readout[:, None], (width, 128))

    inner_s, outer_s = pl.pallas_call(
        pick_kernel,
        out_shape=(bf(line + TAIL, width),) * 2,
        in_specs=[VMEM, ANY, ANY, ANY],
        out_specs=(VMEM,) * 2,
        scratch_shapes=[sems(4)],
        compiler_params=params,
        name="pick",
    )(numbers, features, ends, side)
    outer, inner = send(outer_s, outer_way), send(inner_s, inner_way)

    patch = bf(rows, line, width)
    edge_shapes = (bf(line, width), bf(line, width), bf(rows * nodes, width))
    square = jax.ShapeDtypeStruct((width, width), F32)
    rim = pltpu.VMEM((rows + 2, line + 2 * nodes, width), BF16)
    whole = pltpu.VMEM((rows, line, width), BF16)
    strip = pltpu.VMEM((line, width), BF16)
    loads = [pltpu.VMEM(tiles.shape, BF16), pltpu.VMEM(tiles.shape, BF16), pltpu.VMEM((width, width), BF16)]
    product = 2 * rows * line * width * 6 * nodes
    dense = 2 * rows * line * width * width
    moves = 2 * rows * line * width

    def cost(denses, passes):
        return pl.CostEstimate(
            flops=product + denses * dense, bytes_accessed=passes * moves, transcendentals=rows * line * width
        )

    table, x_one, m_one, inner_s, outer_s, side_s = pl.pallas_call(
        functools.partial(first_kernel, nodes, cols),
        out_shape=(jax.ShapeDtypeStruct((5 * step,), jnp.int32), patch, patch) + edge_shapes,
        in_specs=[ANY] * 10,
        out_specs=(SMEM,) + (ANY,) * 5,
        scratch_shapes=[rim, whole, whole]
        + loads
        + [
            pltpu.VMEM((3, TAIL, width), BF16),
            pltpu.VMEM((3, TAIL, 128), jnp.int32),
            pltpu.SMEM((3, TAIL, 128), jnp.int32),
            sems(11 + rows),
        ],
        compiler_params=params,
        cost_estimate=cost(1, 4),
        name="layer_one",
    )(numbers, features, ends, middle, inner, outer, side, tiles, turned, w_first)

    inner, outer, side = edges(inner_s, outer_s, side_s)
    g_two, inner_s, outer_s, side_s, pred, second, readout_part, goal = pl.pallas_call(
        functools.partial(second_kernel, nodes, cols, scale),
        out_shape=(patch,) + edge_shapes
        + (
            jax.ShapeDtypeStruct(target.shape, F32),
            square,
            jax.ShapeDtypeStruct((8, width), F32),
            jax.ShapeDtypeStruct(target.shape, F32),
        ),
        in_specs=[SMEM] + [ANY] * 7 + [VMEM] * 4,
        out_specs=(ANY,) * 4 + (VMEM,) * 4,
        scratch_shapes=[rim, whole, strip, strip] + loads + [sems(6 + rows)],
        compiler_params=params,
        cost_estimate=cost(3, 3),
        name="layer_two",
    )(table, x_one, inner, outer, side, tiles, turned, w_second, readf, spread, target, goal_swap)

    inner, outer, side = edges(inner_s, outer_s, side_s)
    pred_swap = send(pred, swap)
    share = width // count
    *outs, pred_out = pl.pallas_call(
        functools.partial(third_kernel, nodes, cols, scale),
        out_shape=shares_shape(count // 4, 2 * share, width) + (jax.ShapeDtypeStruct(target.shape, F32),),
        in_specs=[SMEM] + [ANY] * 8 + [VMEM] * 6,
        out_specs=(VMEM,) * 5,
        scratch_shapes=[pltpu.VMEM((width, width), F32), pltpu.VMEM((count, 2 * share, width), F32), rim, whole, strip]
        + loads
        + [sems(7 + rows)],
        compiler_params=params,
        cost_estimate=cost(2, 3),
        name="layer_one_back",
    )(table, g_two, inner, outer, side, tiles, turned, m_one, w_first, readf, pred, pred_swap, goal, second, readout_part)
    first, second, extra = sum_shares(outs, count, share, width, params)
    return pred_out, first, second, extra[0]


def solution(mesh):
    in_specs = (
        P(("groups", "wide"), "narrow", None, None),
        P(("groups", "wide"), "narrow", None),
        P(),
        P(),
        P(),
        P(),
        P(("groups", "wide"), "narrow", None),
    )
    out_specs = (
        P(("groups", "wide"), "narrow", None),
        P(("groups", "wide", "narrow"), None),
        P(("groups", "wide", "narrow"), None),
        P("groups"),
    )
    return jax.shard_map(
        per_device, mesh=mesh, in_specs=in_specs, out_specs=out_specs, check_vma=False
    )
```

```python
import functools

import jax
import jax.numpy as jnp
import numpy as np
from jax import lax
from jax.experimental import pallas as pl
from jax.experimental.pallas import tpu as pltpu
from jax.sharding import PartitionSpec as P

F32 = jnp.float32
BF16 = jnp.bfloat16
AXES = ("wide", "narrow")
VMEM_LIMIT = 16 * 1024 * 1024
ANY = pl.BlockSpec(memory_space=pl.ANY)
VMEM = pl.BlockSpec(memory_space=pltpu.VMEM)
SMEM = pl.BlockSpec(memory_space=pltpu.SMEM)

SELF, EAST, WEST, NORTH, SOUTH = 0, 1, 2, 3, 4
TAIL = 16


def routes(wide):
    depth = wide // 2

    def at(z, y, c):
        return (2 * z + y) * 2 + c

    every = [(z, y, c) for z in range(depth) for y in range(2) for c in range(2)]
    swap = [(at(z, c, y), at(z, y, c)) for z, y, c in every if y != c]
    first_side = [(at(z, c, 1 - y), at(z, y, c)) for z, y, c in every]
    inner = [(at(z, y, 1 - c), at(z, y, c)) for z, y, c in every]
    outer = [(at(z - 1, y, 1), at(z, y, 0)) for z, y, c in every if c == 0 and z > 0]
    outer += [(at(z + 1, y, 0), at(z, y, 1)) for z, y, c in every if c == 1 and z + 1 < depth]
    side = [(at(z, 1 - y, c), at(z, y, c)) for z, y, c in every]
    return swap, first_side, inner, outer, side


def place():
    half = lax.axis_index("narrow")
    side = lax.rem(lax.axis_index("wide"), 2)
    return half, side, half != side


def start_all(pairs, sems, first=0):
    copies = [pltpu.make_async_copy(a, b, sems.at[first + i]) for i, (a, b) in enumerate(pairs)]
    for copy in copies:
        copy.start()
    return copies


def wait_all(copies):
    for copy in copies:
        copy.wait()


def at_block(col, nodes):
    return pl.ds(col * nodes if isinstance(col, int) else pl.multiple_of(col * nodes, nodes), nodes)


def block_product(table, field, tiles, turned, row, col, shape):
    nodes, rows, cols = shape
    at = row * cols + col
    step = rows * cols

    def block(r, c):
        return field[r, at_block(c, nodes)]

    lhs = jnp.concatenate(
        [
            tiles[table[SELF * step + at]],
            turned[table[SELF * step + at]],
            tiles[table[EAST * step + at]],
            turned[table[WEST * step + at]],
            tiles[table[NORTH * step + at]],
            turned[table[SOUTH * step + at]],
        ],
        axis=1,
    )
    centre = block(row + 1, col + 1)
    rhs = jnp.concatenate(
        [
            centre,
            centre,
            block(row + 2, col + 1),
            block(row, col + 1),
            block(row + 1, col + 2),
            block(row + 1, col),
        ],
        axis=0,
    )
    return jnp.dot(lhs, rhs, preferred_element_type=F32)


def edge_blocks(shape, body):
    _, rows, cols = shape

    def one_row(i, carry):
        for col in range(0, cols, 2):
            body(i * (rows - 1), [col, col + 1])
        return carry

    lax.fori_loop(0, 2, one_row, 0)
    _, right, _ = place()
    for row in range(1, rows - 1):
        body(row, [jnp.where(right == 0, cols - 1, 0)])


def inner_blocks(shape, body):
    _, rows, cols = shape
    _, right, _ = place()

    def one_row(row, carry):
        for col in range(0, cols - 1, 2):
            body(row, [right + c for c in range(col, min(col + 2, cols - 1))])
        return carry

    lax.fori_loop(1, rows - 1, one_row, 0)


def group(cols, nodes):
    start = cols[0] * nodes
    return pl.ds(start if isinstance(start, int) else pl.multiple_of(start, nodes), len(cols) * nodes)


def group_in_field(cols, nodes):
    return group([cols[0] + 1] + cols[1:], nodes)


def forward_one(shape, table, field, tiles, turned, weight, x_field, m_all):
    nodes = shape[0]

    def body(row, cols):
        for col in cols:
            m_all[row, at_block(col, nodes)] = block_product(table, field, tiles, turned, row, col, shape).astype(BF16)
        z = jnp.dot(m_all[row, group(cols, nodes)], weight[...], preferred_element_type=F32)
        inside = group_in_field(cols, nodes)
        x_field[row + 1, inside] = (field[row + 1, inside].astype(F32) + jnp.tanh(z)).astype(BF16)

    return body


def residual_columns(seen, goal, scale):
    gp = (seen - goal) * scale
    column = jnp.broadcast_to(gp, (gp.shape[1], gp.shape[1])).T
    return jnp.concatenate([column, column], axis=1)


def through_two(shape, scale, table, field, tiles, turned, weight, readout, goals, m_all, gz_all, g_field, preds, sums):
    nodes = shape[0]
    eight = jnp.broadcast_to(readout[...], (8, readout.shape[1]))
    readf = readout[...].astype(F32)

    def body(row, cols):
        for col in cols:
            m_all[row, at_block(col, nodes)] = block_product(table, field, tiles, turned, row, col, shape).astype(BF16)
        here, inside = group(cols, nodes), group_in_field(cols, nodes)
        t = jnp.tanh(jnp.dot(m_all[row, here], weight[...], preferred_element_type=F32))
        x = (field[row + 1, inside].astype(F32) + t).astype(BF16)
        seen = lax.dot_general(eight, x, (((1,), (1,)), ((), ())), preferred_element_type=F32)[0:1]
        parts = []
        for k, col in enumerate(cols):
            one = seen[:, k * nodes : (k + 1) * nodes]
            preds[row, pl.ds(col, 1)] = one
            parts.append(residual_columns(one, goals[row, pl.ds(col, 1)], scale))
        gp = jnp.concatenate(parts, axis=0) if len(parts) > 1 else parts[0]
        sums[...] += (x.astype(F32) * gp).reshape(gp.shape[0] // 8, 8, gp.shape[1]).sum(axis=0)
        gz = (gp * readf * (1.0 - t * t)).astype(BF16)
        gz_all[row, here] = gz
        g_field[row + 1, inside] = lax.dot_general(
            gz, weight[...], (((1,), (1,)), ((), ())), preferred_element_type=F32
        ).astype(BF16)

    return body


def back_one(shape, scale, table, field, tiles, turned, weight, readout, goals, preds, m_all, gz_all):
    nodes = shape[0]
    readf = readout[...].astype(F32)

    def body(row, cols):
        here = group(cols, nodes)
        t = jnp.tanh(jnp.dot(m_all[row, here], weight[...], preferred_element_type=F32))
        for k, col in enumerate(cols):
            gp = residual_columns(preds[row, pl.ds(col, 1)], goals[row, pl.ds(col, 1)], scale)
            gx = gp * readf + block_product(table, field, tiles, turned, row, col, shape)
            tk = t[k * nodes : (k + 1) * nodes]
            gz_all[row, at_block(col, nodes)] = (gx * (1.0 - tk * tk)).astype(BF16)

    return body


def over_nodes(left, right):
    return lax.dot_general(left, right, (((0,), (0,)), ((), ())), preferred_element_type=F32)


def zero_rim(field, shape):
    nodes, rows, cols = shape
    field[0] = jnp.zeros(field.shape[1:], field.dtype)
    field[rows + 1] = jnp.zeros(field.shape[1:], field.dtype)
    for row in range(1, rows + 1):
        for col in (0, cols + 1):
            field[row, at_block(col, nodes)] = jnp.zeros((nodes, field.shape[2]), field.dtype)


def edge_pairs(field, inner, outer, side, shape):
    nodes, rows, cols = shape
    half, right, _ = place()
    inside = pl.ds(nodes, cols * nodes)
    pairs = [
        (field.at[jnp.where(half == 0, rows, 1), inside], inner),
        (field.at[jnp.where(half == 0, 1, rows), inside], outer),
    ]
    for row in range(rows):
        pairs.append((field.at[row + 1, at_block(jnp.where(right == 0, cols, 1), nodes)], side.at[at_block(row, nodes)]))
    return pairs


def rim_pairs(field, inner, outer, side, shape):
    nodes, rows, cols = shape
    half, right, _ = place()
    zero_col = pl.multiple_of(jnp.where(right == 0, 0, (cols + 1) * nodes), nodes)
    side_col = pl.multiple_of(jnp.where(right == 0, (cols + 1) * nodes, 0), nodes)
    inside = pl.ds(nodes, cols * nodes)
    line = pl.ds(0, cols * nodes)
    for row in range(1, rows + 1):
        field[row, pl.ds(zero_col, nodes)] = jnp.zeros((nodes, field.shape[2]), field.dtype)
    pairs = [
        (inner.at[line], field.at[jnp.where(half == 0, rows + 1, 0), inside]),
        (outer.at[line], field.at[jnp.where(half == 0, 0, rows + 1), inside]),
    ]
    for row in range(rows):
        pairs.append((side.at[pl.ds(row * nodes, nodes)], field.at[row + 1, pl.ds(side_col, nodes)]))
    return pairs


def pack_kernel(nodes, cols, ids, own, ends, side, numbers, ids_in, wide_ids, sems):
    rows, line = own.shape[0], own.shape[1]
    ids_copy = start_all([(ids, ids_in)], sems, 2 + rows)
    half, _, _ = place()
    col = pl.multiple_of(jnp.where(half == 1, 0, (cols - 1) * nodes), nodes)
    pairs = [(own.at[0], ends.at[pl.ds(0, line)]), (own.at[rows - 1], ends.at[pl.ds(line, line)])]
    for row in range(rows):
        pairs.append((own.at[row, pl.ds(col, nodes)], side.at[pl.ds(row * nodes, nodes)]))
    copies = start_all(pairs, sems)
    wait_all(ids_copy)
    wide_ids[...] = jnp.zeros_like(wide_ids)
    for kind in range(3):
        wide_ids[kind * rows : (kind + 1) * rows, 0:cols] = ids_in[kind].astype(F32)
    tail = wide_ids[...].astype(BF16)
    numbers[...] = tail
    ends[2 * line :] = tail
    side[rows * nodes :] = tail
    wait_all(copies)


def middle_kernel(own, after, middle, sems):
    wait_all(start_all([(own.at[pl.ds(1, own.shape[0] - 2)], middle)], sems))


def prepare_kernel(tiles, first, second, plain, turned, first_in, second_in, sems):
    wait_all(start_all([(tiles, plain), (first, first_in), (second, second_in)], sems))

    def one_tile(tile, carry):
        turned[tile] = plain[tile].T
        return carry

    lax.fori_loop(0, tiles.shape[0], one_tile, 0)


def pick_kernel(numbers, own, ends, after, later, inner, outer, sems):
    rows, line = own.shape[0], own.shape[1]
    half, _, moved = place()
    whole = pl.ds(0, line)
    tail = pl.ds(line, TAIL)

    @pl.when(moved)
    def _():
        near = pl.multiple_of(jnp.where(half == 0, line, 0), line)
        far = pl.multiple_of(jnp.where(half == 0, 0, line), line)
        wait_all(start_all([
            (ends.at[pl.ds(near, line)], inner.at[whole]),
            (ends.at[pl.ds(far, line)], outer.at[whole]),
            (ends.at[pl.ds(2 * line, TAIL)], inner.at[tail]),
            (ends.at[pl.ds(2 * line, TAIL)], outer.at[tail]),
        ], sems))

    @pl.when(jnp.logical_not(moved))
    def _():
        copies = start_all([
            (own.at[jnp.where(half == 0, rows - 1, 0)], inner.at[whole]),
            (own.at[jnp.where(half == 0, 0, rows - 1)], outer.at[whole]),
        ], sems)
        inner[line:] = numbers[...]
        outer[line:] = numbers[...]
        wait_all(copies)


def first_edge_kernel(shape, numbers, own, ends, middle, inner, outer, side, tiles, turned, weight,
                      table, field, x_field, m_all, inner_out, outer_out, side_out, heads, heads_int, marks, sems):
    nodes, rows, cols = shape
    line = cols * nodes
    step = rows * cols
    half, _, moved = place()
    inside = pl.ds(nodes, line)

    def main_pairs(flag):
        if flag:
            pairs = [
                (ends.at[pl.ds(2 * line, TAIL)], heads.at[0]),
                (ends.at[pl.ds(0, line)], field.at[1, inside]),
                (ends.at[pl.ds(line, line)], field.at[rows, inside]),
                (middle, field.at[pl.ds(2, rows - 2), inside]),
            ]
        else:
            pairs = [(numbers, heads.at[0]), (own, field.at[pl.ds(1, rows), inside])]
        return pairs

    def above_pairs(flag):
        return [((inner if flag else outer).at[pl.ds(line, TAIL)], heads.at[1])]

    def either(flag, build, first):
        @pl.when(flag)
        def _():
            start_all(build(True), sems, first)

        @pl.when(jnp.logical_not(flag))
        def _():
            start_all(build(False), sems, first)

    def either_wait(flag, build, first, low, high):
        def some(value):
            for i, (a, b) in list(enumerate(build(value)))[low:high]:
                pltpu.make_async_copy(a, b, sems.at[first + i]).wait()

        @pl.when(flag)
        def _():
            some(True)

        @pl.when(jnp.logical_not(flag))
        def _():
            some(False)

    either(moved, main_pairs, 0)
    either(half == 1, above_pairs, 4)
    left = start_all([(side.at[pl.ds(rows * nodes, TAIL)], heads.at[2])], sems, 5)
    rest = start_all(
        rim_pairs(field, inner, outer, side, shape),
        sems,
        6,
    )
    either_wait(moved, main_pairs, 0, 0, 1)
    either_wait(half == 1, above_pairs, 4, 0, 1)
    wait_all(left)
    heads_int[...] = heads[:, :, 0:128].astype(F32).astype(jnp.int32)
    wait_all(start_all([(heads_int, marks)], sems, 5))

    def fill(at, carry):
        row, col = at // cols, lax.rem(at, cols)
        last = rows - 1
        up = jnp.where(row == 0, marks[1, rows + last, col], marks[0, rows + jnp.maximum(row - 1, 0), col])
        back = jnp.where(
            col == 0, marks[2, 2 * rows + row, cols - 1], marks[0, 2 * rows + row, jnp.maximum(col - 1, 0)]
        )
        table[SELF * step + at] = marks[0, row, col]
        table[EAST * step + at] = marks[0, rows + row, col]
        table[WEST * step + at] = up
        table[NORTH * step + at] = marks[0, 2 * rows + row, col]
        table[SOUTH * step + at] = back
        return carry

    lax.fori_loop(0, step, fill, 0)
    zero_rim(x_field, shape)
    wait_all(rest)
    either_wait(moved, main_pairs, 0, 1, None)

    edge_blocks(shape, forward_one(shape, table, field, tiles, turned, weight, x_field, m_all))
    wait_all(start_all(edge_pairs(x_field, inner_out, outer_out, side_out, shape), sems))


def middle_compute_kernel(shape, scale, table, field, tiles, turned, weight_one, weight_two, readout, target,
                          target_swap, x_in, m_in, x_field, m_one, m_two, gz_two, g_field, preds, goals, sums):
    _, _, moved = place()

    @pl.when(moved)
    def _():
        goals[...] = target_swap[...]

    @pl.when(jnp.logical_not(moved))
    def _():
        goals[...] = target[...]

    zero_rim(g_field, shape)
    sums[...] = jnp.zeros_like(sums)
    inner_blocks(shape, forward_one(shape, table, field, tiles, turned, weight_one, x_field, m_one))
    inner_blocks(shape, through_two(
        shape, scale, table, x_field, tiles, turned, weight_two, readout, goals, m_two, gz_two, g_field, preds, sums
    ))


def second_edge_kernel(shape, scale, table, inner, outer, side, tiles, turned, weight, readout, goals,
                       x_in, m_in, gz_in, g_in, preds_in, sums_in,
                       x_field, m_two, gz_two, g_field, preds, sums, inner_out, outer_out, side_out, sems):
    wait_all(start_all(rim_pairs(x_field, inner, outer, side, shape), sems))
    edge_blocks(shape, through_two(
        shape, scale, table, x_field, tiles, turned, weight, readout, goals, m_two, gz_two, g_field, preds, sums
    ))
    wait_all(start_all(edge_pairs(g_field, inner_out, outer_out, side_out, shape), sems))


def back_inner_kernel(shape, scale, table, g_field, tiles, turned, weight, readout, goals, preds, m_one, m_two, gz_two,
                      gz_one, first_out, second_out):
    nodes, rows, cols = shape
    _, right, _ = place()
    inner_blocks(shape, back_one(shape, scale, table, g_field, tiles, turned, weight, readout, goals, preds, m_one, gz_one))
    part = pl.ds(pl.multiple_of(right * nodes, nodes), (cols - 1) * nodes)
    first_out[...] = jnp.zeros_like(first_out)
    second_out[...] = jnp.zeros_like(second_out)

    def one_row(row, carry):
        first_out[...] += over_nodes(m_one[row, part], gz_one[row, part])
        return carry

    def each_row(row, carry):
        second_out[...] += over_nodes(m_two[row], gz_two[row])
        return carry

    lax.fori_loop(1, rows - 1, one_row, 0)
    lax.fori_loop(0, rows, each_row, 0)


def back_edge_kernel(shape, scale, table, inner, outer, side, tiles, turned, weight, readout, goals, preds, preds_swap,
                     m_one, first_in, second, sums, g_in, gz_in, g_field, gz_one, keep, one, two, three, pred_out,
                     first_out, parts, sems):
    nodes, rows, cols = shape
    _, right, moved = place()
    copies = start_all(rim_pairs(g_field, inner, outer, side, shape), sems)

    @pl.when(moved)
    def _():
        pred_out[...] = preds_swap[...]

    @pl.when(jnp.logical_not(moved))
    def _():
        pred_out[...] = preds[...]

    wait_all(copies)
    edge_blocks(shape, back_one(shape, scale, table, g_field, tiles, turned, weight, readout, goals, preds, m_one, gz_one))
    first_out[...] = first_in[...]
    for row in (0, rows - 1):
        first_out[...] += over_nodes(m_one[row], gz_one[row])
    beside = at_block(jnp.where(right == 0, cols - 1, 0), nodes)
    for row in range(1, rows - 1):
        first_out[...] += over_nodes(m_one[row, beside], gz_one[row, beside])
    count, size, width = parts.shape
    parts[:, : size // 2] = first_out[...].reshape(count, size // 2, width)
    parts[:, size // 2 :] = second[...].reshape(count, size // 2, width)
    spread_shares(parts, sums[...], lax.rem(lax.axis_index(AXES), 4), (keep, one, two, three))


def spread_shares(parts, extra, digit, outs):
    size = parts.shape[1]
    for k, out in enumerate(outs):
        for group in range(parts.shape[0] // 4):
            out[group * size : (group + 1) * size] = parts[4 * group + jnp.bitwise_xor(digit, k)]
        out[out.shape[0] - 8 :] = extra


def fold_kernel(base, keep, one, two, three, *refs):
    digit = lax.rem(lax.axis_index(AXES) // base, 4)
    parts = refs[-1]
    count, size, width = parts.shape
    total = keep[...] + one[...] + two[...] + three[...]
    parts[...] = total[: count * size].reshape(count, size, width)
    spread_shares(parts, total[count * size :], digit, refs[:-1])


def last_fold_kernel(keep, one, two, three, first, second, readout):
    share = first.shape[0]
    total = keep[...] + one[...] + two[...] + three[...]
    first[...] = total[:share]
    second[...] = total[share : 2 * share]
    readout[...] = total[2 * share :].sum(axis=0, keepdims=True)


def shares_shape(groups, size, width):
    return (jax.ShapeDtypeStruct((groups * size + 8, width), F32),) * 4


def sum_shares(outs, count, share, width, params):
    base, groups = 1, count // 4
    while True:
        got = [
            lax.ppermute(outs[k], AXES, [(i, i ^ (k * base)) for i in range(count)]) for k in (1, 2, 3)
        ]
        if groups == 1:
            break
        base *= 4
        outs = pl.pallas_call(
            functools.partial(fold_kernel, base),
            out_shape=shares_shape(groups // 4, 2 * share, width),
            in_specs=[VMEM] * 4,
            out_specs=(VMEM,) * 4,
            scratch_shapes=[pltpu.VMEM((groups, 2 * share, width), F32)],
            compiler_params=params,
            name="fold",
        )(outs[0], *got)
        groups //= 4
    small = jax.ShapeDtypeStruct((share, width), F32)
    return pl.pallas_call(
        last_fold_kernel,
        out_shape=(small, small, jax.ShapeDtypeStruct((1, width), F32)),
        in_specs=[VMEM] * 4,
        out_specs=(VMEM,) * 3,
        compiler_params=params,
        name="last_fold",
    )(outs[0], *got)


def per_device(features, tile_ids, tiles, w_first, w_second, readout, target):
    rows, cols, nodes, width = features.shape
    wide, narrow = lax.axis_size("wide"), lax.axis_size("narrow")
    count = wide * narrow
    line, step = cols * nodes, rows * cols
    swap, first_side, inner_way, outer_way, side_way = routes(wide)
    scale = float(np.sqrt(np.float32(width) / np.float32(rows * line * count)))
    params = pltpu.CompilerParams(vmem_limit_bytes=VMEM_LIMIT)

    def send(value, way):
        return lax.ppermute(value, AXES, way)

    def edges(inner, outer, side):
        return send(inner, inner_way), send(outer, outer_way), send(side, side_way)

    def bf(*shape):
        return jax.ShapeDtypeStruct(shape, BF16)

    def sems(number):
        return pltpu.SemaphoreType.DMA((number,))

    features = features.reshape(rows, line, width)
    ends_s, side_s, numbers = pl.pallas_call(
        functools.partial(pack_kernel, nodes, cols),
        out_shape=(bf(2 * line + TAIL, width), bf(rows * nodes + TAIL, width), bf(TAIL, width)),
        in_specs=[ANY, ANY],
        out_specs=(VMEM,) * 3,
        scratch_shapes=[pltpu.VMEM((3, rows, cols), jnp.int32), pltpu.VMEM((TAIL, width), F32), sems(3 + rows)],
        compiler_params=params,
        name="pack",
    )(jnp.transpose(tile_ids, (2, 0, 1)), features)
    ends = send(ends_s, swap)
    side = send(side_s, first_side)
    middle_s = pl.pallas_call(
        middle_kernel,
        out_shape=bf(rows - 2, line, width),
        in_specs=[ANY, ANY],
        out_specs=VMEM,
        scratch_shapes=[sems(1)],
        compiler_params=params,
        name="pack_middle",
    )(features, side_s)
    middle = send(middle_s, swap)
    target, tiles, w_first, w_second, _ = lax.optimization_barrier((target, tiles, w_first, w_second, middle_s))
    goal_swap = send(target, swap)
    tiles, turned, w_first, w_second = pl.pallas_call(
        prepare_kernel,
        out_shape=(bf(*tiles.shape), bf(*tiles.shape), bf(width, width), bf(width, width)),
        in_specs=[ANY] * 3,
        out_specs=(VMEM,) * 4,
        scratch_shapes=[sems(3)],
        compiler_params=params,
        name="prepare",
    )(tiles, w_first, w_second)
    readout = readout[None]

    inner_s, outer_s = pl.pallas_call(
        pick_kernel,
        out_shape=(bf(line + TAIL, width),) * 2,
        in_specs=[VMEM, ANY, ANY, ANY, ANY],
        out_specs=(VMEM,) * 2,
        scratch_shapes=[sems(4)],
        compiler_params=params,
        name="pick",
    )(numbers, features, ends, side, goal_swap)
    outer, inner = send(outer_s, outer_way), send(inner_s, inner_way)

    shape = (nodes, rows, cols)
    patch, padded = bf(rows, line, width), bf(rows + 2, line + 2 * nodes, width)
    edge_shapes = (bf(line, width), bf(line, width), bf(rows * nodes, width))
    square = jax.ShapeDtypeStruct((width, width), F32)
    sums_shape = jax.ShapeDtypeStruct((8, width), F32)
    goal_shape = jax.ShapeDtypeStruct(target.shape, F32)
    block = nodes * width
    edge, inside = 2 * cols + rows - 2, (rows - 2) * (cols - 1)

    def cost(products, denses):
        return pl.CostEstimate(
            flops=2 * block * (products * 6 * nodes + denses * width),
            bytes_accessed=4 * block * (products + denses),
            transcendentals=block * products,
        )

    table, f_field, x_field, m_one, inner_s, outer_s, side_s = pl.pallas_call(
        functools.partial(first_edge_kernel, shape),
        out_shape=(jax.ShapeDtypeStruct((5 * step,), jnp.int32), padded, padded, patch) + edge_shapes,
        in_specs=[ANY] * 7 + [VMEM] * 3,
        out_specs=(SMEM,) + (VMEM,) * 6,
        scratch_shapes=[
            pltpu.VMEM((3, TAIL, width), BF16),
            pltpu.VMEM((3, TAIL, 128), jnp.int32),
            pltpu.SMEM((3, TAIL, 128), jnp.int32),
            sems(8 + rows),
        ],
        compiler_params=params,
        cost_estimate=cost(edge, edge),
        name="first_edge",
    )(numbers, features, ends, middle, inner, outer, side, tiles, turned, w_first)

    inner, outer, side = edges(inner_s, outer_s, side_s)
    x_field, m_one, m_two, gz_two, g_field, preds, goals, sums = pl.pallas_call(
        functools.partial(middle_compute_kernel, shape, scale),
        out_shape=(padded, patch, patch, patch, padded, goal_shape, goal_shape, sums_shape),
        in_specs=[SMEM] + [VMEM] * 10,
        out_specs=(VMEM,) * 8,
        input_output_aliases={9: 0, 10: 1},
        compiler_params=params,
        cost_estimate=cost(2 * inside, 3 * inside),
        name="inner_forward",
    )(table, f_field, tiles, turned, w_first, w_second, readout, target, goal_swap, x_field, m_one)

    x_field, m_two, gz_two, g_field, preds, sums, inner_s, outer_s, side_s = pl.pallas_call(
        functools.partial(second_edge_kernel, shape, scale),
        out_shape=(padded, patch, patch, padded, goal_shape, sums_shape) + edge_shapes,
        in_specs=[SMEM] + [ANY] * 3 + [VMEM] * 11,
        out_specs=(VMEM,) * 9,
        input_output_aliases={9 + i: i for i in range(6)},
        scratch_shapes=[sems(2 + rows)],
        compiler_params=params,
        cost_estimate=cost(edge, 2 * edge),
        name="second_edge",
    )(table, inner, outer, side, tiles, turned, w_second, readout, goals, x_field, m_two, gz_two, g_field, preds, sums)

    inner, outer, side = edges(inner_s, outer_s, side_s)
    preds_swap = send(preds, swap)
    gz_one, first, second = pl.pallas_call(
        functools.partial(back_inner_kernel, shape, scale),
        out_shape=(patch, square, square),
        in_specs=[SMEM] + [VMEM] * 10,
        out_specs=(VMEM,) * 3,
        compiler_params=params,
        cost_estimate=cost(inside, 2 * inside + rows * cols),
        name="back_inner",
    )(table, g_field, tiles, turned, w_first, readout, goals, preds, m_one, m_two, gz_two)

    share = width // count
    _, _, *outs, pred_out = pl.pallas_call(
        functools.partial(back_edge_kernel, shape, scale),
        out_shape=(padded, patch) + shares_shape(count // 4, 2 * share, width) + (goal_shape,),
        in_specs=[SMEM] + [ANY] * 3 + [VMEM] * 13,
        out_specs=(VMEM,) * 7,
        input_output_aliases={15: 0, 16: 1},
        scratch_shapes=[pltpu.VMEM((width, width), F32), pltpu.VMEM((count, 2 * share, width), F32), sems(2 + rows)],
        compiler_params=params,
        cost_estimate=cost(edge, 2 * edge),
        name="back_edge",
    )(table, inner, outer, side, tiles, turned, w_first, readout, goals, preds, preds_swap, m_one, first, second, sums,
      g_field, gz_one)
    first, second, extra = sum_shares(outs, count, share, width, params)
    return pred_out, first, second, extra[0]


def solution(mesh):
    in_specs = (
        P(("groups", "wide"), "narrow", None, None),
        P(("groups", "wide"), "narrow", None),
        P(),
        P(),
        P(),
        P(),
        P(("groups", "wide"), "narrow", None),
    )
    out_specs = (
        P(("groups", "wide"), "narrow", None),
        P(("groups", "wide", "narrow"), None),
        P(("groups", "wide", "narrow"), None),
        P("groups"),
    )
    return jax.shard_map(
        per_device, mesh=mesh, in_specs=in_specs, out_specs=out_specs, check_vma=False
    )
```

```python
import functools

import jax
import jax.numpy as jnp
import numpy as np
from jax import lax
from jax.experimental import pallas as pl
from jax.experimental.pallas import tpu as pltpu
from jax.sharding import PartitionSpec as P

F32 = jnp.float32
BF16 = jnp.bfloat16
AXES = ("wide", "narrow")
VMEM_LIMIT = 16 * 1024 * 1024
ANY = pl.BlockSpec(memory_space=pl.ANY)
VMEM = pl.BlockSpec(memory_space=pltpu.VMEM)
SMEM = pl.BlockSpec(memory_space=pltpu.SMEM)

SELF, EAST, WEST, NORTH, SOUTH = 0, 1, 2, 3, 4
TAIL = 16


def routes(wide):
    depth = wide // 2

    def at(z, y, c):
        return (2 * z + y) * 2 + c

    every = [(z, y, c) for z in range(depth) for y in range(2) for c in range(2)]
    swap = [(at(z, c, y), at(z, y, c)) for z, y, c in every if y != c]
    first_side = [(at(z, c, 1 - y), at(z, y, c)) for z, y, c in every]
    inner = [(at(z, y, 1 - c), at(z, y, c)) for z, y, c in every]
    outer = [(at(z - 1, y, 1), at(z, y, 0)) for z, y, c in every if c == 0 and z > 0]
    outer += [(at(z + 1, y, 0), at(z, y, 1)) for z, y, c in every if c == 1 and z + 1 < depth]
    side = [(at(z, 1 - y, c), at(z, y, c)) for z, y, c in every]
    return swap, first_side, inner, outer, side


def place():
    half = lax.axis_index("narrow")
    side = lax.rem(lax.axis_index("wide"), 2)
    return half, side, half != side


def start_all(pairs, sems, first=0):
    copies = [pltpu.make_async_copy(a, b, sems.at[first + i]) for i, (a, b) in enumerate(pairs)]
    for copy in copies:
        copy.start()
    return copies


def wait_all(copies):
    for copy in copies:
        copy.wait()


def at_block(col, nodes):
    return pl.ds(col * nodes if isinstance(col, int) else pl.multiple_of(col * nodes, nodes), nodes)


def block_product(table, field, tiles, turned, row, col, shape):
    nodes, rows, cols = shape
    at = row * cols + col
    step = rows * cols

    def block(r, c):
        return field[r, at_block(c, nodes)]

    lhs = jnp.concatenate(
        [
            tiles[table[SELF * step + at]],
            turned[table[SELF * step + at]],
            tiles[table[EAST * step + at]],
            turned[table[WEST * step + at]],
            tiles[table[NORTH * step + at]],
            turned[table[SOUTH * step + at]],
        ],
        axis=1,
    )
    centre = block(row + 1, col + 1)
    rhs = jnp.concatenate(
        [
            centre,
            centre,
            block(row + 2, col + 1),
            block(row, col + 1),
            block(row + 1, col + 2),
            block(row + 1, col),
        ],
        axis=0,
    )
    return jnp.dot(lhs, rhs, preferred_element_type=F32)


def edge_blocks(shape, body, after_row=None):
    _, rows, cols = shape
    half, right, _ = place()

    def one_row(i, carry):
        for col in range(0, cols, 2):
            body(jnp.where(half == i, 0, rows - 1), [col, col + 1])
        if after_row is not None:
            after_row(i)
        return carry

    lax.fori_loop(0, 2, one_row, 0)
    for row in range(1, rows - 1):
        body(row, [jnp.where(right == 0, cols - 1, 0)])


def inner_blocks(shape, body):
    _, rows, cols = shape
    _, right, _ = place()

    def one_row(row, carry):
        for col in range(0, cols - 1, 2):
            body(row, [right + c for c in range(col, min(col + 2, cols - 1))])
        return carry

    lax.fori_loop(1, rows - 1, one_row, 0)


def group(cols, nodes):
    start = cols[0] * nodes
    return pl.ds(start if isinstance(start, int) else pl.multiple_of(start, nodes), len(cols) * nodes)


def group_in_field(cols, nodes):
    return group([cols[0] + 1] + cols[1:], nodes)


def messages(table, field, tiles, turned, row, cols, shape):
    parts = [block_product(table, field, tiles, turned, row, col, shape).astype(BF16) for col in cols]
    return jnp.concatenate(parts, axis=0) if len(parts) > 1 else parts[0]


def forward_one(shape, table, field, tiles, turned, weight, x_field, m_all):
    nodes = shape[0]

    def body(row, cols):
        m = messages(table, field, tiles, turned, row, cols, shape)
        m_all[row, group(cols, nodes)] = m
        z = jnp.dot(m, weight[...], preferred_element_type=F32)
        inside = group_in_field(cols, nodes)
        x_field[row + 1, inside] = (field[row + 1, inside].astype(F32) + jnp.tanh(z)).astype(BF16)

    return body


def residual_columns(seen, goal, scale):
    gp = (seen - goal) * scale
    column = jnp.broadcast_to(gp, (gp.shape[1], gp.shape[1])).T
    return jnp.concatenate([column, column], axis=1)


def through_two(shape, scale, table, field, tiles, turned, weight, weight_turned, readout, spread, goals, m_all, gz_all, g_field, preds, sums):
    nodes = shape[0]
    readf = readout[...].astype(F32)

    def body(row, cols):
        m = messages(table, field, tiles, turned, row, cols, shape)
        here, inside = group(cols, nodes), group_in_field(cols, nodes)
        m_all[row, here] = m
        t = jnp.tanh(jnp.dot(m, weight[...], preferred_element_type=F32))
        x = (field[row + 1, inside].astype(F32) + t).astype(BF16)
        seen = jnp.dot(x, spread[...], preferred_element_type=F32)
        parts = []
        for k, col in enumerate(cols):
            one = seen[k * nodes : (k + 1) * nodes].T[0:1]
            preds[row, pl.ds(col, 1)] = one
            parts.append(residual_columns(one, goals[row, pl.ds(col, 1)], scale))
        gp = jnp.concatenate(parts, axis=0) if len(parts) > 1 else parts[0]
        sums[...] += (x.astype(F32) * gp).reshape(gp.shape[0] // 8, 8, gp.shape[1]).sum(axis=0)
        gz = (gp * readf * (1.0 - t * t)).astype(BF16)
        gz_all[row, here] = gz
        g_field[row + 1, inside] = jnp.dot(gz, weight_turned[...], preferred_element_type=F32).astype(BF16)

    return body


def back_one(shape, scale, table, field, tiles, turned, weight, readout, goals, preds, m_all, gz_all):
    nodes = shape[0]
    readf = readout[...].astype(F32)

    def body(row, cols):
        here = group(cols, nodes)
        t = jnp.tanh(jnp.dot(m_all[row, here], weight[...], preferred_element_type=F32))
        for k, col in enumerate(cols):
            gp = residual_columns(preds[row, pl.ds(col, 1)], goals[row, pl.ds(col, 1)], scale)
            gx = gp * readf + block_product(table, field, tiles, turned, row, col, shape)
            tk = t[k * nodes : (k + 1) * nodes]
            gz_all[row, at_block(col, nodes)] = (gx * (1.0 - tk * tk)).astype(BF16)

    return body


def over_nodes(left, right):
    return lax.dot_general(left, right, (((0,), (0,)), ((), ())), preferred_element_type=F32)


def zero_rim(field, shape):
    nodes, rows, cols = shape
    field[0] = jnp.zeros(field.shape[1:], field.dtype)
    field[rows + 1] = jnp.zeros(field.shape[1:], field.dtype)
    for row in range(1, rows + 1):
        for col in (0, cols + 1):
            field[row, at_block(col, nodes)] = jnp.zeros((nodes, field.shape[2]), field.dtype)


def send_edges(field, outer, inner, side, shape, sems, body):
    nodes, rows, cols = shape
    half, right, _ = place()
    inside = pl.ds(nodes, cols * nodes)
    lines = [
        pltpu.make_async_copy(field.at[jnp.where(half == i, 1, rows), inside], line, sems.at[i])
        for i, line in enumerate((outer, inner))
    ]

    def after_row(i):
        @pl.when(i == 0)
        def _():
            lines[0].start()

        @pl.when(i == 1)
        def _():
            lines[1].start()

    edge_blocks(shape, body, after_row)
    beside = [
        (field.at[row + 1, at_block(jnp.where(right == 0, cols, 1), nodes)], side.at[at_block(row, nodes)])
        for row in range(rows)
    ]
    wait_all(lines + start_all(beside, sems, 2))


def rim_pairs(field, inner, outer, side, shape):
    nodes, rows, cols = shape
    half, right, _ = place()
    zero_col = pl.multiple_of(jnp.where(right == 0, 0, (cols + 1) * nodes), nodes)
    side_col = pl.multiple_of(jnp.where(right == 0, (cols + 1) * nodes, 0), nodes)
    inside = pl.ds(nodes, cols * nodes)
    line = pl.ds(0, cols * nodes)
    for row in range(1, rows + 1):
        field[row, pl.ds(zero_col, nodes)] = jnp.zeros((nodes, field.shape[2]), field.dtype)
    pairs = [
        (inner.at[line], field.at[jnp.where(half == 0, rows + 1, 0), inside]),
        (outer.at[line], field.at[jnp.where(half == 0, 0, rows + 1), inside]),
    ]
    for row in range(rows):
        pairs.append((side.at[pl.ds(row * nodes, nodes)], field.at[row + 1, pl.ds(side_col, nodes)]))
    return pairs


def pack_kernel(nodes, cols, ids, own, ends, side, numbers, ids_in, wide_ids, sems):
    rows, line = own.shape[0], own.shape[1]
    ids_copy = start_all([(ids, ids_in)], sems, 2 + rows)
    half, _, _ = place()
    col = pl.multiple_of(jnp.where(half == 1, 0, (cols - 1) * nodes), nodes)
    pairs = [(own.at[0], ends.at[pl.ds(0, line)]), (own.at[rows - 1], ends.at[pl.ds(line, line)])]
    for row in range(rows):
        pairs.append((own.at[row, pl.ds(col, nodes)], side.at[pl.ds(row * nodes, nodes)]))
    copies = start_all(pairs, sems)
    wait_all(ids_copy)
    wide_ids[...] = jnp.zeros_like(wide_ids)
    for kind in range(3):
        wide_ids[kind * rows : (kind + 1) * rows, 0:cols] = ids_in[kind].astype(F32)
    tail = wide_ids[...].astype(BF16)
    numbers[...] = tail
    ends[2 * line :] = tail
    side[rows * nodes :] = tail
    wait_all(copies)


def middle_kernel(own, after, middle, sems):
    wait_all(start_all([(own.at[pl.ds(1, own.shape[0] - 2)], middle)], sems))


def prepare_kernel(tiles, first, second, plain, turned, first_in, second_in, second_turned, sems):
    wait_all(start_all([(tiles, plain), (first, first_in), (second, second_in)], sems))

    second_turned[...] = second_in[...].T

    def one_tile(tile, carry):
        turned[tile] = plain[tile].T
        return carry

    lax.fori_loop(0, tiles.shape[0], one_tile, 0)


def pick_kernel(numbers, own, ends, after, outer, inner, sems):
    rows, line = own.shape[0], own.shape[1]
    half, _, moved = place()
    whole = pl.ds(0, line)
    tail = pl.ds(line, TAIL)

    @pl.when(moved)
    def _():
        near = pl.multiple_of(jnp.where(half == 0, line, 0), line)
        far = pl.multiple_of(jnp.where(half == 0, 0, line), line)
        wait_all(start_all([
            (ends.at[pl.ds(near, line)], inner.at[whole]),
            (ends.at[pl.ds(far, line)], outer.at[whole]),
            (ends.at[pl.ds(2 * line, TAIL)], inner.at[tail]),
            (ends.at[pl.ds(2 * line, TAIL)], outer.at[tail]),
        ], sems))

    @pl.when(jnp.logical_not(moved))
    def _():
        copies = start_all([
            (own.at[jnp.where(half == 0, rows - 1, 0)], inner.at[whole]),
            (own.at[jnp.where(half == 0, 0, rows - 1)], outer.at[whole]),
        ], sems)
        inner[line:] = numbers[...]
        outer[line:] = numbers[...]
        wait_all(copies)


def first_edge_kernel(shape, numbers, own, ends, middle, outer, inner, side, later, tiles, turned, weight,
                      table, field, x_field, m_all, outer_out, inner_out, side_out, heads, heads_int, marks, sems):
    nodes, rows, cols = shape
    line = cols * nodes
    step = rows * cols
    half, _, moved = place()
    inside = pl.ds(nodes, line)

    def main_pairs(flag):
        if flag:
            pairs = [
                (ends.at[pl.ds(2 * line, TAIL)], heads.at[0]),
                (ends.at[pl.ds(0, line)], field.at[1, inside]),
                (ends.at[pl.ds(line, line)], field.at[rows, inside]),
                (middle, field.at[pl.ds(2, rows - 2), inside]),
            ]
        else:
            pairs = [(numbers, heads.at[0]), (own, field.at[pl.ds(1, rows), inside])]
        return pairs

    def above_pairs(flag):
        return [((inner if flag else outer).at[pl.ds(line, TAIL)], heads.at[1])]

    def either(flag, build, first):
        @pl.when(flag)
        def _():
            start_all(build(True), sems, first)

        @pl.when(jnp.logical_not(flag))
        def _():
            start_all(build(False), sems, first)

    def either_wait(flag, build, first, low, high):
        def some(value):
            for i, (a, b) in list(enumerate(build(value)))[low:high]:
                pltpu.make_async_copy(a, b, sems.at[first + i]).wait()

        @pl.when(flag)
        def _():
            some(True)

        @pl.when(jnp.logical_not(flag))
        def _():
            some(False)

    either(moved, main_pairs, 0)
    either(half == 1, above_pairs, 4)
    left = start_all([(side.at[pl.ds(rows * nodes, TAIL)], heads.at[2])], sems, 5)
    rest = start_all(
        rim_pairs(field, inner, outer, side, shape),
        sems,
        6,
    )
    either_wait(moved, main_pairs, 0, 0, 1)
    either_wait(half == 1, above_pairs, 4, 0, 1)
    wait_all(left)
    heads_int[...] = heads[:, :, 0:128].astype(F32).astype(jnp.int32)
    wait_all(start_all([(heads_int, marks)], sems, 5))

    def fill(at, carry):
        row, col = at // cols, lax.rem(at, cols)
        last = rows - 1
        up = jnp.where(row == 0, marks[1, rows + last, col], marks[0, rows + jnp.maximum(row - 1, 0), col])
        back = jnp.where(
            col == 0, marks[2, 2 * rows + row, cols - 1], marks[0, 2 * rows + row, jnp.maximum(col - 1, 0)]
        )
        table[SELF * step + at] = marks[0, row, col]
        table[EAST * step + at] = marks[0, rows + row, col]
        table[WEST * step + at] = up
        table[NORTH * step + at] = marks[0, 2 * rows + row, col]
        table[SOUTH * step + at] = back
        return carry

    lax.fori_loop(0, step, fill, 0)
    zero_rim(x_field, shape)
    wait_all(rest)
    either_wait(moved, main_pairs, 0, 1, None)

    body = forward_one(shape, table, field, tiles, turned, weight, x_field, m_all)
    send_edges(x_field, outer_out, inner_out, side_out, shape, sems, body)


def middle_compute_kernel(shape, scale, table, field, tiles, turned, weight_one, weight_two, two_turned, readout, spread, target,
                          target_swap, x_in, m_in, x_field, m_one, m_two, gz_two, g_field, preds, goals, sums):
    _, _, moved = place()

    @pl.when(moved)
    def _():
        goals[...] = target_swap[...]

    @pl.when(jnp.logical_not(moved))
    def _():
        goals[...] = target[...]

    zero_rim(g_field, shape)
    sums[...] = jnp.zeros_like(sums)
    inner_blocks(shape, forward_one(shape, table, field, tiles, turned, weight_one, x_field, m_one))
    inner_blocks(shape, through_two(
        shape, scale, table, x_field, tiles, turned, weight_two, two_turned, readout, spread, goals, m_two, gz_two, g_field, preds, sums
    ))


def second_edge_kernel(shape, scale, table, outer, inner, side, tiles, turned, weight, weight_turned, readout, spread, goals,
                       x_in, m_in, gz_in, g_in, preds_in, sums_in,
                       x_field, m_two, gz_two, g_field, preds, sums, outer_out, inner_out, side_out, sems):
    wait_all(start_all(rim_pairs(x_field, inner, outer, side, shape), sems))
    body = through_two(
        shape, scale, table, x_field, tiles, turned, weight, weight_turned, readout, spread, goals, m_two, gz_two,
        g_field, preds, sums,
    )
    send_edges(g_field, outer_out, inner_out, side_out, shape, sems, body)


def back_inner_kernel(shape, scale, table, g_field, tiles, turned, weight, readout, goals, preds, m_one, m_two, gz_two,
                      gz_one, first_out, second_out):
    nodes, rows, cols = shape
    _, right, _ = place()
    inner_blocks(shape, back_one(shape, scale, table, g_field, tiles, turned, weight, readout, goals, preds, m_one, gz_one))
    part = pl.ds(pl.multiple_of(right * nodes, nodes), (cols - 1) * nodes)
    first_out[...] = jnp.zeros_like(first_out)
    second_out[...] = jnp.zeros_like(second_out)

    def one_row(row, carry):
        first_out[...] += over_nodes(m_one[row, part], gz_one[row, part])
        return carry

    def each_row(row, carry):
        second_out[...] += over_nodes(m_two[row], gz_two[row])
        return carry

    lax.fori_loop(1, rows - 1, one_row, 0)
    lax.fori_loop(0, rows, each_row, 0)


def back_edge_kernel(shape, scale, table, outer, inner, side, tiles, turned, weight, readout, goals, preds, preds_swap,
                     m_one, first_in, second, sums, g_in, gz_in, g_field, gz_one, keep, one, two, three, pred_out,
                     first_out, parts, sems):
    nodes, rows, cols = shape
    _, right, moved = place()
    copies = start_all(rim_pairs(g_field, inner, outer, side, shape), sems)

    @pl.when(moved)
    def _():
        pred_out[...] = preds_swap[...]

    @pl.when(jnp.logical_not(moved))
    def _():
        pred_out[...] = preds[...]

    wait_all(copies)
    edge_blocks(shape, back_one(shape, scale, table, g_field, tiles, turned, weight, readout, goals, preds, m_one, gz_one))
    first_out[...] = first_in[...]
    for row in (0, rows - 1):
        first_out[...] += over_nodes(m_one[row], gz_one[row])
    beside = at_block(jnp.where(right == 0, cols - 1, 0), nodes)
    for row in range(1, rows - 1):
        first_out[...] += over_nodes(m_one[row, beside], gz_one[row, beside])
    count, size, width = parts.shape
    parts[:, : size // 2] = first_out[...].reshape(count, size // 2, width)
    parts[:, size // 2 :] = second[...].reshape(count, size // 2, width)
    spread_shares(parts, sums[...], lax.rem(lax.axis_index(AXES), 4), (keep, one, two, three))


def spread_shares(parts, extra, digit, outs):
    size = parts.shape[1]
    for k, out in enumerate(outs):
        for group in range(parts.shape[0] // 4):
            out[group * size : (group + 1) * size] = parts[4 * group + jnp.bitwise_xor(digit, k)]
        out[out.shape[0] - 8 :] = extra


def fold_kernel(base, keep, one, two, three, *refs):
    digit = lax.rem(lax.axis_index(AXES) // base, 4)
    parts = refs[-1]
    count, size, width = parts.shape
    total = keep[...] + one[...] + two[...] + three[...]
    parts[...] = total[: count * size].reshape(count, size, width)
    spread_shares(parts, total[count * size :], digit, refs[:-1])


def last_fold_kernel(keep, one, two, three, first, second, readout):
    share = first.shape[0]
    total = keep[...] + one[...] + two[...] + three[...]
    first[...] = total[:share]
    second[...] = total[share : 2 * share]
    readout[...] = total[2 * share :].sum(axis=0, keepdims=True)


def shares_shape(groups, size, width):
    return (jax.ShapeDtypeStruct((groups * size + 8, width), F32),) * 4


def sum_shares(outs, count, share, width, params):
    base, groups = 1, count // 4
    while True:
        got = [
            lax.ppermute(outs[k], AXES, [(i, i ^ (k * base)) for i in range(count)]) for k in (1, 2, 3)
        ]
        if groups == 1:
            break
        base *= 4
        outs = pl.pallas_call(
            functools.partial(fold_kernel, base),
            out_shape=shares_shape(groups // 4, 2 * share, width),
            in_specs=[VMEM] * 4,
            out_specs=(VMEM,) * 4,
            scratch_shapes=[pltpu.VMEM((groups, 2 * share, width), F32)],
            compiler_params=params,
            name="fold",
        )(outs[0], *got)
        groups //= 4
    small = jax.ShapeDtypeStruct((share, width), F32)
    return pl.pallas_call(
        last_fold_kernel,
        out_shape=(small, small, jax.ShapeDtypeStruct((1, width), F32)),
        in_specs=[VMEM] * 4,
        out_specs=(VMEM,) * 3,
        compiler_params=params,
        name="last_fold",
    )(outs[0], *got)


def per_device(features, tile_ids, tiles, w_first, w_second, readout, target):
    rows, cols, nodes, width = features.shape
    wide, narrow = lax.axis_size("wide"), lax.axis_size("narrow")
    count = wide * narrow
    line, step = cols * nodes, rows * cols
    swap, first_side, inner_way, outer_way, side_way = routes(wide)
    scale = float(np.sqrt(np.float32(width) / np.float32(rows * line * count)))
    params = pltpu.CompilerParams(vmem_limit_bytes=VMEM_LIMIT)

    def send(value, way):
        return lax.ppermute(value, AXES, way)

    def edges(outer, inner, side):
        return send(outer, outer_way), send(inner, inner_way), send(side, side_way)

    def bf(*shape):
        return jax.ShapeDtypeStruct(shape, BF16)

    def sems(number):
        return pltpu.SemaphoreType.DMA((number,))

    features = features.reshape(rows, line, width)
    ends_s, side_s, numbers = pl.pallas_call(
        functools.partial(pack_kernel, nodes, cols),
        out_shape=(bf(2 * line + TAIL, width), bf(rows * nodes + TAIL, width), bf(TAIL, width)),
        in_specs=[ANY, ANY],
        out_specs=(VMEM,) * 3,
        scratch_shapes=[pltpu.VMEM((3, rows, cols), jnp.int32), pltpu.VMEM((TAIL, width), F32), sems(3 + rows)],
        compiler_params=params,
        name="pack",
    )(jnp.transpose(tile_ids, (2, 0, 1)), features)
    ends = send(ends_s, swap)
    side = send(side_s, first_side)
    middle_s = pl.pallas_call(
        middle_kernel,
        out_shape=bf(rows - 2, line, width),
        in_specs=[ANY, ANY],
        out_specs=VMEM,
        scratch_shapes=[sems(1)],
        compiler_params=params,
        name="pack_middle",
    )(features, side_s)
    middle = send(middle_s, swap)
    tiles, w_first, w_second, _ = lax.optimization_barrier((tiles, w_first, w_second, middle_s))
    tiles, turned, w_first, w_second, w_turned = pl.pallas_call(
        prepare_kernel,
        out_shape=(bf(*tiles.shape), bf(*tiles.shape)) + (bf(width, width),) * 3,
        in_specs=[ANY] * 3,
        out_specs=(VMEM,) * 5,
        scratch_shapes=[sems(3)],
        compiler_params=params,
        name="prepare",
    )(tiles, w_first, w_second)
    spread = jnp.broadcast_to(readout[:, None], (width, 128))
    readout = readout[None]

    outer_s, inner_s = pl.pallas_call(
        pick_kernel,
        out_shape=(bf(line + TAIL, width),) * 2,
        in_specs=[VMEM, ANY, ANY, ANY],
        out_specs=(VMEM,) * 2,
        scratch_shapes=[sems(4)],
        compiler_params=params,
        name="pick",
    )(numbers, features, ends, side)
    outer, inner = send(outer_s, outer_way), send(inner_s, inner_way)
    target_s, _ = lax.optimization_barrier((target, inner_s))
    goal_swap = send(target_s, swap)

    shape = (nodes, rows, cols)
    patch, padded = bf(rows, line, width), bf(rows + 2, line + 2 * nodes, width)
    edge_shapes = (bf(line, width), bf(line, width), bf(rows * nodes, width))
    square = jax.ShapeDtypeStruct((width, width), F32)
    sums_shape = jax.ShapeDtypeStruct((8, width), F32)
    goal_shape = jax.ShapeDtypeStruct(target.shape, F32)
    block = nodes * width
    edge, inside = 2 * cols + rows - 2, (rows - 2) * (cols - 1)

    def cost(products, denses):
        return pl.CostEstimate(
            flops=2 * block * (products * 6 * nodes + denses * width),
            bytes_accessed=4 * block * (products + denses),
            transcendentals=block * products,
        )

    table, f_field, x_field, m_one, outer_s, inner_s, side_s = pl.pallas_call(
        functools.partial(first_edge_kernel, shape),
        out_shape=(jax.ShapeDtypeStruct((5 * step,), jnp.int32), padded, padded, patch) + edge_shapes,
        in_specs=[ANY] * 8 + [VMEM] * 3,
        out_specs=(SMEM,) + (VMEM,) * 6,
        scratch_shapes=[
            pltpu.VMEM((3, TAIL, width), BF16),
            pltpu.VMEM((3, TAIL, 128), jnp.int32),
            pltpu.SMEM((3, TAIL, 128), jnp.int32),
            sems(8 + rows),
        ],
        compiler_params=params,
        cost_estimate=cost(edge, edge),
        name="first_edge",
    )(numbers, features, ends, middle, outer, inner, side, goal_swap, tiles, turned, w_first)

    outer, inner, side = edges(outer_s, inner_s, side_s)
    x_field, m_one, m_two, gz_two, g_field, preds, goals, sums = pl.pallas_call(
        functools.partial(middle_compute_kernel, shape, scale),
        out_shape=(padded, patch, patch, patch, padded, goal_shape, goal_shape, sums_shape),
        in_specs=[SMEM] + [VMEM] * 12,
        out_specs=(VMEM,) * 8,
        input_output_aliases={11: 0, 12: 1},
        compiler_params=params,
        cost_estimate=cost(2 * inside, 3 * inside),
        name="inner_forward",
    )(table, f_field, tiles, turned, w_first, w_second, w_turned, readout, spread, target, goal_swap, x_field, m_one)

    x_field, m_two, gz_two, g_field, preds, sums, outer_s, inner_s, side_s = pl.pallas_call(
        functools.partial(second_edge_kernel, shape, scale),
        out_shape=(padded, patch, patch, padded, goal_shape, sums_shape) + edge_shapes,
        in_specs=[SMEM] + [ANY] * 3 + [VMEM] * 13,
        out_specs=(VMEM,) * 9,
        input_output_aliases={11 + i: i for i in range(6)},
        scratch_shapes=[sems(2 + rows)],
        compiler_params=params,
        cost_estimate=cost(edge, 2 * edge),
        name="second_edge",
    )(table, outer, inner, side, tiles, turned, w_second, w_turned, readout, spread, goals, x_field, m_two, gz_two, g_field, preds, sums)

    outer, inner, side = edges(outer_s, inner_s, side_s)
    preds_swap = send(preds, swap)
    gz_one, first, second = pl.pallas_call(
        functools.partial(back_inner_kernel, shape, scale),
        out_shape=(patch, square, square),
        in_specs=[SMEM] + [VMEM] * 10,
        out_specs=(VMEM,) * 3,
        compiler_params=params,
        cost_estimate=cost(inside, 2 * inside + rows * cols),
        name="back_inner",
    )(table, g_field, tiles, turned, w_first, readout, goals, preds, m_one, m_two, gz_two)

    share = width // count
    _, _, *outs, pred_out = pl.pallas_call(
        functools.partial(back_edge_kernel, shape, scale),
        out_shape=(padded, patch) + shares_shape(count // 4, 2 * share, width) + (goal_shape,),
        in_specs=[SMEM] + [ANY] * 3 + [VMEM] * 13,
        out_specs=(VMEM,) * 7,
        input_output_aliases={15: 0, 16: 1},
        scratch_shapes=[pltpu.VMEM((width, width), F32), pltpu.VMEM((count, 2 * share, width), F32), sems(2 + rows)],
        compiler_params=params,
        cost_estimate=cost(edge, 2 * edge),
        name="back_edge",
    )(table, outer, inner, side, tiles, turned, w_first, readout, goals, preds, preds_swap, m_one, first, second, sums,
      g_field, gz_one)
    first, second, extra = sum_shares(outs, count, share, width, params)
    return pred_out, first, second, extra[0]


def solution(mesh):
    in_specs = (
        P(("groups", "wide"), "narrow", None, None),
        P(("groups", "wide"), "narrow", None),
        P(),
        P(),
        P(),
        P(),
        P(("groups", "wide"), "narrow", None),
    )
    out_specs = (
        P(("groups", "wide"), "narrow", None),
        P(("groups", "wide", "narrow"), None),
        P(("groups", "wide", "narrow"), None),
        P("groups"),
    )
    return jax.shard_map(
        per_device, mesh=mesh, in_specs=in_specs, out_specs=out_specs, check_vma=False
    )
```

```python
import functools

import jax
import jax.numpy as jnp
import numpy as np
from jax import lax
from jax.experimental import pallas as pl
from jax.experimental.pallas import tpu as pltpu
from jax.sharding import PartitionSpec as P

F32 = jnp.float32
BF16 = jnp.bfloat16
AXES = ("wide", "narrow")
VMEM_LIMIT = 16 * 1024 * 1024
ANY = pl.BlockSpec(memory_space=pl.ANY)
VMEM = pl.BlockSpec(memory_space=pltpu.VMEM)
SMEM = pl.BlockSpec(memory_space=pltpu.SMEM)

SELF, EAST, WEST, NORTH, SOUTH = 0, 1, 2, 3, 4
TAIL = 16


def routes(wide):
    depth = wide // 2

    def at(z, y, c):
        return (2 * z + y) * 2 + c

    every = [(z, y, c) for z in range(depth) for y in range(2) for c in range(2)]
    swap = [(at(z, c, y), at(z, y, c)) for z, y, c in every if y != c]
    first_side = [(at(z, c, 1 - y), at(z, y, c)) for z, y, c in every]
    inner = [(at(z, y, 1 - c), at(z, y, c)) for z, y, c in every]
    outer = [(at(z - 1, y, 1), at(z, y, 0)) for z, y, c in every if c == 0 and z > 0]
    outer += [(at(z + 1, y, 0), at(z, y, 1)) for z, y, c in every if c == 1 and z + 1 < depth]
    side = [(at(z, 1 - y, c), at(z, y, c)) for z, y, c in every]
    return swap, first_side, inner, outer, side


def place():
    half = lax.axis_index("narrow")
    side = lax.rem(lax.axis_index("wide"), 2)
    return half, side, half != side


def start_all(pairs, sems, first=0):
    copies = [pltpu.make_async_copy(a, b, sems.at[first + i]) for i, (a, b) in enumerate(pairs)]
    for copy in copies:
        copy.start()
    return copies


def wait_all(copies):
    for copy in copies:
        copy.wait()


def at_block(col, nodes):
    return pl.ds(col * nodes if isinstance(col, int) else pl.multiple_of(col * nodes, nodes), nodes)


def block_product(table, field, tiles, turned, row, col, shape):
    nodes, rows, cols = shape

    def number(kind):
        return table[kind * rows + row, col]

    def block(r, c):
        return field[r, at_block(c, nodes)]

    lhs = jnp.concatenate(
        [
            tiles[number(SELF)],
            turned[number(SELF)],
            tiles[number(EAST)],
            turned[number(WEST)],
            tiles[number(NORTH)],
            turned[number(SOUTH)],
        ],
        axis=1,
    )
    centre = block(row + 1, col + 1)
    rhs = jnp.concatenate(
        [
            centre,
            centre,
            block(row + 2, col + 1),
            block(row, col + 1),
            block(row + 1, col + 2),
            block(row + 1, col),
        ],
        axis=0,
    )
    return jnp.dot(lhs, rhs, preferred_element_type=F32)


def edge_blocks(shape):
    _, rows, cols = shape
    half, right, _ = place()
    outer, inner = jnp.where(half == 0, 0, rows - 1), jnp.where(half == 0, rows - 1, 0)
    beside = jnp.where(right == 0, cols - 1, 0)
    blocks = [(outer, col) for col in range(cols)] + [(inner, col) for col in range(cols)]
    return blocks + [(row, beside) for row in range(1, rows - 1)]


def inner_blocks(shape):
    _, rows, cols = shape
    _, right, _ = place()
    return [(row, right + col) for row in range(1, rows - 1) for col in range(cols - 1)]


def gather(read, blocks):
    return jnp.concatenate([read(row, col) for row, col in blocks], axis=0)


def scatter(ref, blocks, value, nodes, shift):
    for k, (row, col) in enumerate(blocks):
        ref[row + shift, at_block(col + shift, nodes)] = value[k * nodes : (k + 1) * nodes]


def messages(table, field, tiles, turned, blocks, shape):
    return gather(
        lambda row, col: block_product(table, field, tiles, turned, row, col, shape).astype(BF16), blocks
    )


def forward_one(shape, table, field, tiles, turned, weight, x_field, m_all):
    nodes = shape[0]

    def body(blocks):
        m = messages(table, field, tiles, turned, blocks, shape)
        scatter(m_all, blocks, m, nodes, 0)
        z = jnp.dot(m, weight[...], preferred_element_type=F32)
        base = gather(lambda row, col: field[row + 1, at_block(col + 1, nodes)], blocks)
        scatter(x_field, blocks, (base.astype(F32) + jnp.tanh(z)).astype(BF16), nodes, 1)

    return body


def residual_columns(seen, goal, scale):
    gp = (seen - goal) * scale
    column = jnp.broadcast_to(gp, (gp.shape[1], gp.shape[1])).T
    return jnp.concatenate([column, column], axis=1)


def through_two(shape, scale, table, field, tiles, turned, weight, weight_turned, readout, spread, goals, m_all, gz_all, g_field, preds, sums):
    nodes = shape[0]
    readf = readout[...].astype(F32)

    def body(blocks):
        m = messages(table, field, tiles, turned, blocks, shape)
        scatter(m_all, blocks, m, nodes, 0)
        t = jnp.tanh(jnp.dot(m, weight[...], preferred_element_type=F32))
        base = gather(lambda row, col: field[row + 1, at_block(col + 1, nodes)], blocks)
        x = (base.astype(F32) + t).astype(BF16)
        seen = jnp.dot(x, spread[...], preferred_element_type=F32)
        parts = []
        for k, (row, col) in enumerate(blocks):
            one = seen[k * nodes : (k + 1) * nodes].T[0:1]
            preds[row, pl.ds(col, 1)] = one
            parts.append(residual_columns(one, goals[row, pl.ds(col, 1)], scale))
        gp = jnp.concatenate(parts, axis=0)
        sums[...] += (x.astype(F32) * gp).reshape(gp.shape[0] // 8, 8, gp.shape[1]).sum(axis=0)
        gz = (gp * readf * (1.0 - t * t)).astype(BF16)
        scatter(gz_all, blocks, gz, nodes, 0)
        g = jnp.dot(gz, weight_turned[...], preferred_element_type=F32).astype(BF16)
        scatter(g_field, blocks, g, nodes, 1)

    return body


def back_one(shape, scale, table, field, tiles, turned, weight, readout, goals, preds, m_all, gz_all):
    nodes = shape[0]
    readf = readout[...].astype(F32)

    def body(blocks):
        m = gather(lambda row, col: m_all[row, at_block(col, nodes)], blocks)
        t = jnp.tanh(jnp.dot(m, weight[...], preferred_element_type=F32))
        gp = gather(
            lambda row, col: residual_columns(preds[row, pl.ds(col, 1)], goals[row, pl.ds(col, 1)], scale), blocks
        )
        gx = gp * readf + gather(
            lambda row, col: block_product(table, field, tiles, turned, row, col, shape), blocks
        )
        scatter(gz_all, blocks, (gx * (1.0 - t * t)).astype(BF16), nodes, 0)

    return body


def over_nodes(left, right):
    return lax.dot_general(left, right, (((0,), (0,)), ((), ())), preferred_element_type=F32)


def zero_rim(field, shape):
    nodes, rows, cols = shape
    field[0] = jnp.zeros(field.shape[1:], field.dtype)
    field[rows + 1] = jnp.zeros(field.shape[1:], field.dtype)
    for row in range(1, rows + 1):
        for col in (0, cols + 1):
            field[row, at_block(col, nodes)] = jnp.zeros((nodes, field.shape[2]), field.dtype)


def take_edges(field, outer, inner, side, shape):
    nodes, rows, cols = shape
    half, right, _ = place()
    inside = pl.ds(nodes, cols * nodes)
    outer[...] = field[jnp.where(half == 0, 1, rows), inside]
    inner[...] = field[jnp.where(half == 0, rows, 1), inside]
    column = at_block(jnp.where(right == 0, cols, 1), nodes)
    for row in range(rows):
        side[at_block(row, nodes)] = field[row + 1, column]


def fill_rim(field, outer, inner, side, shape):
    nodes, rows, cols = shape
    half, right, _ = place()
    inside = pl.ds(nodes, cols * nodes)
    line = pl.ds(0, cols * nodes)
    field[jnp.where(half == 0, 0, rows + 1), inside] = outer[line]
    field[jnp.where(half == 0, rows + 1, 0), inside] = inner[line]
    empty, column = jnp.where(right == 0, 0, cols + 1), jnp.where(right == 0, cols + 1, 0)
    for row in range(rows):
        field[row + 1, at_block(empty, nodes)] = jnp.zeros((nodes, field.shape[2]), field.dtype)
        field[row + 1, at_block(column, nodes)] = side[at_block(row, nodes)]


def pack_kernel(nodes, cols, ids, own, ends, side, numbers, ids_in, wide_ids, sems):
    rows, line = own.shape[0], own.shape[1]
    ids_copy = start_all([(ids, ids_in)], sems, 2 + rows)
    half, _, _ = place()
    col = pl.multiple_of(jnp.where(half == 1, 0, (cols - 1) * nodes), nodes)
    pairs = [(own.at[0], ends.at[pl.ds(0, line)]), (own.at[rows - 1], ends.at[pl.ds(line, line)])]
    for row in range(rows):
        pairs.append((own.at[row, pl.ds(col, nodes)], side.at[pl.ds(row * nodes, nodes)]))
    copies = start_all(pairs, sems)
    wait_all(ids_copy)
    wide_ids[...] = jnp.zeros_like(wide_ids)
    for kind in range(3):
        wide_ids[kind * rows : (kind + 1) * rows, 0:cols] = ids_in[kind].astype(F32)
    tail = wide_ids[...].astype(BF16)
    numbers[...] = tail
    ends[2 * line :] = tail
    side[rows * nodes :] = tail
    wait_all(copies)


def middle_kernel(own, after, middle, sems):
    wait_all(start_all([(own.at[pl.ds(1, own.shape[0] - 2)], middle)], sems))


def prepare_kernel(tiles, first, second, plain, turned, first_in, second_in, second_turned, sems):
    wait_all(start_all([(tiles, plain), (first, first_in), (second, second_in)], sems))

    second_turned[...] = second_in[...].T

    def one_tile(tile, carry):
        turned[tile] = plain[tile].T
        return carry

    lax.fori_loop(0, tiles.shape[0], one_tile, 0)


def pick_kernel(numbers, own, ends, after, outer, inner, sems):
    rows, line = own.shape[0], own.shape[1]
    half, _, moved = place()
    whole = pl.ds(0, line)
    tail = pl.ds(line, TAIL)

    @pl.when(moved)
    def _():
        near = pl.multiple_of(jnp.where(half == 0, line, 0), line)
        far = pl.multiple_of(jnp.where(half == 0, 0, line), line)
        wait_all(start_all([
            (ends.at[pl.ds(near, line)], inner.at[whole]),
            (ends.at[pl.ds(far, line)], outer.at[whole]),
            (ends.at[pl.ds(2 * line, TAIL)], inner.at[tail]),
            (ends.at[pl.ds(2 * line, TAIL)], outer.at[tail]),
        ], sems))

    @pl.when(jnp.logical_not(moved))
    def _():
        copies = start_all([
            (own.at[jnp.where(half == 0, rows - 1, 0)], inner.at[whole]),
            (own.at[jnp.where(half == 0, 0, rows - 1)], outer.at[whole]),
        ], sems)
        inner[line:] = numbers[...]
        outer[line:] = numbers[...]
        wait_all(copies)


def first_edge_kernel(shape, numbers, own, ends, middle, outer, inner, side, later, tiles, turned, weight,
                      table, field, x_field, m_all, outer_out, inner_out, side_out, own_ids, above_ids, spots, sems):
    nodes, rows, cols = shape
    line = cols * nodes
    half, right, moved = place()
    inside = pl.ds(nodes, line)
    tail = pl.ds(line, TAIL)

    @pl.when(moved)
    def _():
        own_ids[...] = ends[pl.ds(2 * line, TAIL)].astype(F32)

    @pl.when(jnp.logical_not(moved))
    def _():
        own_ids[...] = numbers[...].astype(F32)

    @pl.when(half == 1)
    def _():
        above_ids[...] = inner[tail].astype(F32)

    @pl.when(half == 0)
    def _():
        above_ids[...] = outer[tail].astype(F32)

    left = side[pl.ds(rows * nodes, TAIL)].astype(F32)[2 * rows : 3 * rows, 0:128]
    north = own_ids[2 * rows : 3 * rows, 0:128]
    lanes = lax.broadcasted_iota(jnp.int32, north.shape, 1)
    last = jnp.broadcast_to(left[:, cols - 1 : cols], left.shape)
    spots[0 : 2 * rows] = own_ids[0 : 2 * rows, 0:128].astype(jnp.int32)
    spots[WEST * rows : WEST * rows + 1] = above_ids[2 * rows - 1 : 2 * rows, 0:128].astype(jnp.int32)
    spots[WEST * rows + 1 : (WEST + 1) * rows] = own_ids[rows : 2 * rows - 1, 0:128].astype(jnp.int32)
    spots[NORTH * rows : (NORTH + 1) * rows] = north.astype(jnp.int32)
    spots[SOUTH * rows : (SOUTH + 1) * rows] = jnp.where(lanes == 0, last, pltpu.roll(north, 1, 1)).astype(jnp.int32)
    copies = start_all([(spots, table)], sems)

    @pl.when(moved)
    def _():
        field[1, inside] = ends[pl.ds(0, line)]
        field[rows, inside] = ends[pl.ds(line, line)]
        for row in range(2, rows):
            field[row, inside] = middle[row - 2]

    @pl.when(jnp.logical_not(moved))
    def _():
        for row in range(rows):
            field[row + 1, inside] = own[row]

    fill_rim(field, outer, inner, side, shape)
    zero_rim(x_field, shape)
    wait_all(copies)
    forward_one(shape, table, field, tiles, turned, weight, x_field, m_all)(edge_blocks(shape))
    take_edges(x_field, outer_out, inner_out, side_out, shape)


def middle_compute_kernel(shape, scale, table, field, tiles, turned, weight_one, weight_two, two_turned, readout, spread, target,
                          target_swap, x_in, m_in, x_field, m_one, m_two, gz_two, g_field, preds, goals, sums):
    _, _, moved = place()

    @pl.when(moved)
    def _():
        goals[...] = target_swap[...]

    @pl.when(jnp.logical_not(moved))
    def _():
        goals[...] = target[...]

    zero_rim(g_field, shape)
    sums[...] = jnp.zeros_like(sums)
    blocks = inner_blocks(shape)
    forward_one(shape, table, field, tiles, turned, weight_one, x_field, m_one)(blocks)
    through_two(
        shape, scale, table, x_field, tiles, turned, weight_two, two_turned, readout, spread, goals, m_two, gz_two,
        g_field, preds, sums,
    )(blocks)


def second_edge_kernel(shape, scale, table, outer, inner, side, tiles, turned, weight, weight_turned, readout, spread, goals,
                       x_in, m_in, gz_in, g_in, preds_in, sums_in,
                       x_field, m_two, gz_two, g_field, preds, sums, outer_out, inner_out, side_out):
    fill_rim(x_field, outer, inner, side, shape)
    through_two(
        shape, scale, table, x_field, tiles, turned, weight, weight_turned, readout, spread, goals, m_two, gz_two,
        g_field, preds, sums,
    )(edge_blocks(shape))
    take_edges(g_field, outer_out, inner_out, side_out, shape)


def back_inner_kernel(shape, scale, table, g_field, tiles, turned, weight, readout, goals, preds, m_one, m_two, gz_two,
                      gz_one, first_out, second_out):
    nodes, rows, cols = shape
    _, right, _ = place()
    back_one(shape, scale, table, g_field, tiles, turned, weight, readout, goals, preds, m_one, gz_one)(
        inner_blocks(shape)
    )
    part = pl.ds(pl.multiple_of(right * nodes, nodes), (cols - 1) * nodes)
    first_out[...] = jnp.zeros_like(first_out)
    second_out[...] = jnp.zeros_like(second_out)

    def one_row(row, carry):
        first_out[...] += over_nodes(m_one[row, part], gz_one[row, part])
        return carry

    def each_row(row, carry):
        second_out[...] += over_nodes(m_two[row], gz_two[row])
        return carry

    lax.fori_loop(1, rows - 1, one_row, 0)
    lax.fori_loop(0, rows, each_row, 0)


def back_edge_kernel(shape, scale, table, outer, inner, side, tiles, turned, weight, readout, goals, preds,
                     m_one, first_in, second, sums, g_in, gz_in, g_field, gz_one, keep, one, two, three,
                     first_out, parts):
    nodes, rows, cols = shape
    _, right, _ = place()
    fill_rim(g_field, outer, inner, side, shape)
    back_one(shape, scale, table, g_field, tiles, turned, weight, readout, goals, preds, m_one, gz_one)(
        edge_blocks(shape)
    )
    first_out[...] = first_in[...]
    for row in (0, rows - 1):
        first_out[...] += over_nodes(m_one[row], gz_one[row])
    beside = at_block(jnp.where(right == 0, cols - 1, 0), nodes)
    for row in range(1, rows - 1):
        first_out[...] += over_nodes(m_one[row, beside], gz_one[row, beside])
    count, size, width = parts.shape
    parts[:, : size // 2] = first_out[...].reshape(count, size // 2, width)
    parts[:, size // 2 :] = second[...].reshape(count, size // 2, width)
    spread_shares(parts, sums[...], lax.rem(lax.axis_index(AXES), 4), (keep, one, two, three))
    ride_preds(preds, three)


def spread_shares(parts, extra, digit, outs):
    size = parts.shape[1]
    for k, out in enumerate(outs):
        for group in range(parts.shape[0] // 4):
            out[group * size : (group + 1) * size] = parts[4 * group + jnp.bitwise_xor(digit, k)]
        out[parts.shape[0] // 4 * size : parts.shape[0] // 4 * size + 8] = extra


def take_preds(preds, riding, pred_out):
    _, _, moved = place()
    start = riding.shape[0] - preds.shape[0] * preds.shape[1] // 2

    @pl.when(moved)
    def _():
        for row in range(preds.shape[0]):
            at = start + row // 2 * preds.shape[1]
            lane = row % 2 * preds.shape[2]
            pred_out[row] = riding[at : at + preds.shape[1], lane : lane + preds.shape[2]]

    @pl.when(jnp.logical_not(moved))
    def _():
        pred_out[...] = preds[...]


def ride_preds(preds, riding):
    start = riding.shape[0] - preds.shape[0] * preds.shape[1] // 2
    for row in range(preds.shape[0]):
        at = start + row // 2 * preds.shape[1]
        lane = row % 2 * preds.shape[2]
        riding[at : at + preds.shape[1], lane : lane + preds.shape[2]] = preds[row]


def fold_kernel(base, keep, one, two, three, preds, *refs):
    digit = lax.rem(lax.axis_index(AXES) // base, 4)
    *outs, parts = refs
    if base == 4:
        take_preds(preds, three, outs.pop())
    count, size, width = parts.shape
    total = keep[...] + one[...] + two[...] + three[: keep.shape[0]]
    parts[...] = total[: count * size].reshape(count, size, width)
    spread_shares(parts, total[count * size :], digit, outs)


def last_fold_kernel(keep, one, two, three, first, second, readout):
    share = first.shape[0]
    total = keep[...] + one[...] + two[...] + three[...]
    first[...] = total[:share]
    second[...] = total[share : 2 * share]
    readout[...] = total[2 * share :].sum(axis=0, keepdims=True)


def shares_shape(groups, size, width, riding=0):
    rows = (groups * size + 8,) * 3 + (groups * size + 8 + riding,)
    return tuple(jax.ShapeDtypeStruct((number, width), F32) for number in rows)


def sum_shares(outs, preds, count, share, width, params):
    base, groups, pred_out = 1, count // 4, ()
    while True:
        got = [
            lax.ppermute(outs[k], AXES, [(i, i ^ (k * base)) for i in range(count)]) for k in (1, 2, 3)
        ]
        if groups == 1:
            break
        base *= 4
        more = (jax.ShapeDtypeStruct(preds.shape, F32),) if base == 4 else ()
        *outs, last = pl.pallas_call(
            functools.partial(fold_kernel, base),
            out_shape=shares_shape(groups // 4, 2 * share, width) + more,
            in_specs=[VMEM] * 5,
            out_specs=(VMEM,) * (4 + len(more)),
            scratch_shapes=[pltpu.VMEM((groups, 2 * share, width), F32)],
            compiler_params=params,
            name="fold",
        )(outs[0], *got, preds)
        if more:
            pred_out = last
        else:
            outs.append(last)
        groups //= 4
    small = jax.ShapeDtypeStruct((share, width), F32)
    sums = pl.pallas_call(
        last_fold_kernel,
        out_shape=(small, small, jax.ShapeDtypeStruct((1, width), F32)),
        in_specs=[VMEM] * 4,
        out_specs=(VMEM,) * 3,
        compiler_params=params,
        name="last_fold",
    )(outs[0], *got)
    return *sums, pred_out


def per_device(features, tile_ids, tiles, w_first, w_second, readout, target):
    rows, cols, nodes, width = features.shape
    wide, narrow = lax.axis_size("wide"), lax.axis_size("narrow")
    count = wide * narrow
    line, step = cols * nodes, rows * cols
    swap, first_side, inner_way, outer_way, side_way = routes(wide)
    scale = float(np.sqrt(np.float32(width) / np.float32(rows * line * count)))
    params = pltpu.CompilerParams(vmem_limit_bytes=VMEM_LIMIT)

    def send(value, way):
        return lax.ppermute(value, AXES, way)

    def edges(outer, inner, side):
        return send(outer, outer_way), send(inner, inner_way), send(side, side_way)

    def bf(*shape):
        return jax.ShapeDtypeStruct(shape, BF16)

    def sems(number):
        return pltpu.SemaphoreType.DMA((number,))

    features = features.reshape(rows, line, width)
    ends_s, side_s, numbers = pl.pallas_call(
        functools.partial(pack_kernel, nodes, cols),
        out_shape=(bf(2 * line + TAIL, width), bf(rows * nodes + TAIL, width), bf(TAIL, width)),
        in_specs=[ANY, ANY],
        out_specs=(VMEM,) * 3,
        scratch_shapes=[pltpu.VMEM((3, rows, cols), jnp.int32), pltpu.VMEM((TAIL, width), F32), sems(3 + rows)],
        compiler_params=params,
        name="pack",
    )(jnp.transpose(tile_ids, (2, 0, 1)), features)
    ends = send(ends_s, swap)
    side = send(side_s, first_side)
    middle_s = pl.pallas_call(
        middle_kernel,
        out_shape=bf(rows - 2, line, width),
        in_specs=[ANY, ANY],
        out_specs=VMEM,
        scratch_shapes=[sems(1)],
        compiler_params=params,
        name="pack_middle",
    )(features, side_s)
    middle = send(middle_s, swap)
    tiles, w_first, w_second, _ = lax.optimization_barrier((tiles, w_first, w_second, middle_s))
    tiles, turned, w_first, w_second, w_turned = pl.pallas_call(
        prepare_kernel,
        out_shape=(bf(*tiles.shape), bf(*tiles.shape)) + (bf(width, width),) * 3,
        in_specs=[ANY] * 3,
        out_specs=(VMEM,) * 5,
        scratch_shapes=[sems(3)],
        compiler_params=params,
        name="prepare",
    )(tiles, w_first, w_second)
    spread = jnp.broadcast_to(readout[:, None], (width, 128))
    readout = readout[None]

    outer_s, inner_s = pl.pallas_call(
        pick_kernel,
        out_shape=(bf(line + TAIL, width),) * 2,
        in_specs=[VMEM, ANY, ANY, ANY],
        out_specs=(VMEM,) * 2,
        scratch_shapes=[sems(4)],
        compiler_params=params,
        name="pick",
    )(numbers, features, ends, side)
    outer, inner = send(outer_s, outer_way), send(inner_s, inner_way)
    target_s, _ = lax.optimization_barrier((target, inner_s))
    goal_swap = send(target_s, swap)

    shape = (nodes, rows, cols)
    patch, padded = bf(rows, line, width), bf(rows + 2, line + 2 * nodes, width)
    edge_shapes = (bf(line, width), bf(line, width), bf(rows * nodes, width))
    square = jax.ShapeDtypeStruct((width, width), F32)
    sums_shape = jax.ShapeDtypeStruct((8, width), F32)
    goal_shape = jax.ShapeDtypeStruct(target.shape, F32)
    block = nodes * width
    edge, inside = 2 * cols + rows - 2, (rows - 2) * (cols - 1)

    def cost(products, denses):
        return pl.CostEstimate(
            flops=2 * block * (products * 6 * nodes + denses * width),
            bytes_accessed=4 * block * (products + denses),
            transcendentals=block * products,
        )

    table, f_field, x_field, m_one, outer_s, inner_s, side_s = pl.pallas_call(
        functools.partial(first_edge_kernel, shape),
        out_shape=(jax.ShapeDtypeStruct((5 * rows, 128), jnp.int32), padded, padded, patch) + edge_shapes,
        in_specs=[VMEM] * 7 + [ANY] + [VMEM] * 3,
        out_specs=(SMEM,) + (VMEM,) * 6,
        scratch_shapes=[
            pltpu.VMEM((TAIL, width), F32),
            pltpu.VMEM((TAIL, width), F32),
            pltpu.VMEM((5 * rows, 128), jnp.int32),
            sems(1),
        ],
        compiler_params=params,
        cost_estimate=cost(edge, edge),
        name="first_edge",
    )(numbers, features, ends, middle, outer, inner, side, goal_swap, tiles, turned, w_first)

    outer, inner, side = edges(outer_s, inner_s, side_s)
    x_field, m_one, m_two, gz_two, g_field, preds, goals, sums = pl.pallas_call(
        functools.partial(middle_compute_kernel, shape, scale),
        out_shape=(padded, patch, patch, patch, padded, goal_shape, goal_shape, sums_shape),
        in_specs=[SMEM] + [VMEM] * 12,
        out_specs=(VMEM,) * 8,
        input_output_aliases={11: 0, 12: 1},
        compiler_params=params,
        cost_estimate=cost(2 * inside, 3 * inside),
        name="inner_forward",
    )(table, f_field, tiles, turned, w_first, w_second, w_turned, readout, spread, target, goal_swap, x_field, m_one)

    x_field, m_two, gz_two, g_field, preds, sums, outer_s, inner_s, side_s = pl.pallas_call(
        functools.partial(second_edge_kernel, shape, scale),
        out_shape=(padded, patch, patch, padded, goal_shape, sums_shape) + edge_shapes,
        in_specs=[SMEM] + [VMEM] * 16,
        out_specs=(VMEM,) * 9,
        input_output_aliases={11 + i: i for i in range(6)},
        compiler_params=params,
        cost_estimate=cost(edge, 2 * edge),
        name="second_edge",
    )(table, outer, inner, side, tiles, turned, w_second, w_turned, readout, spread, goals, x_field, m_two, gz_two, g_field, preds, sums)

    outer, inner, side = edges(outer_s, inner_s, side_s)
    gz_one, first, second = pl.pallas_call(
        functools.partial(back_inner_kernel, shape, scale),
        out_shape=(patch, square, square),
        in_specs=[SMEM] + [VMEM] * 10,
        out_specs=(VMEM,) * 3,
        compiler_params=params,
        cost_estimate=cost(inside, 2 * inside + rows * cols),
        name="back_inner",
    )(table, g_field, tiles, turned, w_first, readout, goals, preds, m_one, m_two, gz_two)

    share = width // count
    _, _, *outs = pl.pallas_call(
        functools.partial(back_edge_kernel, shape, scale),
        out_shape=(padded, patch) + shares_shape(count // 4, 2 * share, width, step * nodes // width),
        in_specs=[SMEM] + [VMEM] * 15,
        out_specs=(VMEM,) * 6,
        input_output_aliases={14: 0, 15: 1},
        scratch_shapes=[pltpu.VMEM((width, width), F32), pltpu.VMEM((count, 2 * share, width), F32)],
        compiler_params=params,
        cost_estimate=cost(edge, 2 * edge),
        name="back_edge",
    )(table, outer, inner, side, tiles, turned, w_first, readout, goals, preds, m_one, first, second, sums,
      g_field, gz_one)
    first, second, extra, pred_out = sum_shares(outs, preds, count, share, width, params)
    return pred_out, first, second, extra[0]


def solution(mesh):
    in_specs = (
        P(("groups", "wide"), "narrow", None, None),
        P(("groups", "wide"), "narrow", None),
        P(),
        P(),
        P(),
        P(),
        P(("groups", "wide"), "narrow", None),
    )
    out_specs = (
        P(("groups", "wide"), "narrow", None),
        P(("groups", "wide", "narrow"), None),
        P(("groups", "wide", "narrow"), None),
        P("groups"),
    )
    return jax.shard_map(
        per_device, mesh=mesh, in_specs=in_specs, out_specs=out_specs, check_vma=False
    )
```

```python
import functools

import jax
import jax.numpy as jnp
import numpy as np
from jax import lax
from jax.experimental import pallas as pl
from jax.experimental.pallas import tpu as pltpu
from jax.sharding import PartitionSpec as P

F32 = jnp.float32
BF16 = jnp.bfloat16
AXES = ("wide", "narrow")
VMEM_LIMIT = 16 * 1024 * 1024
ANY = pl.BlockSpec(memory_space=pl.ANY)
VMEM = pl.BlockSpec(memory_space=pltpu.VMEM)
SMEM = pl.BlockSpec(memory_space=pltpu.SMEM)

SELF, EAST, WEST, NORTH, SOUTH = 0, 1, 2, 3, 4
TAIL = 16


def routes(wide):
    depth = wide // 2

    def at(z, y, c):
        return (2 * z + y) * 2 + c

    every = [(z, y, c) for z in range(depth) for y in range(2) for c in range(2)]
    swap = [(at(z, c, y), at(z, y, c)) for z, y, c in every if y != c]
    first_side = [(at(z, c, 1 - y), at(z, y, c)) for z, y, c in every]
    inner = [(at(z, y, 1 - c), at(z, y, c)) for z, y, c in every]
    outer = [(at(z - 1, y, 1), at(z, y, 0)) for z, y, c in every if c == 0 and z > 0]
    outer += [(at(z + 1, y, 0), at(z, y, 1)) for z, y, c in every if c == 1 and z + 1 < depth]
    side = [(at(z, 1 - y, c), at(z, y, c)) for z, y, c in every]
    return swap, first_side, inner, outer, side


def place():
    half = lax.axis_index("narrow")
    side = lax.rem(lax.axis_index("wide"), 2)
    return half, side, half != side


def start_all(pairs, sems, first=0):
    copies = [pltpu.make_async_copy(a, b, sems.at[first + i]) for i, (a, b) in enumerate(pairs)]
    for copy in copies:
        copy.start()
    return copies


def wait_all(copies):
    for copy in copies:
        copy.wait()


def at_block(col, nodes):
    return pl.ds(col * nodes if isinstance(col, int) else pl.multiple_of(col * nodes, nodes), nodes)


def block_product(table, field, tiles, row, col, shape):
    nodes, rows, cols = shape

    def number(kind):
        return table[kind * rows + row, col]

    def block(r, c):
        return field[r, at_block(c, nodes)]

    half = tiles.shape[0] // 2
    lhs = jnp.concatenate(
        [
            tiles[number(SELF)],
            tiles[half + number(SELF)],
            tiles[number(EAST)],
            tiles[half + number(WEST)],
            tiles[number(NORTH)],
            tiles[half + number(SOUTH)],
        ],
        axis=1,
    )
    centre = block(row + 1, col + 1)
    rhs = jnp.concatenate(
        [
            centre,
            centre,
            block(row + 2, col + 1),
            block(row, col + 1),
            block(row + 1, col + 2),
            block(row + 1, col),
        ],
        axis=0,
    )
    return jnp.dot(lhs, rhs, preferred_element_type=F32)


def edge_blocks(shape):
    _, rows, cols = shape
    half, right, _ = place()
    outer, inner = jnp.where(half == 0, 0, rows - 1), jnp.where(half == 0, rows - 1, 0)
    beside = jnp.where(right == 0, cols - 1, 0)
    blocks = [(outer, col) for col in range(cols)] + [(inner, col) for col in range(cols)]
    return blocks + [(row, beside) for row in range(1, rows - 1)]


def inner_blocks(shape):
    _, rows, cols = shape
    _, right, _ = place()
    return [(row, right + col) for row in range(1, rows - 1) for col in range(cols - 1)]


def gather(read, blocks):
    return jnp.concatenate([read(row, col) for row, col in blocks], axis=0)


def scatter(ref, blocks, value, nodes, shift):
    for k, (row, col) in enumerate(blocks):
        ref[row + shift, at_block(col + shift, nodes)] = value[k * nodes : (k + 1) * nodes]


def messages(table, field, tiles, blocks, shape):
    return gather(
        lambda row, col: block_product(table, field, tiles, row, col, shape).astype(BF16), blocks
    )


def rim_terms(table, tiles, outer, inner, side, shape):
    nodes, rows, cols = shape
    half, right, _ = place()
    turned = tiles.shape[0] // 2

    def product(tile, block):
        return jnp.dot(tiles[tile], block, preferred_element_type=F32)

    def beside(row):
        tile = jnp.where(right == 0, table[NORTH * rows + row, cols - 1], turned + table[SOUTH * rows + row, 0])
        return product(tile, side[at_block(row, nodes)])

    terms = []
    first, last = jnp.where(half == 0, 0, rows - 1), jnp.where(half == 0, rows - 1, 0)
    for line, row, upward in ((outer, first, half == 0), (inner, last, half == 1)):
        corner = beside(row)
        for col in range(cols):
            tile = jnp.where(upward, turned + table[WEST * rows + row, col], table[EAST * rows + row, col])
            term = product(tile, line[at_block(col, nodes)])
            if col in (0, cols - 1):
                term = term + jnp.where((right == 0) == (col > 0), corner, 0.0)
            terms.append(term)
    return jnp.concatenate(terms + [beside(row) for row in range(1, rows - 1)], axis=0)


def products(table, field, tiles, blocks, shape):
    return gather(lambda row, col: block_product(table, field, tiles, row, col, shape), blocks)


def forward_one(shape, table, field, tiles, weight, x_field, m_all):
    nodes = shape[0]

    def body(blocks):
        m = messages(table, field, tiles, blocks, shape)
        scatter(m_all, blocks, m, nodes, 0)
        z = jnp.dot(m, weight[...], preferred_element_type=F32)
        base = gather(lambda row, col: field[row + 1, at_block(col + 1, nodes)], blocks)
        scatter(x_field, blocks, (base.astype(F32) + jnp.tanh(z)).astype(BF16), nodes, 1)

    return body


def residual_columns(seen, goal, scale):
    gp = (seen - goal) * scale
    column = jnp.broadcast_to(gp, (gp.shape[1], gp.shape[1])).T
    return jnp.concatenate([column, column], axis=1)


def through_two(shape, scale, table, field, tiles, weight, weight_turned, readout, spread, goals, m_all, gz_all, g_field, preds, sums):
    nodes = shape[0]
    readf = readout[...].astype(F32)

    def body(blocks, m):
        scatter(m_all, blocks, m, nodes, 0)
        t = jnp.tanh(jnp.dot(m, weight[...], preferred_element_type=F32))
        base = gather(lambda row, col: field[row + 1, at_block(col + 1, nodes)], blocks)
        x = (base.astype(F32) + t).astype(BF16)
        seen = jnp.dot(x, spread[...], preferred_element_type=F32)
        parts = []
        for k, (row, col) in enumerate(blocks):
            one = seen[k * nodes : (k + 1) * nodes].T[0:1]
            preds[row, pl.ds(col, 1)] = one
            parts.append(residual_columns(one, goals[row, pl.ds(col, 1)], scale))
        gp = jnp.concatenate(parts, axis=0)
        sums[...] += (x.astype(F32) * gp).reshape(gp.shape[0] // 8, 8, gp.shape[1]).sum(axis=0)
        gz = (gp * readf * (1.0 - t * t)).astype(BF16)
        scatter(gz_all, blocks, gz, nodes, 0)
        g = jnp.dot(gz, weight_turned[...], preferred_element_type=F32).astype(BF16)
        scatter(g_field, blocks, g, nodes, 1)

    return body


def back_terms(scale, weight, readout, goals, preds, m_all, blocks, nodes):
    m = gather(lambda row, col: m_all[row, at_block(col, nodes)], blocks)
    t = jnp.tanh(jnp.dot(m, weight[...], preferred_element_type=F32))
    gp = gather(
        lambda row, col: residual_columns(preds[row, pl.ds(col, 1)], goals[row, pl.ds(col, 1)], scale), blocks
    )
    return gp * readout[...].astype(F32), 1.0 - t * t


def over_nodes(left, right):
    return lax.dot_general(left, right, (((0,), (0,)), ((), ())), preferred_element_type=F32)


def zero_rim(field, shape):
    nodes, rows, cols = shape
    field[0] = jnp.zeros(field.shape[1:], field.dtype)
    field[rows + 1] = jnp.zeros(field.shape[1:], field.dtype)
    for row in range(1, rows + 1):
        for col in (0, cols + 1):
            field[row, at_block(col, nodes)] = jnp.zeros((nodes, field.shape[2]), field.dtype)


def take_edges(field, outer, inner, side, shape):
    nodes, rows, cols = shape
    half, right, _ = place()
    inside = pl.ds(nodes, cols * nodes)
    outer[...] = field[jnp.where(half == 0, 1, rows), inside]
    inner[...] = field[jnp.where(half == 0, rows, 1), inside]
    column = at_block(jnp.where(right == 0, cols, 1), nodes)
    for row in range(rows):
        side[at_block(row, nodes)] = field[row + 1, column]


def fill_rim(field, outer, inner, side, shape):
    nodes, rows, cols = shape
    half, right, _ = place()
    inside = pl.ds(nodes, cols * nodes)
    line = pl.ds(0, cols * nodes)
    field[jnp.where(half == 0, 0, rows + 1), inside] = outer[line]
    field[jnp.where(half == 0, rows + 1, 0), inside] = inner[line]
    empty, column = jnp.where(right == 0, 0, cols + 1), jnp.where(right == 0, cols + 1, 0)
    for row in range(rows):
        field[row + 1, at_block(empty, nodes)] = jnp.zeros((nodes, field.shape[2]), field.dtype)
        field[row + 1, at_block(column, nodes)] = side[at_block(row, nodes)]


def pack_kernel(nodes, cols, ids, own, ends, side, numbers, ids_in, wide_ids, sems):
    rows, line = own.shape[0], own.shape[1]
    ids_copy = start_all([(ids, ids_in)], sems, 2 + rows)
    half, _, _ = place()
    col = pl.multiple_of(jnp.where(half == 1, 0, (cols - 1) * nodes), nodes)
    pairs = [(own.at[0], ends.at[pl.ds(0, line)]), (own.at[rows - 1], ends.at[pl.ds(line, line)])]
    for row in range(rows):
        pairs.append((own.at[row, pl.ds(col, nodes)], side.at[pl.ds(row * nodes, nodes)]))
    copies = start_all(pairs, sems)
    wait_all(ids_copy)
    wide_ids[...] = jnp.zeros_like(wide_ids)
    for kind in range(3):
        wide_ids[kind * rows : (kind + 1) * rows, 0:cols] = ids_in[kind].astype(F32)
    tail = wide_ids[...].astype(BF16)
    numbers[...] = tail
    ends[2 * line :] = tail
    side[rows * nodes :] = tail
    wait_all(copies)


def middle_kernel(own, after, middle, sems):
    wait_all(start_all([(own.at[pl.ds(1, own.shape[0] - 2)], middle)], sems))


def prepare_kernel(tiles, first, second, both, first_in, second_in, second_turned, sems):
    number = tiles.shape[0]
    wait_all(start_all([(tiles, both.at[pl.ds(0, number)]), (first, first_in), (second, second_in)], sems))

    second_turned[...] = second_in[...].T

    def one_tile(tile, carry):
        both[number + tile] = both[tile].T
        return carry

    lax.fori_loop(0, number, one_tile, 0)


def pick_kernel(numbers, own, ends, after, outer, inner, sems):
    rows, line = own.shape[0], own.shape[1]
    half, _, moved = place()
    whole = pl.ds(0, line)
    tail = pl.ds(line, TAIL)

    @pl.when(moved)
    def _():
        outer[tail] = ends[pl.ds(2 * line, TAIL)]
        inner[tail] = ends[pl.ds(2 * line, TAIL)]
        outer[whole] = ends[pl.ds(pl.multiple_of(half * line, line), line)]
        inner[whole] = ends[pl.ds(pl.multiple_of((1 - half) * line, line), line)]

    @pl.when(jnp.logical_not(moved))
    def _():
        copies = start_all([
            (own.at[jnp.where(half == 0, 0, rows - 1)], outer.at[whole]),
            (own.at[jnp.where(half == 0, rows - 1, 0)], inner.at[whole]),
        ], sems)
        outer[tail] = numbers[...]
        inner[tail] = numbers[...]
        wait_all(copies)


def first_edge_kernel(shape, numbers, own, ends, middle, outer, inner, side, later, tiles, weight,
                      table, field, x_field, m_all, outer_out, inner_out, side_out, own_ids, above_ids, spots, sems):
    nodes, rows, cols = shape
    line = cols * nodes
    half, right, moved = place()
    inside = pl.ds(nodes, line)
    tail = pl.ds(line, TAIL)

    @pl.when(moved)
    def _():
        own_ids[...] = ends[pl.ds(2 * line, TAIL)].astype(F32)

    @pl.when(jnp.logical_not(moved))
    def _():
        own_ids[...] = numbers[...].astype(F32)

    @pl.when(half == 1)
    def _():
        above_ids[...] = inner[tail].astype(F32)

    @pl.when(half == 0)
    def _():
        above_ids[...] = outer[tail].astype(F32)

    left = side[pl.ds(rows * nodes, TAIL)].astype(F32)[2 * rows : 3 * rows, 0:128]
    north = own_ids[2 * rows : 3 * rows, 0:128]
    lanes = lax.broadcasted_iota(jnp.int32, north.shape, 1)
    beside = jnp.broadcast_to(left[:, cols - 1 : cols], left.shape)
    spots[0 : 2 * rows] = own_ids[0 : 2 * rows, 0:128].astype(jnp.int32)
    spots[WEST * rows : WEST * rows + 1] = above_ids[2 * rows - 1 : 2 * rows, 0:128].astype(jnp.int32)
    spots[WEST * rows + 1 : (WEST + 1) * rows] = own_ids[rows : 2 * rows - 1, 0:128].astype(jnp.int32)
    spots[NORTH * rows : (NORTH + 1) * rows] = north.astype(jnp.int32)
    spots[SOUTH * rows : (SOUTH + 1) * rows] = jnp.where(lanes == 0, beside, pltpu.roll(north, 1, 1)).astype(jnp.int32)
    copies = start_all([(spots, table)], sems)

    @pl.when(moved)
    def _():
        field[1, inside] = ends[pl.ds(0, line)]
        field[rows, inside] = ends[pl.ds(line, line)]
        for row in range(2, rows):
            field[row, inside] = middle[row - 2]

    @pl.when(jnp.logical_not(moved))
    def _():
        for row in range(rows):
            field[row + 1, inside] = own[row]

    fill_rim(field, outer, inner, side, shape)
    wait_all(copies)
    forward_one(shape, table, field, tiles, weight, x_field, m_all)(edge_blocks(shape))
    take_edges(x_field, outer_out, inner_out, side_out, shape)


def middle_compute_kernel(shape, scale, table, field, tiles, weight_one, weight_two, two_turned, readout, spread, target,
                          target_swap, x_in, m_in, x_field, m_one, m_two, gz_two, g_field, preds, goals, sums, local):
    _, _, moved = place()

    @pl.when(moved)
    def _():
        goals[...] = target_swap[...]

    @pl.when(jnp.logical_not(moved))
    def _():
        goals[...] = target[...]

    zero_rim(x_field, shape)
    zero_rim(g_field, shape)
    sums[...] = jnp.zeros_like(sums)
    blocks = inner_blocks(shape)
    forward_one(shape, table, field, tiles, weight_one, x_field, m_one)(blocks)
    through_two(
        shape, scale, table, x_field, tiles, weight_two, two_turned, readout, spread, goals, m_two, gz_two,
        g_field, preds, sums,
    )(blocks, messages(table, x_field, tiles, blocks, shape))
    local[...] = products(table, x_field, tiles, edge_blocks(shape), shape)


def second_edge_kernel(shape, scale, table, outer, inner, side, tiles, weight, weight_turned, readout, spread, goals,
                       x_field, local, m_in, gz_in, g_in, preds_in, sums_in,
                       m_two, gz_two, g_field, preds, sums, outer_out, inner_out, side_out):
    m = (local[...] + rim_terms(table, tiles, outer, inner, side, shape)).astype(BF16)
    through_two(
        shape, scale, table, x_field, tiles, weight, weight_turned, readout, spread, goals, m_two, gz_two,
        g_field, preds, sums,
    )(edge_blocks(shape), m)
    take_edges(g_field, outer_out, inner_out, side_out, shape)


def back_inner_kernel(shape, scale, table, g_field, tiles, weight, readout, goals, preds, m_one, m_two, gz_two,
                      first_out, second_out, local, slopes):
    nodes, rows, cols = shape
    blocks = inner_blocks(shape)
    gx, slope = back_terms(scale, weight, readout, goals, preds, m_one, blocks, nodes)
    gz = ((gx + products(table, g_field, tiles, blocks, shape)) * slope).astype(BF16)
    first_out[...] = over_nodes(gather(lambda row, col: m_one[row, at_block(col, nodes)], blocks), gz)
    gx, slope = back_terms(scale, weight, readout, goals, preds, m_one, edge_blocks(shape), nodes)
    local[...] = gx + products(table, g_field, tiles, edge_blocks(shape), shape)
    slopes[...] = slope
    second_out[...] = jnp.zeros_like(second_out)

    def each_row(row, carry):
        second_out[...] += over_nodes(m_two[row], gz_two[row])
        return carry

    lax.fori_loop(0, rows, each_row, 0)


def back_edge_kernel(shape, table, outer, inner, side, tiles, preds, m_one, first_in, second, sums, local, slopes,
                     keep, one, two, three, parts):
    nodes = shape[0]
    gx = local[...] + rim_terms(table, tiles, outer, inner, side, shape)
    gz = (gx * slopes[...]).astype(BF16)
    m = gather(lambda row, col: m_one[row, at_block(col, nodes)], edge_blocks(shape))
    first = first_in[...] + over_nodes(m, gz)
    count, size, width = parts.shape
    parts[:, : size // 2] = first.reshape(count, size // 2, width)
    parts[:, size // 2 :] = second[...].reshape(count, size // 2, width)
    spread_shares(parts, sums[...], lax.rem(lax.axis_index(AXES), 4), (keep, one, two, three))
    ride_preds(preds, three)


def spread_shares(parts, extra, digit, outs):
    size = parts.shape[1]
    for k, out in enumerate(outs):
        for group in range(parts.shape[0] // 4):
            out[group * size : (group + 1) * size] = parts[4 * group + jnp.bitwise_xor(digit, k)]
        out[parts.shape[0] // 4 * size : parts.shape[0] // 4 * size + 8] = extra


def take_preds(preds, riding, pred_out):
    _, _, moved = place()
    start = riding.shape[0] - preds.shape[0] * preds.shape[1] // 2

    @pl.when(moved)
    def _():
        for row in range(preds.shape[0]):
            at = start + row // 2 * preds.shape[1]
            lane = row % 2 * preds.shape[2]
            pred_out[row] = riding[at : at + preds.shape[1], lane : lane + preds.shape[2]]

    @pl.when(jnp.logical_not(moved))
    def _():
        pred_out[...] = preds[...]


def ride_preds(preds, riding):
    start = riding.shape[0] - preds.shape[0] * preds.shape[1] // 2
    for row in range(preds.shape[0]):
        at = start + row // 2 * preds.shape[1]
        lane = row % 2 * preds.shape[2]
        riding[at : at + preds.shape[1], lane : lane + preds.shape[2]] = preds[row]


def fold_kernel(base, keep, one, two, three, preds, *refs):
    digit = lax.rem(lax.axis_index(AXES) // base, 4)
    *outs, parts = refs
    if base == 4:
        take_preds(preds, three, outs.pop())
    count, size, width = parts.shape
    total = keep[...] + one[...] + two[...] + three[: keep.shape[0]]
    parts[...] = total[: count * size].reshape(count, size, width)
    spread_shares(parts, total[count * size :], digit, outs)


def last_fold_kernel(keep, one, two, three, first, second, readout):
    share = first.shape[0]
    total = keep[...] + one[...] + two[...] + three[...]
    first[...] = total[:share]
    second[...] = total[share : 2 * share]
    readout[...] = total[2 * share :].sum(axis=0, keepdims=True)


def shares_shape(groups, size, width, riding=0):
    rows = (groups * size + 8,) * 3 + (groups * size + 8 + riding,)
    return tuple(jax.ShapeDtypeStruct((number, width), F32) for number in rows)


def sum_shares(outs, preds, count, share, width, params):
    base, groups, pred_out = 1, count // 4, ()
    while True:
        got = [
            lax.ppermute(outs[k], AXES, [(i, i ^ (k * base)) for i in range(count)]) for k in (1, 2, 3)
        ]
        if groups == 1:
            break
        base *= 4
        more = (jax.ShapeDtypeStruct(preds.shape, F32),) if base == 4 else ()
        *outs, last = pl.pallas_call(
            functools.partial(fold_kernel, base),
            out_shape=shares_shape(groups // 4, 2 * share, width) + more,
            in_specs=[VMEM] * 5,
            out_specs=(VMEM,) * (4 + len(more)),
            scratch_shapes=[pltpu.VMEM((groups, 2 * share, width), F32)],
            compiler_params=params,
            name="fold",
        )(outs[0], *got, preds)
        if more:
            pred_out = last
        else:
            outs.append(last)
        groups //= 4
    small = jax.ShapeDtypeStruct((share, width), F32)
    sums = pl.pallas_call(
        last_fold_kernel,
        out_shape=(small, small, jax.ShapeDtypeStruct((1, width), F32)),
        in_specs=[VMEM] * 4,
        out_specs=(VMEM,) * 3,
        compiler_params=params,
        name="last_fold",
    )(outs[0], *got)
    return *sums, pred_out


def per_device(features, tile_ids, tiles, w_first, w_second, readout, target):
    rows, cols, nodes, width = features.shape
    wide, narrow = lax.axis_size("wide"), lax.axis_size("narrow")
    count = wide * narrow
    line, step = cols * nodes, rows * cols
    swap, first_side, inner_way, outer_way, side_way = routes(wide)
    scale = float(np.sqrt(np.float32(width) / np.float32(rows * line * count)))
    params = pltpu.CompilerParams(vmem_limit_bytes=VMEM_LIMIT)

    def send(value, way):
        return lax.ppermute(value, AXES, way)

    def edges(outer, inner, side):
        return send(outer, outer_way), send(inner, inner_way), send(side, side_way)

    def bf(*shape):
        return jax.ShapeDtypeStruct(shape, BF16)

    def sems(number):
        return pltpu.SemaphoreType.DMA((number,))

    features = features.reshape(rows, line, width)
    ends_s, side_s, numbers = pl.pallas_call(
        functools.partial(pack_kernel, nodes, cols),
        out_shape=(bf(2 * line + TAIL, width), bf(rows * nodes + TAIL, width), bf(TAIL, width)),
        in_specs=[ANY, ANY],
        out_specs=(VMEM,) * 3,
        scratch_shapes=[pltpu.VMEM((3, rows, cols), jnp.int32), pltpu.VMEM((TAIL, width), F32), sems(3 + rows)],
        compiler_params=params,
        name="pack",
    )(jnp.transpose(tile_ids, (2, 0, 1)), features)
    ends = send(ends_s, swap)
    side = send(side_s, first_side)
    middle_s = pl.pallas_call(
        middle_kernel,
        out_shape=bf(rows - 2, line, width),
        in_specs=[ANY, ANY],
        out_specs=VMEM,
        scratch_shapes=[sems(1)],
        compiler_params=params,
        name="pack_middle",
    )(features, side_s)
    middle = send(middle_s, swap)
    tiles, w_first, w_second, _ = lax.optimization_barrier((tiles, w_first, w_second, middle_s))
    tiles, w_first, w_second, w_turned = pl.pallas_call(
        prepare_kernel,
        out_shape=(bf(2 * tiles.shape[0], nodes, nodes),) + (bf(width, width),) * 3,
        in_specs=[ANY] * 3,
        out_specs=(VMEM,) * 4,
        scratch_shapes=[sems(3)],
        compiler_params=params,
        name="prepare",
    )(tiles, w_first, w_second)
    spread = jnp.broadcast_to(readout[:, None], (width, 128))
    readout = readout[None]

    outer_s, inner_s = pl.pallas_call(
        pick_kernel,
        out_shape=(bf(line + TAIL, width),) * 2,
        in_specs=[VMEM, ANY, VMEM, ANY],
        out_specs=(VMEM,) * 2,
        scratch_shapes=[sems(4)],
        compiler_params=params,
        name="pick",
    )(numbers, features, ends, side)
    outer, inner = send(outer_s, outer_way), send(inner_s, inner_way)
    target_s, _ = lax.optimization_barrier((target, inner_s))
    goal_swap = send(target_s, swap)

    shape = (nodes, rows, cols)
    patch, padded = bf(rows, line, width), bf(rows + 2, line + 2 * nodes, width)
    edge_shapes = (bf(line, width), bf(line, width), bf(rows * nodes, width))
    square = jax.ShapeDtypeStruct((width, width), F32)
    sums_shape = jax.ShapeDtypeStruct((8, width), F32)
    goal_shape = jax.ShapeDtypeStruct(target.shape, F32)
    block = nodes * width
    edge, inside = 2 * cols + rows - 2, (rows - 2) * (cols - 1)

    def cost(products, denses):
        return pl.CostEstimate(
            flops=2 * block * (products * 6 * nodes + denses * width),
            bytes_accessed=4 * block * (products + denses),
            transcendentals=block * products,
        )

    table, f_field, x_field, m_one, outer_s, inner_s, side_s = pl.pallas_call(
        functools.partial(first_edge_kernel, shape),
        out_shape=(jax.ShapeDtypeStruct((5 * rows, 128), jnp.int32), padded, padded, patch) + edge_shapes,
        in_specs=[VMEM] * 7 + [ANY] + [VMEM] * 2,
        out_specs=(SMEM,) + (VMEM,) * 6,
        scratch_shapes=[
            pltpu.VMEM((TAIL, width), F32),
            pltpu.VMEM((TAIL, width), F32),
            pltpu.VMEM((5 * rows, 128), jnp.int32),
            sems(1),
        ],
        compiler_params=params,
        cost_estimate=cost(edge, edge),
        name="first_edge",
    )(numbers, features, ends, middle, outer, inner, side, goal_swap, tiles, w_first)

    outer, inner, side = edges(outer_s, inner_s, side_s)
    edge_terms = jax.ShapeDtypeStruct((edge * nodes, width), F32)
    x_field, m_one, m_two, gz_two, g_field, preds, goals, sums, local = pl.pallas_call(
        functools.partial(middle_compute_kernel, shape, scale),
        out_shape=(padded, patch, patch, patch, padded, goal_shape, goal_shape, sums_shape, edge_terms),
        in_specs=[SMEM] + [VMEM] * 11,
        out_specs=(VMEM,) * 9,
        input_output_aliases={10: 0, 11: 1},
        compiler_params=params,
        cost_estimate=cost(2 * inside + edge, 3 * inside),
        name="inner_forward",
    )(table, f_field, tiles, w_first, w_second, w_turned, readout, spread, target, goal_swap, x_field, m_one)

    m_two, gz_two, g_field, preds, sums, outer_s, inner_s, side_s = pl.pallas_call(
        functools.partial(second_edge_kernel, shape, scale),
        out_shape=(patch, patch, padded, goal_shape, sums_shape) + edge_shapes,
        in_specs=[SMEM] + [VMEM] * 16,
        out_specs=(VMEM,) * 8,
        input_output_aliases={12 + i: i for i in range(5)},
        compiler_params=params,
        cost_estimate=cost(edge // 4, 2 * edge),
        name="second_edge",
    )(table, outer, inner, side, tiles, w_second, w_turned, readout, spread, goals, x_field, local,
      m_two, gz_two, g_field, preds, sums)

    outer, inner, side = edges(outer_s, inner_s, side_s)
    first, second, local, slopes = pl.pallas_call(
        functools.partial(back_inner_kernel, shape, scale),
        out_shape=(square, square, edge_terms, edge_terms),
        in_specs=[SMEM] + [VMEM] * 9,
        out_specs=(VMEM,) * 4,
        compiler_params=params,
        cost_estimate=cost(rows * cols, 3 * rows * cols),
        name="back_inner",
    )(table, g_field, tiles, w_first, readout, goals, preds, m_one, m_two, gz_two)

    share = width // count
    outs = pl.pallas_call(
        functools.partial(back_edge_kernel, shape),
        out_shape=shares_shape(count // 4, 2 * share, width, step * nodes // width),
        in_specs=[SMEM] + [VMEM] * 11,
        out_specs=(VMEM,) * 4,
        scratch_shapes=[pltpu.VMEM((count, 2 * share, width), F32)],
        compiler_params=params,
        cost_estimate=cost(edge // 4, edge),
        name="back_edge",
    )(table, outer, inner, side, tiles, preds, m_one, first, second, sums, local, slopes)
    first, second, extra, pred_out = sum_shares(outs, preds, count, share, width, params)
    return pred_out, first, second, extra[0]


def solution(mesh):
    in_specs = (
        P(("groups", "wide"), "narrow", None, None),
        P(("groups", "wide"), "narrow", None),
        P(),
        P(),
        P(),
        P(),
        P(("groups", "wide"), "narrow", None),
    )
    out_specs = (
        P(("groups", "wide"), "narrow", None),
        P(("groups", "wide", "narrow"), None),
        P(("groups", "wide", "narrow"), None),
        P("groups"),
    )
    return jax.shard_map(
        per_device, mesh=mesh, in_specs=in_specs, out_specs=out_specs, check_vma=False
    )
```

```python
import functools

import jax
import jax.numpy as jnp
import numpy as np
from jax import lax
from jax.experimental import pallas as pl
from jax.experimental.pallas import tpu as pltpu
from jax.sharding import PartitionSpec as P

F32 = jnp.float32
BF16 = jnp.bfloat16
AXES = ("wide", "narrow")
VMEM_LIMIT = 16 * 1024 * 1024
ANY = pl.BlockSpec(memory_space=pl.ANY)
VMEM = pl.BlockSpec(memory_space=pltpu.VMEM)
SMEM = pl.BlockSpec(memory_space=pltpu.SMEM)

SELF, EAST, WEST, NORTH, SOUTH = 0, 1, 2, 3, 4
TAIL = 16


def routes(wide):
    depth = wide // 2

    def at(z, y, c):
        return (2 * z + y) * 2 + c

    every = [(z, y, c) for z in range(depth) for y in range(2) for c in range(2)]
    swap = [(at(z, c, y), at(z, y, c)) for z, y, c in every if y != c]
    first_side = [(at(z, c, 1 - y), at(z, y, c)) for z, y, c in every]
    inner = [(at(z, y, 1 - c), at(z, y, c)) for z, y, c in every]
    outer = [(at(z - 1, y, 1), at(z, y, 0)) for z, y, c in every if c == 0 and z > 0]
    outer += [(at(z + 1, y, 0), at(z, y, 1)) for z, y, c in every if c == 1 and z + 1 < depth]
    side = [(at(z, 1 - y, c), at(z, y, c)) for z, y, c in every]
    return swap, first_side, inner, outer, side


def place():
    half = lax.axis_index("narrow")
    side = lax.rem(lax.axis_index("wide"), 2)
    return half, side, half != side


def start_all(pairs, sems, first=0):
    copies = [pltpu.make_async_copy(a, b, sems.at[first + i]) for i, (a, b) in enumerate(pairs)]
    for copy in copies:
        copy.start()
    return copies


def wait_all(copies):
    for copy in copies:
        copy.wait()


def at_block(col, nodes):
    return pl.ds(col * nodes if isinstance(col, int) else pl.multiple_of(col * nodes, nodes), nodes)


def block_product(table, field, tiles, row, col, shape):
    nodes, rows, cols = shape

    def number(kind):
        return table[kind * rows + row, col]

    def block(r, c):
        return field[r, at_block(c, nodes)]

    half = tiles.shape[0] // 2
    lhs = jnp.concatenate(
        [
            tiles[number(SELF)],
            tiles[half + number(SELF)],
            tiles[number(EAST)],
            tiles[half + number(WEST)],
            tiles[number(NORTH)],
            tiles[half + number(SOUTH)],
        ],
        axis=1,
    )
    centre = block(row + 1, col + 1)
    rhs = jnp.concatenate(
        [
            centre,
            centre,
            block(row + 2, col + 1),
            block(row, col + 1),
            block(row + 1, col + 2),
            block(row + 1, col),
        ],
        axis=0,
    )
    return jnp.dot(lhs, rhs, preferred_element_type=F32)


def edge_blocks(shape):
    _, rows, cols = shape
    half, right, _ = place()
    outer, inner = jnp.where(half == 0, 0, rows - 1), jnp.where(half == 0, rows - 1, 0)
    beside = jnp.where(right == 0, cols - 1, 0)
    blocks = [(outer, col) for col in range(cols)] + [(inner, col) for col in range(cols)]
    return blocks + [(row, beside) for row in range(1, rows - 1)]


def inner_blocks(shape):
    _, rows, cols = shape
    _, right, _ = place()
    return [(row, right + col) for row in range(1, rows - 1) for col in range(cols - 1)]


def gather(read, blocks):
    return jnp.concatenate([read(row, col) for row, col in blocks], axis=0)


def scatter(ref, blocks, value, nodes, shift):
    for k, (row, col) in enumerate(blocks):
        ref[row + shift, at_block(col + shift, nodes)] = value[k * nodes : (k + 1) * nodes]


def messages(table, field, tiles, blocks, shape):
    return gather(
        lambda row, col: block_product(table, field, tiles, row, col, shape).astype(BF16), blocks
    )


def rim_terms(table, tiles, outer, inner, side, shape):
    nodes, rows, cols = shape
    half, right, _ = place()
    turned = tiles.shape[0] // 2

    def product(tile, block):
        return jnp.dot(tiles[tile], block, preferred_element_type=F32)

    def beside(row):
        tile = jnp.where(right == 0, table[NORTH * rows + row, cols - 1], turned + table[SOUTH * rows + row, 0])
        return product(tile, side[at_block(row, nodes)])

    terms = []
    first, last = jnp.where(half == 0, 0, rows - 1), jnp.where(half == 0, rows - 1, 0)
    for line, row, upward in ((outer, first, half == 0), (inner, last, half == 1)):
        corner = beside(row)
        for col in range(cols):
            tile = jnp.where(upward, turned + table[WEST * rows + row, col], table[EAST * rows + row, col])
            term = product(tile, line[at_block(col, nodes)])
            if col in (0, cols - 1):
                term = term + jnp.where((right == 0) == (col > 0), corner, 0.0)
            terms.append(term)
    return jnp.concatenate(terms + [beside(row) for row in range(1, rows - 1)], axis=0)


def products(table, field, tiles, blocks, shape):
    return gather(lambda row, col: block_product(table, field, tiles, row, col, shape), blocks)


def forward_one(shape, table, field, tiles, weight, x_field, m_all):
    nodes = shape[0]

    def body(blocks):
        m = messages(table, field, tiles, blocks, shape)
        scatter(m_all, blocks, m, nodes, 0)
        z = jnp.dot(m, weight[...], preferred_element_type=F32)
        base = gather(lambda row, col: field[row + 1, at_block(col + 1, nodes)], blocks)
        scatter(x_field, blocks, (base.astype(F32) + jnp.tanh(z)).astype(BF16), nodes, 1)

    return body


def residual_columns(seen, goal, scale):
    gp = (seen - goal) * scale
    column = jnp.broadcast_to(gp, (gp.shape[1], gp.shape[1])).T
    return jnp.concatenate([column, column], axis=1)


def through_two(shape, scale, table, field, tiles, weight, weight_turned, readout, spread, goals, m_all, gz_all, g_field, preds, sums):
    nodes = shape[0]
    readf = readout[...].astype(F32)

    def body(blocks, m):
        scatter(m_all, blocks, m, nodes, 0)
        t = jnp.tanh(jnp.dot(m, weight[...], preferred_element_type=F32))
        base = gather(lambda row, col: field[row + 1, at_block(col + 1, nodes)], blocks)
        x = (base.astype(F32) + t).astype(BF16)
        seen = jnp.dot(x, spread[...], preferred_element_type=F32)
        parts = []
        for k, (row, col) in enumerate(blocks):
            one = seen[k * nodes : (k + 1) * nodes].T[0:1]
            preds[row, pl.ds(col, 1)] = one
            parts.append(residual_columns(one, goals[row, pl.ds(col, 1)], scale))
        gp = jnp.concatenate(parts, axis=0)
        sums[...] += (x.astype(F32) * gp).reshape(gp.shape[0] // 8, 8, gp.shape[1]).sum(axis=0)
        gz = (gp * readf * (1.0 - t * t)).astype(BF16)
        scatter(gz_all, blocks, gz, nodes, 0)
        g = jnp.dot(gz, weight_turned[...], preferred_element_type=F32).astype(BF16)
        scatter(g_field, blocks, g, nodes, 1)

    return body


def back_terms(scale, weight, readout, goals, preds, m_all, blocks, nodes):
    m = gather(lambda row, col: m_all[row, at_block(col, nodes)], blocks)
    t = jnp.tanh(jnp.dot(m, weight[...], preferred_element_type=F32))
    gp = gather(
        lambda row, col: residual_columns(preds[row, pl.ds(col, 1)], goals[row, pl.ds(col, 1)], scale), blocks
    )
    return gp * readout[...].astype(F32), 1.0 - t * t


def over_nodes(left, right):
    return lax.dot_general(left, right, (((0,), (0,)), ((), ())), preferred_element_type=F32)


def zero_rim(field, shape):
    nodes, rows, cols = shape
    field[0] = jnp.zeros(field.shape[1:], field.dtype)
    field[rows + 1] = jnp.zeros(field.shape[1:], field.dtype)
    for row in range(1, rows + 1):
        for col in (0, cols + 1):
            field[row, at_block(col, nodes)] = jnp.zeros((nodes, field.shape[2]), field.dtype)


def take_edges(field, outer, inner, side, shape):
    nodes, rows, cols = shape
    half, right, _ = place()
    inside = pl.ds(nodes, cols * nodes)
    outer[...] = field[jnp.where(half == 0, 1, rows), inside]
    inner[...] = field[jnp.where(half == 0, rows, 1), inside]
    column = at_block(jnp.where(right == 0, cols, 1), nodes)
    for row in range(rows):
        side[at_block(row, nodes)] = field[row + 1, column]


def fill_rim(field, outer, inner, side, shape):
    nodes, rows, cols = shape
    half, right, _ = place()
    inside = pl.ds(nodes, cols * nodes)
    line = pl.ds(0, cols * nodes)
    field[jnp.where(half == 0, 0, rows + 1), inside] = outer[line]
    field[jnp.where(half == 0, rows + 1, 0), inside] = inner[line]
    empty, column = jnp.where(right == 0, 0, cols + 1), jnp.where(right == 0, cols + 1, 0)
    for row in range(rows):
        field[row + 1, at_block(empty, nodes)] = jnp.zeros((nodes, field.shape[2]), field.dtype)
        field[row + 1, at_block(column, nodes)] = side[at_block(row, nodes)]


def pack_kernel(nodes, cols, ids, own, ends, side, numbers, ids_in, wide_ids, sems):
    rows, line = own.shape[0], own.shape[1]
    ids_copy = start_all([(ids, ids_in)], sems, 2 + rows)
    half, _, _ = place()
    col = pl.multiple_of(jnp.where(half == 1, 0, (cols - 1) * nodes), nodes)
    pairs = [(own.at[0], ends.at[pl.ds(0, line)]), (own.at[rows - 1], ends.at[pl.ds(line, line)])]
    for row in range(rows):
        pairs.append((own.at[row, pl.ds(col, nodes)], side.at[pl.ds(row * nodes, nodes)]))
    copies = start_all(pairs, sems)
    wait_all(ids_copy)
    wide_ids[...] = jnp.zeros_like(wide_ids)
    for kind in range(3):
        wide_ids[kind * rows : (kind + 1) * rows, 0:cols] = ids_in[kind].astype(F32)
    tail = wide_ids[...].astype(BF16)
    numbers[...] = tail
    ends[2 * line :] = tail
    side[rows * nodes :] = tail
    wait_all(copies)


def middle_kernel(own, after, middle, sems):
    wait_all(start_all([(own.at[pl.ds(1, own.shape[0] - 2)], middle)], sems))


def prepare_kernel(tiles, first, second, both, first_in, second_in, second_turned, sems):
    number = tiles.shape[0]
    wait_all(start_all([(tiles, both.at[pl.ds(0, number)]), (first, first_in), (second, second_in)], sems))

    second_turned[...] = second_in[...].T

    def one_tile(tile, carry):
        both[number + tile] = both[tile].T
        return carry

    lax.fori_loop(0, number, one_tile, 0)


def pick_kernel(numbers, own, ends, after, outer, inner, sems):
    rows, line = own.shape[0], own.shape[1]
    half, _, moved = place()
    whole = pl.ds(0, line)
    tail = pl.ds(line, TAIL)

    @pl.when(moved)
    def _():
        outer[tail] = ends[pl.ds(2 * line, TAIL)]
        inner[tail] = ends[pl.ds(2 * line, TAIL)]
        outer[whole] = ends[pl.ds(pl.multiple_of(half * line, line), line)]
        inner[whole] = ends[pl.ds(pl.multiple_of((1 - half) * line, line), line)]

    @pl.when(jnp.logical_not(moved))
    def _():
        copies = start_all([
            (own.at[jnp.where(half == 0, 0, rows - 1)], outer.at[whole]),
            (own.at[jnp.where(half == 0, rows - 1, 0)], inner.at[whole]),
        ], sems)
        outer[tail] = numbers[...]
        inner[tail] = numbers[...]
        wait_all(copies)


def first_edge_kernel(shape, numbers, own, ends, middle, outer, inner, side, later, tiles, weight,
                      table, field, x_field, m_all, outer_out, inner_out, side_out, own_ids, above_ids, spots, sems):
    nodes, rows, cols = shape
    line = cols * nodes
    half, right, moved = place()
    inside = pl.ds(nodes, line)
    tail = pl.ds(line, TAIL)

    @pl.when(moved)
    def _():
        own_ids[...] = ends[pl.ds(2 * line, TAIL)].astype(F32)

    @pl.when(jnp.logical_not(moved))
    def _():
        own_ids[...] = numbers[...].astype(F32)

    @pl.when(half == 1)
    def _():
        above_ids[...] = inner[tail].astype(F32)

    @pl.when(half == 0)
    def _():
        above_ids[...] = outer[tail].astype(F32)

    left = side[pl.ds(rows * nodes, TAIL)].astype(F32)[2 * rows : 3 * rows, 0:128]
    north = own_ids[2 * rows : 3 * rows, 0:128]
    lanes = lax.broadcasted_iota(jnp.int32, north.shape, 1)
    beside = jnp.broadcast_to(left[:, cols - 1 : cols], left.shape)
    spots[0 : 2 * rows] = own_ids[0 : 2 * rows, 0:128].astype(jnp.int32)
    spots[WEST * rows : WEST * rows + 1] = above_ids[2 * rows - 1 : 2 * rows, 0:128].astype(jnp.int32)
    spots[WEST * rows + 1 : (WEST + 1) * rows] = own_ids[rows : 2 * rows - 1, 0:128].astype(jnp.int32)
    spots[NORTH * rows : (NORTH + 1) * rows] = north.astype(jnp.int32)
    spots[SOUTH * rows : (SOUTH + 1) * rows] = jnp.where(lanes == 0, beside, pltpu.roll(north, 1, 1)).astype(jnp.int32)
    copies = start_all([(spots, table)], sems)

    @pl.when(moved)
    def _():
        field[1, inside] = ends[pl.ds(0, line)]
        field[rows, inside] = ends[pl.ds(line, line)]
        for row in range(2, rows):
            field[row, inside] = middle[row - 2]

    @pl.when(jnp.logical_not(moved))
    def _():
        for row in range(rows):
            field[row + 1, inside] = own[row]

    fill_rim(field, outer, inner, side, shape)
    wait_all(copies)
    forward_one(shape, table, field, tiles, weight, x_field, m_all)(edge_blocks(shape))
    take_edges(x_field, outer_out, inner_out, side_out, shape)


def middle_compute_kernel(shape, scale, table, field, tiles, weight_one, weight_two, two_turned, readout, spread, target,
                          target_swap, x_in, m_in, x_field, m_one, m_two, gz_two, g_field, preds, goals, sums, local):
    _, _, moved = place()

    @pl.when(moved)
    def _():
        goals[...] = target_swap[...]

    @pl.when(jnp.logical_not(moved))
    def _():
        goals[...] = target[...]

    zero_rim(x_field, shape)
    zero_rim(g_field, shape)
    sums[...] = jnp.zeros_like(sums)
    blocks = inner_blocks(shape)
    forward_one(shape, table, field, tiles, weight_one, x_field, m_one)(blocks)
    through_two(
        shape, scale, table, x_field, tiles, weight_two, two_turned, readout, spread, goals, m_two, gz_two,
        g_field, preds, sums,
    )(blocks, messages(table, x_field, tiles, blocks, shape))
    local[...] = products(table, x_field, tiles, edge_blocks(shape), shape)


def second_edge_kernel(shape, scale, table, outer, inner, side, tiles, weight, weight_turned, readout, spread, goals,
                       x_field, local, m_in, gz_in, g_in, preds_in, sums_in,
                       m_two, gz_two, g_field, preds, sums, outer_out, inner_out, side_out):
    m = (local[...] + rim_terms(table, tiles, outer, inner, side, shape)).astype(BF16)
    through_two(
        shape, scale, table, x_field, tiles, weight, weight_turned, readout, spread, goals, m_two, gz_two,
        g_field, preds, sums,
    )(edge_blocks(shape), m)
    take_edges(g_field, outer_out, inner_out, side_out, shape)


def back_inner_kernel(shape, scale, table, g_field, tiles, weight, readout, goals, preds, m_one, m_two, gz_two,
                      first_out, second_out, local, slopes):
    nodes, rows, cols = shape
    blocks = inner_blocks(shape)
    gx, slope = back_terms(scale, weight, readout, goals, preds, m_one, blocks, nodes)
    gz = ((gx + products(table, g_field, tiles, blocks, shape)) * slope).astype(BF16)
    first_out[...] = over_nodes(gather(lambda row, col: m_one[row, at_block(col, nodes)], blocks), gz)
    gx, slope = back_terms(scale, weight, readout, goals, preds, m_one, edge_blocks(shape), nodes)
    local[...] = gx + products(table, g_field, tiles, edge_blocks(shape), shape)
    slopes[...] = slope
    second_out[...] = jnp.zeros_like(second_out)

    def each_row(row, carry):
        second_out[...] += over_nodes(m_two[row], gz_two[row])
        return carry

    lax.fori_loop(0, rows, each_row, 0)


def back_edge_kernel(shape, table, outer, inner, side, tiles, preds, m_one, first_in, second, sums, local, slopes,
                     keep, one, parts):
    nodes = shape[0]
    gx = local[...] + rim_terms(table, tiles, outer, inner, side, shape)
    gz = (gx * slopes[...]).astype(BF16)
    m = gather(lambda row, col: m_one[row, at_block(col, nodes)], edge_blocks(shape))
    first = first_in[...] + over_nodes(m, gz)
    count, size, width = parts.shape
    parts[:, : size // 2] = first.reshape(count, size // 2, width)
    parts[:, size // 2 :] = second[...].reshape(count, size // 2, width)
    spread_shares(parts, sums[...], lax.axis_index("narrow"), (keep, one))
    ride_preds(preds, one)


def spread_shares(parts, extra, digit, outs):
    size, radix = parts.shape[1], len(outs)
    groups = parts.shape[0] // radix
    for k, out in enumerate(outs):
        for group in range(groups):
            out[group * size : (group + 1) * size] = parts[radix * group + jnp.bitwise_xor(digit, k)]
        out[groups * size : groups * size + 8] = extra


def take_preds(preds, riding, pred_out):
    _, _, moved = place()
    start = riding.shape[0] - preds.shape[0] * preds.shape[1] // 2

    @pl.when(moved)
    def _():
        for row in range(preds.shape[0]):
            at = start + row // 2 * preds.shape[1]
            lane = row % 2 * preds.shape[2]
            pred_out[row] = riding[at : at + preds.shape[1], lane : lane + preds.shape[2]]

    @pl.when(jnp.logical_not(moved))
    def _():
        pred_out[...] = preds[...]


def ride_preds(preds, riding):
    start = riding.shape[0] - preds.shape[0] * preds.shape[1] // 2
    for row in range(preds.shape[0]):
        at = start + row // 2 * preds.shape[1]
        lane = row % 2 * preds.shape[2]
        riding[at : at + preds.shape[1], lane : lane + preds.shape[2]] = preds[row]


def fold_kernel(base, step, radix, keep, *refs):
    *got, preds = refs[: -1 - radix - (step == 2)]
    outs, parts = list(refs[len(got) + 1 : -1]), refs[-1]
    if step == 2:
        take_preds(preds, got[0], outs.pop())
    count, size, _ = parts.shape
    total = keep[...]
    for one in got:
        total = total + one[: keep.shape[0]]
    parts[...] = total[: count * size].reshape(parts.shape)
    spread_shares(parts, total[count * size :], lax.rem(lax.axis_index(AXES) // base, radix), outs)
    if step == 1:
        riding = got[0].shape[0] - keep.shape[0]
        outs[1][outs[1].shape[0] - riding :] = got[0][keep.shape[0] :]


def last_fold_kernel(keep, *refs):
    *got, first, second, readout = refs
    share = first.shape[0]
    total = keep[...]
    for one in got:
        total = total + one[...]
    first[...] = total[:share]
    second[...] = total[share : 2 * share]
    readout[...] = total[2 * share :].sum(axis=0, keepdims=True)


def shares_shape(groups, size, width, radix, riding=0):
    rows = [groups * size + 8] * radix
    rows[1] += riding
    return tuple(jax.ShapeDtypeStruct((number, width), F32) for number in rows)


def sum_shares(outs, preds, count, share, width, riding, params):
    radices, left = [2, 2], count // 4
    while left > 1:
        radices.append(min(4, left))
        left //= radices[-1]
    base, groups, pred_out = 1, count // 2, None
    for step, radix in enumerate(radices):
        got = [
            lax.ppermute(outs[k], AXES, [(i, i ^ (k * base)) for i in range(count)]) for k in range(1, radix)
        ]
        if step == len(radices) - 1:
            break
        base *= radix
        radix = radices[step + 1]
        more = (jax.ShapeDtypeStruct(preds.shape, F32),) if step == 1 else ()
        shapes = shares_shape(groups // radix, 2 * share, width, radix, riding if step == 0 else 0) + more
        folded = pl.pallas_call(
            functools.partial(fold_kernel, base, step + 1, radix),
            out_shape=shapes,
            in_specs=[VMEM] * (2 + len(got)),
            out_specs=(VMEM,) * len(shapes),
            scratch_shapes=[pltpu.VMEM((groups, 2 * share, width), F32)],
            compiler_params=params,
            name="fold",
        )(outs[0], *got, preds)
        outs = folded[:radix]
        if more:
            pred_out = folded[-1]
        groups //= radix
    small = jax.ShapeDtypeStruct((share, width), F32)
    sums = pl.pallas_call(
        last_fold_kernel,
        out_shape=(small, small, jax.ShapeDtypeStruct((1, width), F32)),
        in_specs=[VMEM] * (1 + len(got)),
        out_specs=(VMEM,) * 3,
        compiler_params=params,
        name="last_fold",
    )(outs[0], *got)
    return *sums, pred_out


def per_device(features, tile_ids, tiles, w_first, w_second, readout, target):
    rows, cols, nodes, width = features.shape
    wide, narrow = lax.axis_size("wide"), lax.axis_size("narrow")
    count = wide * narrow
    line, step = cols * nodes, rows * cols
    swap, first_side, inner_way, outer_way, side_way = routes(wide)
    scale = float(np.sqrt(np.float32(width) / np.float32(rows * line * count)))
    params = pltpu.CompilerParams(vmem_limit_bytes=VMEM_LIMIT)

    def send(value, way):
        return lax.ppermute(value, AXES, way)

    def edges(outer, inner, side):
        return send(outer, outer_way), send(inner, inner_way), send(side, side_way)

    def bf(*shape):
        return jax.ShapeDtypeStruct(shape, BF16)

    def sems(number):
        return pltpu.SemaphoreType.DMA((number,))

    features = features.reshape(rows, line, width)
    ends_s, side_s, numbers = pl.pallas_call(
        functools.partial(pack_kernel, nodes, cols),
        out_shape=(bf(2 * line + TAIL, width), bf(rows * nodes + TAIL, width), bf(TAIL, width)),
        in_specs=[ANY, ANY],
        out_specs=(VMEM,) * 3,
        scratch_shapes=[pltpu.VMEM((3, rows, cols), jnp.int32), pltpu.VMEM((TAIL, width), F32), sems(3 + rows)],
        compiler_params=params,
        name="pack",
    )(jnp.transpose(tile_ids, (2, 0, 1)), features)
    ends = send(ends_s, swap)
    side = send(side_s, first_side)
    middle_s = pl.pallas_call(
        middle_kernel,
        out_shape=bf(rows - 2, line, width),
        in_specs=[ANY, ANY],
        out_specs=VMEM,
        scratch_shapes=[sems(1)],
        compiler_params=params,
        name="pack_middle",
    )(features, side_s)
    middle = send(middle_s, swap)
    tiles, w_first, w_second, _ = lax.optimization_barrier((tiles, w_first, w_second, middle_s))
    tiles, w_first, w_second, w_turned = pl.pallas_call(
        prepare_kernel,
        out_shape=(bf(2 * tiles.shape[0], nodes, nodes),) + (bf(width, width),) * 3,
        in_specs=[ANY] * 3,
        out_specs=(VMEM,) * 4,
        scratch_shapes=[sems(3)],
        compiler_params=params,
        name="prepare",
    )(tiles, w_first, w_second)
    spread = jnp.broadcast_to(readout[:, None], (width, 128))
    readout = readout[None]

    outer_s, inner_s = pl.pallas_call(
        pick_kernel,
        out_shape=(bf(line + TAIL, width),) * 2,
        in_specs=[VMEM, ANY, VMEM, ANY],
        out_specs=(VMEM,) * 2,
        scratch_shapes=[sems(4)],
        compiler_params=params,
        name="pick",
    )(numbers, features, ends, side)
    outer, inner = send(outer_s, outer_way), send(inner_s, inner_way)
    target_s, _ = lax.optimization_barrier((target, inner_s))
    goal_swap = send(target_s, swap)

    shape = (nodes, rows, cols)
    patch, padded = bf(rows, line, width), bf(rows + 2, line + 2 * nodes, width)
    edge_shapes = (bf(line, width), bf(line, width), bf(rows * nodes, width))
    square = jax.ShapeDtypeStruct((width, width), F32)
    sums_shape = jax.ShapeDtypeStruct((8, width), F32)
    goal_shape = jax.ShapeDtypeStruct(target.shape, F32)
    block = nodes * width
    edge, inside = 2 * cols + rows - 2, (rows - 2) * (cols - 1)

    def cost(products, denses):
        return pl.CostEstimate(
            flops=2 * block * (products * 6 * nodes + denses * width),
            bytes_accessed=4 * block * (products + denses),
            transcendentals=block * products,
        )

    table, f_field, x_field, m_one, outer_s, inner_s, side_s = pl.pallas_call(
        functools.partial(first_edge_kernel, shape),
        out_shape=(jax.ShapeDtypeStruct((5 * rows, 128), jnp.int32), padded, padded, patch) + edge_shapes,
        in_specs=[VMEM] * 7 + [ANY] + [VMEM] * 2,
        out_specs=(SMEM,) + (VMEM,) * 6,
        scratch_shapes=[
            pltpu.VMEM((TAIL, width), F32),
            pltpu.VMEM((TAIL, width), F32),
            pltpu.VMEM((5 * rows, 128), jnp.int32),
            sems(1),
        ],
        compiler_params=params,
        cost_estimate=cost(edge, edge),
        name="first_edge",
    )(numbers, features, ends, middle, outer, inner, side, goal_swap, tiles, w_first)

    outer, inner, side = edges(outer_s, inner_s, side_s)
    edge_terms = jax.ShapeDtypeStruct((edge * nodes, width), F32)
    x_field, m_one, m_two, gz_two, g_field, preds, goals, sums, local = pl.pallas_call(
        functools.partial(middle_compute_kernel, shape, scale),
        out_shape=(padded, patch, patch, patch, padded, goal_shape, goal_shape, sums_shape, edge_terms),
        in_specs=[SMEM] + [VMEM] * 11,
        out_specs=(VMEM,) * 9,
        input_output_aliases={10: 0, 11: 1},
        compiler_params=params,
        cost_estimate=cost(2 * inside + edge, 3 * inside),
        name="inner_forward",
    )(table, f_field, tiles, w_first, w_second, w_turned, readout, spread, target, goal_swap, x_field, m_one)

    m_two, gz_two, g_field, preds, sums, outer_s, inner_s, side_s = pl.pallas_call(
        functools.partial(second_edge_kernel, shape, scale),
        out_shape=(patch, patch, padded, goal_shape, sums_shape) + edge_shapes,
        in_specs=[SMEM] + [VMEM] * 16,
        out_specs=(VMEM,) * 8,
        input_output_aliases={12 + i: i for i in range(5)},
        compiler_params=params,
        cost_estimate=cost(edge // 4, 2 * edge),
        name="second_edge",
    )(table, outer, inner, side, tiles, w_second, w_turned, readout, spread, goals, x_field, local,
      m_two, gz_two, g_field, preds, sums)

    outer, inner, side = edges(outer_s, inner_s, side_s)
    first, second, local, slopes = pl.pallas_call(
        functools.partial(back_inner_kernel, shape, scale),
        out_shape=(square, square, edge_terms, edge_terms),
        in_specs=[SMEM] + [VMEM] * 9,
        out_specs=(VMEM,) * 4,
        compiler_params=params,
        cost_estimate=cost(rows * cols, 3 * rows * cols),
        name="back_inner",
    )(table, g_field, tiles, w_first, readout, goals, preds, m_one, m_two, gz_two)

    share, riding = width // count, step * nodes // width
    outs = pl.pallas_call(
        functools.partial(back_edge_kernel, shape),
        out_shape=shares_shape(count // 2, 2 * share, width, 2, riding),
        in_specs=[SMEM] + [VMEM] * 11,
        out_specs=(VMEM,) * 2,
        scratch_shapes=[pltpu.VMEM((count, 2 * share, width), F32)],
        compiler_params=params,
        cost_estimate=cost(edge // 4, edge),
        name="back_edge",
    )(table, outer, inner, side, tiles, preds, m_one, first, second, sums, local, slopes)
    first, second, extra, pred_out = sum_shares(outs, preds, count, share, width, riding, params)
    return pred_out, first, second, extra[0]


def solution(mesh):
    in_specs = (
        P(("groups", "wide"), "narrow", None, None),
        P(("groups", "wide"), "narrow", None),
        P(),
        P(),
        P(),
        P(),
        P(("groups", "wide"), "narrow", None),
    )
    out_specs = (
        P(("groups", "wide"), "narrow", None),
        P(("groups", "wide", "narrow"), None),
        P(("groups", "wide", "narrow"), None),
        P("groups"),
    )
    return jax.shard_map(
        per_device, mesh=mesh, in_specs=in_specs, out_specs=out_specs, check_vma=False
    )
```

```python
import functools

import jax
import jax.numpy as jnp
import numpy as np
from jax import lax
from jax.experimental import pallas as pl
from jax.experimental.pallas import tpu as pltpu
from jax.sharding import PartitionSpec as P

F32 = jnp.float32
BF16 = jnp.bfloat16
AXES = ("wide", "narrow")
VMEM_LIMIT = 16 * 1024 * 1024
ANY = pl.BlockSpec(memory_space=pl.ANY)
VMEM = pl.BlockSpec(memory_space=pltpu.VMEM)
SMEM = pl.BlockSpec(memory_space=pltpu.SMEM)

SELF, EAST, WEST, NORTH, SOUTH = 0, 1, 2, 3, 4
TAIL = 16


def routes(wide):
    depth = wide // 2

    def at(z, y, c):
        return (2 * z + y) * 2 + c

    every = [(z, y, c) for z in range(depth) for y in range(2) for c in range(2)]
    swap = [(at(z, c, y), at(z, y, c)) for z, y, c in every if y != c]
    first_side = [(at(z, c, 1 - y), at(z, y, c)) for z, y, c in every]
    inner = [(at(z, y, 1 - c), at(z, y, c)) for z, y, c in every]
    outer = [(at(z - 1, y, 1), at(z, y, 0)) for z, y, c in every if c == 0 and z > 0]
    outer += [(at(z + 1, y, 0), at(z, y, 1)) for z, y, c in every if c == 1 and z + 1 < depth]
    side = [(at(z, 1 - y, c), at(z, y, c)) for z, y, c in every]
    above = [(at(z, 0, y), at(z, y, 1)) for z, y, c in every if c == 1]
    above += [(at(z - 1, 1, y), at(z, y, 0)) for z, y, c in every if c == 0 and z > 0]
    return swap, first_side, inner, outer, side, above


def place():
    half = lax.axis_index("narrow")
    side = lax.rem(lax.axis_index("wide"), 2)
    return half, side, half != side


def start_all(pairs, sems, first=0):
    copies = [pltpu.make_async_copy(a, b, sems.at[first + i]) for i, (a, b) in enumerate(pairs)]
    for copy in copies:
        copy.start()
    return copies


def wait_all(copies):
    for copy in copies:
        copy.wait()


def at_block(col, nodes):
    return pl.ds(col * nodes if isinstance(col, int) else pl.multiple_of(col * nodes, nodes), nodes)


def block_product(table, field, tiles, row, col, shape):
    nodes, rows, cols = shape

    def number(kind):
        return table[kind * rows + row, col]

    def block(r, c):
        return field[r, at_block(c, nodes)]

    half = tiles.shape[0] // 2
    lhs = jnp.concatenate(
        [
            tiles[number(SELF)],
            tiles[half + number(SELF)],
            tiles[number(EAST)],
            tiles[half + number(WEST)],
            tiles[number(NORTH)],
            tiles[half + number(SOUTH)],
        ],
        axis=1,
    )
    centre = block(row + 1, col + 1)
    rhs = jnp.concatenate(
        [
            centre,
            centre,
            block(row + 2, col + 1),
            block(row, col + 1),
            block(row + 1, col + 2),
            block(row + 1, col),
        ],
        axis=0,
    )
    return jnp.dot(lhs, rhs, preferred_element_type=F32)


def edge_blocks(shape):
    _, rows, cols = shape
    half, right, _ = place()
    outer, inner = jnp.where(half == 0, 0, rows - 1), jnp.where(half == 0, rows - 1, 0)
    beside = jnp.where(right == 0, cols - 1, 0)
    blocks = [(outer, col) for col in range(cols)] + [(inner, col) for col in range(cols)]
    return blocks + [(row, beside) for row in range(1, rows - 1)]


def inner_blocks(shape):
    _, rows, cols = shape
    _, right, _ = place()
    return [(row, right + col) for row in range(1, rows - 1) for col in range(cols - 1)]


def gather(read, blocks):
    return jnp.concatenate([read(row, col) for row, col in blocks], axis=0)


def scatter(ref, blocks, value, nodes, shift):
    for k, (row, col) in enumerate(blocks):
        ref[row + shift, at_block(col + shift, nodes)] = value[k * nodes : (k + 1) * nodes]


def messages(table, field, tiles, blocks, shape):
    return gather(
        lambda row, col: block_product(table, field, tiles, row, col, shape).astype(BF16), blocks
    )


def rim_terms(table, tiles, outer, inner, side, shape):
    nodes, rows, cols = shape
    half, right, _ = place()
    turned = tiles.shape[0] // 2

    def product(tile, block):
        return jnp.dot(tiles[tile], block, preferred_element_type=F32)

    def beside(row):
        tile = jnp.where(right == 0, table[NORTH * rows + row, cols - 1], turned + table[SOUTH * rows + row, 0])
        return product(tile, side[at_block(row, nodes)])

    terms = []
    first, last = jnp.where(half == 0, 0, rows - 1), jnp.where(half == 0, rows - 1, 0)
    for line, row, upward in ((outer, first, half == 0), (inner, last, half == 1)):
        corner = beside(row)
        for col in range(cols):
            tile = jnp.where(upward, turned + table[WEST * rows + row, col], table[EAST * rows + row, col])
            term = product(tile, line[at_block(col, nodes)])
            if col in (0, cols - 1):
                term = term + jnp.where((right == 0) == (col > 0), corner, 0.0)
            terms.append(term)
    return jnp.concatenate(terms + [beside(row) for row in range(1, rows - 1)], axis=0)


def products(table, field, tiles, blocks, shape):
    return gather(lambda row, col: block_product(table, field, tiles, row, col, shape), blocks)


def forward_one(shape, table, field, tiles, weight, x_field, m_all):
    nodes = shape[0]

    def body(blocks):
        m = messages(table, field, tiles, blocks, shape)
        scatter(m_all, blocks, m, nodes, 0)
        z = jnp.dot(m, weight[...], preferred_element_type=F32)
        base = gather(lambda row, col: field[row + 1, at_block(col + 1, nodes)], blocks)
        scatter(x_field, blocks, (base.astype(F32) + jnp.tanh(z)).astype(BF16), nodes, 1)

    return body


def residual_columns(seen, goal, scale):
    gp = (seen - goal) * scale
    column = jnp.broadcast_to(gp, (gp.shape[1], gp.shape[1])).T
    return jnp.concatenate([column, column], axis=1)


def through_two(shape, scale, table, field, tiles, weight, weight_turned, readout, spread, goals, m_all, gz_all, g_field, preds, sums):
    nodes = shape[0]
    readf = readout[...].astype(F32)

    def body(blocks, m):
        scatter(m_all, blocks, m, nodes, 0)
        t = jnp.tanh(jnp.dot(m, weight[...], preferred_element_type=F32))
        base = gather(lambda row, col: field[row + 1, at_block(col + 1, nodes)], blocks)
        x = (base.astype(F32) + t).astype(BF16)
        seen = jnp.dot(x, spread[...], preferred_element_type=F32)
        parts = []
        for k, (row, col) in enumerate(blocks):
            one = seen[k * nodes : (k + 1) * nodes].T[0:1]
            preds[row, pl.ds(col, 1)] = one
            parts.append(residual_columns(one, goals[row, pl.ds(col, 1)], scale))
        gp = jnp.concatenate(parts, axis=0)
        sums[...] += (x.astype(F32) * gp).reshape(gp.shape[0] // 8, 8, gp.shape[1]).sum(axis=0)
        gz = (gp * readf * (1.0 - t * t)).astype(BF16)
        scatter(gz_all, blocks, gz, nodes, 0)
        g = jnp.dot(gz, weight_turned[...], preferred_element_type=F32).astype(BF16)
        scatter(g_field, blocks, g, nodes, 1)

    return body


def back_terms(scale, weight, readout, goals, preds, m_all, blocks, nodes):
    m = gather(lambda row, col: m_all[row, at_block(col, nodes)], blocks)
    t = jnp.tanh(jnp.dot(m, weight[...], preferred_element_type=F32))
    gp = gather(
        lambda row, col: residual_columns(preds[row, pl.ds(col, 1)], goals[row, pl.ds(col, 1)], scale), blocks
    )
    return gp * readout[...].astype(F32), 1.0 - t * t


def over_nodes(left, right):
    return lax.dot_general(left, right, (((0,), (0,)), ((), ())), preferred_element_type=F32)


def zero_rim(field, shape):
    nodes, rows, cols = shape
    field[0] = jnp.zeros(field.shape[1:], field.dtype)
    field[rows + 1] = jnp.zeros(field.shape[1:], field.dtype)
    for row in range(1, rows + 1):
        for col in (0, cols + 1):
            field[row, at_block(col, nodes)] = jnp.zeros((nodes, field.shape[2]), field.dtype)


def take_edges(field, outer, inner, side, shape):
    nodes, rows, cols = shape
    half, right, _ = place()
    inside = pl.ds(nodes, cols * nodes)
    outer[...] = field[jnp.where(half == 0, 1, rows), inside]
    inner[...] = field[jnp.where(half == 0, rows, 1), inside]
    column = at_block(jnp.where(right == 0, cols, 1), nodes)
    for row in range(rows):
        side[at_block(row, nodes)] = field[row + 1, column]


def fill_rim(field, outer, inner, side, shape):
    nodes, rows, cols = shape
    half, right, _ = place()
    inside = pl.ds(nodes, cols * nodes)
    line = pl.ds(0, cols * nodes)
    field[jnp.where(half == 0, 0, rows + 1), inside] = outer[line]
    field[jnp.where(half == 0, rows + 1, 0), inside] = inner[line]
    empty, column = jnp.where(right == 0, 0, cols + 1), jnp.where(right == 0, cols + 1, 0)
    for row in range(rows):
        field[row + 1, at_block(empty, nodes)] = jnp.zeros((nodes, field.shape[2]), field.dtype)
        field[row + 1, at_block(column, nodes)] = side[at_block(row, nodes)]


def pack_kernel(nodes, cols, ids, own, after, side, numbers, wide_ids, sems):
    rows = own.shape[0]
    half, _, _ = place()
    col = pl.multiple_of(jnp.where(half == 1, 0, (cols - 1) * nodes), nodes)
    copies = start_all(
        [(own.at[row, pl.ds(col, nodes)], side.at[pl.ds(row * nodes, nodes)]) for row in range(rows)], sems
    )
    wide_ids[...] = jnp.zeros_like(wide_ids)
    for kind in range(3):
        wide_ids[kind * rows : (kind + 1) * rows, 0:cols] = ids[kind]
    tail = wide_ids[...].astype(BF16)
    numbers[...] = tail
    side[rows * nodes :] = tail
    wait_all(copies)


def middle_kernel(own, numbers, middle, sems):
    rows, line = own.shape[0], own.shape[1]
    copies = start_all([(own.at[row + 1], middle.at[pl.ds(row * line, line)]) for row in range(rows - 2)], sems)
    middle[(rows - 2) * line :] = numbers[...]
    wait_all(copies)


def prepare_kernel(tiles, first, second, both, first_in, second_in, second_turned, sems):
    number = tiles.shape[0]
    wait_all(start_all([(tiles, both.at[pl.ds(0, number)]), (first, first_in), (second, second_in)], sems))

    second_turned[...] = second_in[...].T

    def one_tile(tile, carry):
        both[number + tile] = both[tile].T
        return carry

    lax.fori_loop(0, number, one_tile, 0)


def pick_kernel(own, ends, after, outer, inner, sems):
    rows, line = own.shape[0], own.shape[1]
    half, _, moved = place()

    @pl.when(moved)
    def _():
        outer[...] = ends[pl.ds(pl.multiple_of(half * line, line), line)]
        inner[...] = ends[pl.ds(pl.multiple_of((1 - half) * line, line), line)]

    @pl.when(jnp.logical_not(moved))
    def _():
        wait_all(start_all([
            (own.at[jnp.where(half == 0, 0, rows - 1)], outer),
            (own.at[jnp.where(half == 0, rows - 1, 0)], inner),
        ], sems))


def first_edge_kernel(shape, numbers, above, own, ends, middle, outer, inner, side, later, tiles, weight,
                      table, field, x_field, m_all, outer_out, inner_out, side_out, own_ids, above_ids, spots, sems):
    nodes, rows, cols = shape
    line = cols * nodes
    _, _, moved = place()
    inside = pl.ds(nodes, line)
    @pl.when(moved)
    def _():
        own_ids[...] = middle[pl.ds((rows - 2) * line, TAIL)].astype(F32)

    @pl.when(jnp.logical_not(moved))
    def _():
        own_ids[...] = numbers[...].astype(F32)

    above_ids[...] = above[...].astype(F32)
    left = side[pl.ds(rows * nodes, TAIL)].astype(F32)[2 * rows : 3 * rows, 0:128]
    north = own_ids[2 * rows : 3 * rows, 0:128]
    lanes = lax.broadcasted_iota(jnp.int32, north.shape, 1)
    beside = jnp.broadcast_to(left[:, cols - 1 : cols], left.shape)
    spots[0 : 2 * rows] = own_ids[0 : 2 * rows, 0:128].astype(jnp.int32)
    spots[WEST * rows : WEST * rows + 1] = above_ids[2 * rows - 1 : 2 * rows, 0:128].astype(jnp.int32)
    spots[WEST * rows + 1 : (WEST + 1) * rows] = own_ids[rows : 2 * rows - 1, 0:128].astype(jnp.int32)
    spots[NORTH * rows : (NORTH + 1) * rows] = north.astype(jnp.int32)
    spots[SOUTH * rows : (SOUTH + 1) * rows] = jnp.where(lanes == 0, beside, pltpu.roll(north, 1, 1)).astype(jnp.int32)
    copies = start_all([(spots, table)], sems)

    @pl.when(moved)
    def _():
        field[1, inside] = ends[pl.ds(0, line)]
        field[rows, inside] = ends[pl.ds(line, line)]
        for row in range(2, rows):
            field[row, inside] = middle[pl.ds((row - 2) * line, line)]

    @pl.when(jnp.logical_not(moved))
    def _():
        for row in range(rows):
            field[row + 1, inside] = own[row]

    fill_rim(field, outer, inner, side, shape)
    wait_all(copies)
    forward_one(shape, table, field, tiles, weight, x_field, m_all)(edge_blocks(shape))
    take_edges(x_field, outer_out, inner_out, side_out, shape)


def middle_compute_kernel(shape, scale, table, field, tiles, weight_one, weight_two, two_turned, readout, spread, target,
                          target_swap, x_in, m_in, x_field, m_one, m_two, gz_two, g_field, preds, goals, sums, local):
    _, _, moved = place()

    @pl.when(moved)
    def _():
        goals[...] = target_swap[...]

    @pl.when(jnp.logical_not(moved))
    def _():
        goals[...] = target[...]

    zero_rim(x_field, shape)
    zero_rim(g_field, shape)
    sums[...] = jnp.zeros_like(sums)
    blocks = inner_blocks(shape)
    forward_one(shape, table, field, tiles, weight_one, x_field, m_one)(blocks)
    through_two(
        shape, scale, table, x_field, tiles, weight_two, two_turned, readout, spread, goals, m_two, gz_two,
        g_field, preds, sums,
    )(blocks, messages(table, x_field, tiles, blocks, shape))
    local[...] = products(table, x_field, tiles, edge_blocks(shape), shape)


def second_edge_kernel(shape, scale, table, outer, inner, side, tiles, weight, weight_turned, readout, spread, goals,
                       x_field, local, m_in, gz_in, g_in, preds_in, sums_in,
                       m_two, gz_two, g_field, preds, sums, outer_out, inner_out, side_out):
    m = (local[...] + rim_terms(table, tiles, outer, inner, side, shape)).astype(BF16)
    through_two(
        shape, scale, table, x_field, tiles, weight, weight_turned, readout, spread, goals, m_two, gz_two,
        g_field, preds, sums,
    )(edge_blocks(shape), m)
    take_edges(g_field, outer_out, inner_out, side_out, shape)


def back_inner_kernel(shape, scale, table, g_field, tiles, weight, readout, goals, preds, m_one, m_two, gz_two,
                      first_out, second_out, local, slopes, m_turned):
    nodes, rows, cols = shape
    blocks = inner_blocks(shape)
    gx, slope = back_terms(scale, weight, readout, goals, preds, m_one, blocks, nodes)
    gz = ((gx + products(table, g_field, tiles, blocks, shape)) * slope).astype(BF16)
    first_out[...] = over_nodes(gather(lambda row, col: m_one[row, at_block(col, nodes)], blocks), gz)
    gx, slope = back_terms(scale, weight, readout, goals, preds, m_one, edge_blocks(shape), nodes)
    local[...] = gx + products(table, g_field, tiles, edge_blocks(shape), shape)
    slopes[...] = slope
    m_turned[...] = gather(lambda row, col: m_one[row, at_block(col, nodes)], edge_blocks(shape)).T
    second_out[...] = jnp.zeros_like(second_out)

    def each_row(row, carry):
        second_out[...] += over_nodes(m_two[row], gz_two[row])
        return carry

    lax.fori_loop(0, rows, each_row, 0)


def back_edge_kernel(shape, table, outer, inner, side, tiles, preds, m_turned, first_in, second, sums, local, slopes,
                     keep, one, parts):
    width = first_in.shape[1]
    gx = local[...] + rim_terms(table, tiles, outer, inner, side, shape)
    gz = (gx * slopes[...]).astype(BF16)
    first = first_in[...] + jnp.dot(m_turned[...], gz, preferred_element_type=F32)
    count, size, _ = parts.shape
    parts[:, : size // 2] = first.reshape(count, size // 2, width)
    parts[:, size // 2 :] = second[...].reshape(count, size // 2, width)
    spread_shares(parts, sums[...], lax.axis_index("narrow"), (keep, one))
    ride_preds(preds, one)


def spread_shares(parts, extra, digit, outs):
    size, radix = parts.shape[1], len(outs)
    groups = parts.shape[0] // radix
    for k, out in enumerate(outs):
        for group in range(groups):
            out[group * size : (group + 1) * size] = parts[radix * group + jnp.bitwise_xor(digit, k)]
        out[groups * size : groups * size + 8] = extra


def take_preds(preds, riding, pred_out):
    _, _, moved = place()
    start = riding.shape[0] - preds.shape[0] * preds.shape[1] // 2

    @pl.when(moved)
    def _():
        for row in range(preds.shape[0]):
            at = start + row // 2 * preds.shape[1]
            lane = row % 2 * preds.shape[2]
            pred_out[row] = riding[at : at + preds.shape[1], lane : lane + preds.shape[2]]

    @pl.when(jnp.logical_not(moved))
    def _():
        pred_out[...] = preds[...]


def ride_preds(preds, riding):
    start = riding.shape[0] - preds.shape[0] * preds.shape[1] // 2
    for row in range(preds.shape[0]):
        at = start + row // 2 * preds.shape[1]
        lane = row % 2 * preds.shape[2]
        riding[at : at + preds.shape[1], lane : lane + preds.shape[2]] = preds[row]


def fold_kernel(base, step, radix, keep, *refs):
    *got, preds = refs[: -1 - radix - (step == 2)]
    outs, parts = list(refs[len(got) + 1 : -1]), refs[-1]
    if step == 2:
        take_preds(preds, got[0], outs.pop())
    count, size, _ = parts.shape
    total = keep[...]
    for one in got:
        total = total + one[: keep.shape[0]]
    parts[...] = total[: count * size].reshape(parts.shape)
    spread_shares(parts, total[count * size :], lax.rem(lax.axis_index(AXES) // base, radix), outs)
    if step == 1:
        riding = got[0].shape[0] - keep.shape[0]
        outs[1][outs[1].shape[0] - riding :] = got[0][keep.shape[0] :]


def last_fold_kernel(keep, *refs):
    *got, first, second, readout = refs
    share = first.shape[0]
    total = keep[...]
    for one in got:
        total = total + one[...]
    first[...] = total[:share]
    second[...] = total[share : 2 * share]
    readout[...] = total[2 * share :].sum(axis=0, keepdims=True)


def shares_shape(groups, size, width, radix, riding=0):
    rows = [groups * size + 8] * radix
    rows[1] += riding
    return tuple(jax.ShapeDtypeStruct((number, width), F32) for number in rows)


def sum_shares(outs, preds, count, share, width, riding, params):
    radices, left = [2, 2], count // 4
    while left > 1:
        radices.append(min(4, left))
        left //= radices[-1]
    base, groups, pred_out = 1, count // 2, None
    for step, radix in enumerate(radices):
        got = [
            lax.ppermute(outs[k], AXES, [(i, i ^ (k * base)) for i in range(count)]) for k in range(1, radix)
        ]
        if step == len(radices) - 1:
            break
        base *= radix
        radix = radices[step + 1]
        more = (jax.ShapeDtypeStruct(preds.shape, F32),) if step == 1 else ()
        shapes = shares_shape(groups // radix, 2 * share, width, radix, riding if step == 0 else 0) + more
        folded = pl.pallas_call(
            functools.partial(fold_kernel, base, step + 1, radix),
            out_shape=shapes,
            in_specs=[VMEM] * (2 + len(got)),
            out_specs=(VMEM,) * len(shapes),
            scratch_shapes=[pltpu.VMEM((groups, 2 * share, width), F32)],
            compiler_params=params,
            name="fold",
        )(outs[0], *got, preds)
        outs = folded[:radix]
        if more:
            pred_out = folded[-1]
        groups //= radix
    small = jax.ShapeDtypeStruct((share, width), F32)
    sums = pl.pallas_call(
        last_fold_kernel,
        out_shape=(small, small, jax.ShapeDtypeStruct((1, width), F32)),
        in_specs=[VMEM] * (1 + len(got)),
        out_specs=(VMEM,) * 3,
        compiler_params=params,
        name="last_fold",
    )(outs[0], *got)
    return *sums, pred_out


def per_device(features, tile_ids, tiles, w_first, w_second, readout, target):
    rows, cols, nodes, width = features.shape
    wide, narrow = lax.axis_size("wide"), lax.axis_size("narrow")
    count = wide * narrow
    line, step = cols * nodes, rows * cols
    swap, first_side, inner_way, outer_way, side_way, above_way = routes(wide)
    scale = float(np.sqrt(np.float32(width) / np.float32(rows * line * count)))
    params = pltpu.CompilerParams(vmem_limit_bytes=VMEM_LIMIT)

    def send(value, way):
        return lax.ppermute(value, AXES, way)

    def edges(outer, inner, side):
        return send(outer, outer_way), send(inner, inner_way), send(side, side_way)

    def bf(*shape):
        return jax.ShapeDtypeStruct(shape, BF16)

    def sems(number):
        return pltpu.SemaphoreType.DMA((number,))

    features = features.reshape(rows, line, width)
    ends_s = features[0 :: rows - 1].reshape(2 * line, width)
    ends = send(ends_s, swap)
    side_s, numbers = pl.pallas_call(
        functools.partial(pack_kernel, nodes, cols),
        out_shape=(bf(rows * nodes + TAIL, width), bf(TAIL, width)),
        in_specs=[VMEM, ANY, ANY],
        out_specs=(VMEM,) * 2,
        scratch_shapes=[pltpu.VMEM((TAIL, width), F32), sems(rows)],
        compiler_params=params,
        name="pack",
    )(jnp.transpose(tile_ids, (2, 0, 1)).astype(F32), features, ends_s)
    side = send(side_s, first_side)
    middle_s = pl.pallas_call(
        middle_kernel,
        out_shape=bf((rows - 2) * line + TAIL, width),
        in_specs=[ANY, VMEM],
        out_specs=VMEM,
        scratch_shapes=[sems(rows - 2)],
        compiler_params=params,
        name="pack_middle",
    )(features, numbers)
    middle = send(middle_s, swap)
    tiles, w_first, w_second, _ = lax.optimization_barrier((tiles, w_first, w_second, middle_s))
    tiles, w_first, w_second, w_turned = pl.pallas_call(
        prepare_kernel,
        out_shape=(bf(2 * tiles.shape[0], nodes, nodes),) + (bf(width, width),) * 3,
        in_specs=[ANY] * 3,
        out_specs=(VMEM,) * 4,
        scratch_shapes=[sems(3)],
        compiler_params=params,
        name="prepare",
    )(tiles, w_first, w_second)
    spread = jnp.broadcast_to(readout[:, None], (width, 128))
    readout = readout[None]

    outer_s, inner_s = pl.pallas_call(
        pick_kernel,
        out_shape=(bf(line, width),) * 2,
        in_specs=[ANY, VMEM, ANY],
        out_specs=(VMEM,) * 2,
        scratch_shapes=[sems(4)],
        compiler_params=params,
        name="pick",
    )(features, ends, side)
    outer, inner = send(outer_s, outer_way), send(inner_s, inner_way)
    target_s, numbers_s, _ = lax.optimization_barrier((target, numbers, inner_s))
    goal_swap = send(target_s, swap)
    above = send(numbers_s, above_way)

    shape = (nodes, rows, cols)
    patch, padded = bf(rows, line, width), bf(rows + 2, line + 2 * nodes, width)
    edge_shapes = (bf(line, width), bf(line, width), bf(rows * nodes, width))
    square = jax.ShapeDtypeStruct((width, width), F32)
    sums_shape = jax.ShapeDtypeStruct((8, width), F32)
    goal_shape = jax.ShapeDtypeStruct(target.shape, F32)
    block = nodes * width
    edge, inside = 2 * cols + rows - 2, (rows - 2) * (cols - 1)

    def cost(products, denses):
        return pl.CostEstimate(
            flops=2 * block * (products * 6 * nodes + denses * width),
            bytes_accessed=4 * block * (products + denses),
            transcendentals=block * products,
        )

    table, f_field, x_field, m_one, outer_s, inner_s, side_s = pl.pallas_call(
        functools.partial(first_edge_kernel, shape),
        out_shape=(jax.ShapeDtypeStruct((5 * rows, 128), jnp.int32), padded, padded, patch) + edge_shapes,
        in_specs=[VMEM] * 8 + [ANY] + [VMEM] * 2,
        out_specs=(SMEM,) + (VMEM,) * 6,
        scratch_shapes=[
            pltpu.VMEM((TAIL, width), F32),
            pltpu.VMEM((TAIL, width), F32),
            pltpu.VMEM((5 * rows, 128), jnp.int32),
            sems(1),
        ],
        compiler_params=params,
        cost_estimate=cost(edge, edge),
        name="first_edge",
    )(numbers, above, features, ends, middle, outer, inner, side, goal_swap, tiles, w_first)

    outer, inner, side = edges(outer_s, inner_s, side_s)
    edge_terms = jax.ShapeDtypeStruct((edge * nodes, width), F32)
    x_field, m_one, m_two, gz_two, g_field, preds, goals, sums, local = pl.pallas_call(
        functools.partial(middle_compute_kernel, shape, scale),
        out_shape=(padded, patch, patch, patch, padded, goal_shape, goal_shape, sums_shape, edge_terms),
        in_specs=[SMEM] + [VMEM] * 11,
        out_specs=(VMEM,) * 9,
        input_output_aliases={10: 0, 11: 1},
        compiler_params=params,
        cost_estimate=cost(2 * inside + edge, 3 * inside),
        name="inner_forward",
    )(table, f_field, tiles, w_first, w_second, w_turned, readout, spread, target, goal_swap, x_field, m_one)

    m_two, gz_two, g_field, preds, sums, outer_s, inner_s, side_s = pl.pallas_call(
        functools.partial(second_edge_kernel, shape, scale),
        out_shape=(patch, patch, padded, goal_shape, sums_shape) + edge_shapes,
        in_specs=[SMEM] + [VMEM] * 16,
        out_specs=(VMEM,) * 8,
        input_output_aliases={12 + i: i for i in range(5)},
        compiler_params=params,
        cost_estimate=cost(edge // 4, 2 * edge),
        name="second_edge",
    )(table, outer, inner, side, tiles, w_second, w_turned, readout, spread, goals, x_field, local,
      m_two, gz_two, g_field, preds, sums)

    outer, inner, side = edges(outer_s, inner_s, side_s)
    first, second, local, slopes, m_turned = pl.pallas_call(
        functools.partial(back_inner_kernel, shape, scale),
        out_shape=(square, square, edge_terms, edge_terms, bf(width, edge * nodes)),
        in_specs=[SMEM] + [VMEM] * 9,
        out_specs=(VMEM,) * 5,
        compiler_params=params,
        cost_estimate=cost(rows * cols, 3 * rows * cols),
        name="back_inner",
    )(table, g_field, tiles, w_first, readout, goals, preds, m_one, m_two, gz_two)

    share, riding = width // count, step * nodes // width
    outs = pl.pallas_call(
        functools.partial(back_edge_kernel, shape),
        out_shape=shares_shape(count // 2, 2 * share, width, 2, riding),
        in_specs=[SMEM] + [VMEM] * 11,
        out_specs=(VMEM,) * 2,
        scratch_shapes=[pltpu.VMEM((count, 2 * share, width), F32)],
        compiler_params=params,
        cost_estimate=cost(edge // 4, edge),
        name="back_edge",
    )(table, outer, inner, side, tiles, preds, m_turned, first, second, sums, local, slopes)
    first, second, extra, pred_out = sum_shares(outs, preds, count, share, width, riding, params)
    return pred_out, first, second, extra[0]


def solution(mesh):
    in_specs = (
        P(("groups", "wide"), "narrow", None, None),
        P(("groups", "wide"), "narrow", None),
        P(),
        P(),
        P(),
        P(),
        P(("groups", "wide"), "narrow", None),
    )
    out_specs = (
        P(("groups", "wide"), "narrow", None),
        P(("groups", "wide", "narrow"), None),
        P(("groups", "wide", "narrow"), None),
        P("groups"),
    )
    return jax.shard_map(
        per_device, mesh=mesh, in_specs=in_specs, out_specs=out_specs, check_vma=False
    )
```

```python
import functools

import jax
import jax.numpy as jnp
import numpy as np
from jax import lax
from jax.experimental import pallas as pl
from jax.experimental.pallas import tpu as pltpu
from jax.sharding import PartitionSpec as P

F32 = jnp.float32
BF16 = jnp.bfloat16
AXES = ("wide", "narrow")
VMEM_LIMIT = 16 * 1024 * 1024
ANY = pl.BlockSpec(memory_space=pl.ANY)
VMEM = pl.BlockSpec(memory_space=pltpu.VMEM)
SMEM = pl.BlockSpec(memory_space=pltpu.SMEM)

SELF, EAST, WEST, NORTH, SOUTH = 0, 1, 2, 3, 4
TAIL = 16


def routes(wide):
    depth = wide // 2

    def at(z, y, c):
        return (2 * z + y) * 2 + c

    every = [(z, y, c) for z in range(depth) for y in range(2) for c in range(2)]
    swap = [(at(z, c, y), at(z, y, c)) for z, y, c in every if y != c]
    first_side = [(at(z, c, 1 - y), at(z, y, c)) for z, y, c in every]
    inner = [(at(z, y, 1 - c), at(z, y, c)) for z, y, c in every]
    outer = [(at(z - 1, y, 1), at(z, y, 0)) for z, y, c in every if c == 0 and z > 0]
    outer += [(at(z + 1, y, 0), at(z, y, 1)) for z, y, c in every if c == 1 and z + 1 < depth]
    side = [(at(z, 1 - y, c), at(z, y, c)) for z, y, c in every]
    above = [(at(z, 0, y), at(z, y, 1)) for z, y, c in every if c == 1]
    above += [(at(z - 1, 1, y), at(z, y, 0)) for z, y, c in every if c == 0 and z > 0]
    return swap, first_side, inner, outer, side, above


def place():
    half = lax.axis_index("narrow")
    side = lax.rem(lax.axis_index("wide"), 2)
    return half, side, half != side


def start_all(pairs, sems, first=0):
    copies = [pltpu.make_async_copy(a, b, sems.at[first + i]) for i, (a, b) in enumerate(pairs)]
    for copy in copies:
        copy.start()
    return copies


def wait_all(copies):
    for copy in copies:
        copy.wait()


def at_block(col, nodes):
    return pl.ds(col * nodes if isinstance(col, int) else pl.multiple_of(col * nodes, nodes), nodes)


def block_product(table, field, tiles, row, col, shape):
    nodes, rows, cols = shape

    def number(kind):
        return table[kind * rows + row, col]

    def block(r, c):
        return field[r, at_block(c, nodes)]

    half = tiles.shape[0] // 2
    lhs = jnp.concatenate(
        [
            tiles[number(SELF)],
            tiles[half + number(SELF)],
            tiles[number(EAST)],
            tiles[half + number(WEST)],
            tiles[number(NORTH)],
            tiles[half + number(SOUTH)],
        ],
        axis=1,
    )
    centre = block(row + 1, col + 1)
    rhs = jnp.concatenate(
        [
            centre,
            centre,
            block(row + 2, col + 1),
            block(row, col + 1),
            block(row + 1, col + 2),
            block(row + 1, col),
        ],
        axis=0,
    )
    return jnp.dot(lhs, rhs, preferred_element_type=F32)


def edge_blocks(shape):
    _, rows, cols = shape
    half, right, _ = place()
    outer, inner = jnp.where(half == 0, 0, rows - 1), jnp.where(half == 0, rows - 1, 0)
    beside = jnp.where(right == 0, cols - 1, 0)
    blocks = [(outer, col) for col in range(cols)] + [(inner, col) for col in range(cols)]
    return blocks + [(row, beside) for row in range(1, rows - 1)]


def inner_blocks(shape):
    _, rows, cols = shape
    _, right, _ = place()
    return [(row, right + col) for row in range(1, rows - 1) for col in range(cols - 1)]


def gather(read, blocks):
    return jnp.concatenate([read(row, col) for row, col in blocks], axis=0)


def scatter(ref, blocks, value, nodes, shift):
    for k, (row, col) in enumerate(blocks):
        ref[row + shift, at_block(col + shift, nodes)] = value[k * nodes : (k + 1) * nodes]


def messages(table, field, tiles, blocks, shape):
    return gather(
        lambda row, col: block_product(table, field, tiles, row, col, shape).astype(BF16), blocks
    )


def rim_terms(table, tiles, outer, inner, side, shape):
    nodes, rows, cols = shape
    half, right, _ = place()
    turned = tiles.shape[0] // 2

    def product(tile, block):
        return jnp.dot(tiles[tile], block, preferred_element_type=F32)

    def beside(row):
        tile = jnp.where(right == 0, table[NORTH * rows + row, cols - 1], turned + table[SOUTH * rows + row, 0])
        return product(tile, side[at_block(row, nodes)])

    terms = []
    first, last = jnp.where(half == 0, 0, rows - 1), jnp.where(half == 0, rows - 1, 0)
    for line, row, upward in ((outer, first, half == 0), (inner, last, half == 1)):
        corner = beside(row)
        for col in range(cols):
            tile = jnp.where(upward, turned + table[WEST * rows + row, col], table[EAST * rows + row, col])
            term = product(tile, line[at_block(col, nodes)])
            if col in (0, cols - 1):
                term = term + jnp.where((right == 0) == (col > 0), corner, 0.0)
            terms.append(term)
    return jnp.concatenate(terms + [beside(row) for row in range(1, rows - 1)], axis=0)


def products(table, field, tiles, blocks, shape):
    return gather(lambda row, col: block_product(table, field, tiles, row, col, shape), blocks)


def forward_one(shape, table, field, tiles, weight, x_field, m_all):
    nodes = shape[0]

    def body(blocks):
        m = messages(table, field, tiles, blocks, shape)
        scatter(m_all, blocks, m, nodes, 0)
        z = jnp.dot(m, weight[...], preferred_element_type=F32)
        base = gather(lambda row, col: field[row + 1, at_block(col + 1, nodes)], blocks)
        scatter(x_field, blocks, (base.astype(F32) + jnp.tanh(z)).astype(BF16), nodes, 1)

    return body


def residual_columns(seen, goal, scale):
    gp = (seen - goal) * scale
    column = jnp.broadcast_to(gp, (gp.shape[1], gp.shape[1])).T
    return jnp.concatenate([column, column], axis=1)


def through_two(shape, scale, table, field, tiles, weight, weight_turned, readout, spread, goals, m_all, gz_all, g_field, preds, sums):
    nodes = shape[0]
    readf = readout[...].astype(F32)

    def body(blocks, m):
        scatter(m_all, blocks, m, nodes, 0)
        t = jnp.tanh(jnp.dot(m, weight[...], preferred_element_type=F32))
        base = gather(lambda row, col: field[row + 1, at_block(col + 1, nodes)], blocks)
        x = (base.astype(F32) + t).astype(BF16)
        seen = jnp.dot(x, spread[...], preferred_element_type=F32)
        parts = []
        for k, (row, col) in enumerate(blocks):
            one = seen[k * nodes : (k + 1) * nodes].T[0:1]
            preds[row, pl.ds(col, 1)] = one
            parts.append(residual_columns(one, goals[row, pl.ds(col, 1)], scale))
        gp = jnp.concatenate(parts, axis=0)
        sums[...] += (x.astype(F32) * gp).reshape(gp.shape[0] // 8, 8, gp.shape[1]).sum(axis=0)
        gz = (gp * readf * (1.0 - t * t)).astype(BF16)
        scatter(gz_all, blocks, gz, nodes, 0)
        g = jnp.dot(gz, weight_turned[...], preferred_element_type=F32).astype(BF16)
        scatter(g_field, blocks, g, nodes, 1)

    return body


def back_terms(scale, weight, readout, goals, preds, m_all, blocks, nodes):
    m = gather(lambda row, col: m_all[row, at_block(col, nodes)], blocks)
    t = jnp.tanh(jnp.dot(m, weight[...], preferred_element_type=F32))
    gp = gather(
        lambda row, col: residual_columns(preds[row, pl.ds(col, 1)], goals[row, pl.ds(col, 1)], scale), blocks
    )
    return gp * readout[...].astype(F32), 1.0 - t * t


def over_nodes(left, right):
    return lax.dot_general(left, right, (((0,), (0,)), ((), ())), preferred_element_type=F32)


def zero_rim(field, shape):
    nodes, rows, cols = shape
    field[0] = jnp.zeros(field.shape[1:], field.dtype)
    field[rows + 1] = jnp.zeros(field.shape[1:], field.dtype)
    for row in range(1, rows + 1):
        for col in (0, cols + 1):
            field[row, at_block(col, nodes)] = jnp.zeros((nodes, field.shape[2]), field.dtype)


def take_edges(field, outer, inner, side, shape):
    nodes, rows, cols = shape
    half, right, _ = place()
    inside = pl.ds(nodes, cols * nodes)
    outer[...] = field[jnp.where(half == 0, 1, rows), inside]
    inner[...] = field[jnp.where(half == 0, rows, 1), inside]
    column = at_block(jnp.where(right == 0, cols, 1), nodes)
    for row in range(rows):
        side[at_block(row, nodes)] = field[row + 1, column]


def fill_rim(field, outer, inner, side, shape):
    nodes, rows, cols = shape
    half, right, _ = place()
    inside = pl.ds(nodes, cols * nodes)
    line = pl.ds(0, cols * nodes)
    field[jnp.where(half == 0, 0, rows + 1), inside] = outer[line]
    field[jnp.where(half == 0, rows + 1, 0), inside] = inner[line]
    empty, column = jnp.where(right == 0, 0, cols + 1), jnp.where(right == 0, cols + 1, 0)
    for row in range(rows):
        field[row + 1, at_block(empty, nodes)] = jnp.zeros((nodes, field.shape[2]), field.dtype)
        field[row + 1, at_block(column, nodes)] = side[at_block(row, nodes)]


def pack_kernel(nodes, cols, ids, own, after, side, numbers, wide_ids, sems):
    rows = own.shape[0]
    half, _, _ = place()
    col = pl.multiple_of(jnp.where(half == 1, 0, (cols - 1) * nodes), nodes)
    copies = start_all(
        [(own.at[row, pl.ds(col, nodes)], side.at[pl.ds(row * nodes, nodes)]) for row in range(rows)], sems
    )
    wide_ids[...] = jnp.zeros_like(wide_ids)
    for kind in range(3):
        wide_ids[kind * rows : (kind + 1) * rows, 0:cols] = ids[kind]
    tail = wide_ids[...].astype(BF16)
    numbers[...] = tail
    side[rows * nodes :] = tail
    wait_all(copies)


def middle_kernel(own, numbers, middle, sems):
    rows, line = own.shape[0], own.shape[1]
    copies = start_all([(own.at[row + 1], middle.at[pl.ds(row * line, line)]) for row in range(rows - 2)], sems)
    middle[(rows - 2) * line :] = numbers[...]
    wait_all(copies)


def prepare_kernel(tiles, first, second, both, first_in, second_in, second_turned, sems):
    number = tiles.shape[0]
    wait_all(start_all([(tiles, both.at[pl.ds(0, number)]), (first, first_in), (second, second_in)], sems))

    second_turned[...] = second_in[...].T

    def one_tile(tile, carry):
        both[number + tile] = both[tile].T
        return carry

    lax.fori_loop(0, number, one_tile, 0)


def pick_kernel(own, ends, after, outer, inner, sems):
    rows, line = own.shape[0], own.shape[1]
    half, _, moved = place()

    @pl.when(moved)
    def _():
        outer[...] = ends[pl.ds(pl.multiple_of(half * line, line), line)]
        inner[...] = ends[pl.ds(pl.multiple_of((1 - half) * line, line), line)]

    @pl.when(jnp.logical_not(moved))
    def _():
        wait_all(start_all([
            (own.at[jnp.where(half == 0, 0, rows - 1)], outer),
            (own.at[jnp.where(half == 0, rows - 1, 0)], inner),
        ], sems))


def first_edge_kernel(shape, numbers, above, own, ends, middle, outer, inner, side, later, tiles, weight,
                      table, field, x_field, m_all, outer_out, inner_out, side_out, own_ids, above_ids, spots, sems):
    nodes, rows, cols = shape
    line = cols * nodes
    _, _, moved = place()
    inside = pl.ds(nodes, line)
    @pl.when(moved)
    def _():
        own_ids[...] = middle[pl.ds((rows - 2) * line, TAIL)].astype(F32)

    @pl.when(jnp.logical_not(moved))
    def _():
        own_ids[...] = numbers[...].astype(F32)

    above_ids[...] = above[...].astype(F32)
    left = side[pl.ds(rows * nodes, TAIL)].astype(F32)[2 * rows : 3 * rows, 0:128]
    north = own_ids[2 * rows : 3 * rows, 0:128]
    lanes = lax.broadcasted_iota(jnp.int32, north.shape, 1)
    beside = jnp.broadcast_to(left[:, cols - 1 : cols], left.shape)
    spots[0 : 2 * rows] = own_ids[0 : 2 * rows, 0:128].astype(jnp.int32)
    spots[WEST * rows : WEST * rows + 1] = above_ids[2 * rows - 1 : 2 * rows, 0:128].astype(jnp.int32)
    spots[WEST * rows + 1 : (WEST + 1) * rows] = own_ids[rows : 2 * rows - 1, 0:128].astype(jnp.int32)
    spots[NORTH * rows : (NORTH + 1) * rows] = north.astype(jnp.int32)
    spots[SOUTH * rows : (SOUTH + 1) * rows] = jnp.where(lanes == 0, beside, pltpu.roll(north, 1, 1)).astype(jnp.int32)
    copies = start_all([(spots, table)], sems)

    @pl.when(moved)
    def _():
        field[1, inside] = ends[pl.ds(0, line)]
        field[rows, inside] = ends[pl.ds(line, line)]
        for row in range(2, rows):
            field[row, inside] = middle[pl.ds((row - 2) * line, line)]

    @pl.when(jnp.logical_not(moved))
    def _():
        for row in range(rows):
            field[row + 1, inside] = own[row]

    fill_rim(field, outer, inner, side, shape)
    wait_all(copies)
    forward_one(shape, table, field, tiles, weight, x_field, m_all)(edge_blocks(shape))
    take_edges(x_field, outer_out, inner_out, side_out, shape)


def middle_compute_kernel(shape, scale, table, field, tiles, weight_one, weight_two, two_turned, readout, spread, target,
                          target_swap, x_in, m_in, x_field, m_one, m_two, gz_two, g_field, preds, goals, sums, local):
    _, _, moved = place()

    @pl.when(moved)
    def _():
        goals[...] = target_swap[...]

    @pl.when(jnp.logical_not(moved))
    def _():
        goals[...] = target[...]

    zero_rim(x_field, shape)
    zero_rim(g_field, shape)
    sums[...] = jnp.zeros_like(sums)
    blocks = inner_blocks(shape)
    forward_one(shape, table, field, tiles, weight_one, x_field, m_one)(blocks)
    through_two(
        shape, scale, table, x_field, tiles, weight_two, two_turned, readout, spread, goals, m_two, gz_two,
        g_field, preds, sums,
    )(blocks, messages(table, x_field, tiles, blocks, shape))
    local[...] = products(table, x_field, tiles, edge_blocks(shape), shape)


def second_edge_kernel(shape, scale, table, outer, inner, side, tiles, weight, weight_turned, readout, spread, goals,
                       x_field, local, m_in, gz_in, g_in, preds_in, sums_in,
                       m_two, gz_two, g_field, preds, sums, outer_out, inner_out, side_out):
    m = (local[...] + rim_terms(table, tiles, outer, inner, side, shape)).astype(BF16)
    through_two(
        shape, scale, table, x_field, tiles, weight, weight_turned, readout, spread, goals, m_two, gz_two,
        g_field, preds, sums,
    )(edge_blocks(shape), m)
    take_edges(g_field, outer_out, inner_out, side_out, shape)


def back_inner_kernel(shape, scale, table, g_field, tiles, weight, readout, goals, preds, m_one, m_two, gz_two,
                      first_out, second_out, local, slopes, m_turned):
    nodes, rows, cols = shape
    blocks = inner_blocks(shape)
    gx, slope = back_terms(scale, weight, readout, goals, preds, m_one, blocks, nodes)
    gz = ((gx + products(table, g_field, tiles, blocks, shape)) * slope).astype(BF16)
    first_out[...] = over_nodes(gather(lambda row, col: m_one[row, at_block(col, nodes)], blocks), gz)
    gx, slope = back_terms(scale, weight, readout, goals, preds, m_one, edge_blocks(shape), nodes)
    local[...] = gx + products(table, g_field, tiles, edge_blocks(shape), shape)
    slopes[...] = slope
    m_turned[...] = gather(lambda row, col: m_one[row, at_block(col, nodes)], edge_blocks(shape)).T
    second_out[...] = jnp.zeros_like(second_out)

    def each_row(row, carry):
        second_out[...] += over_nodes(m_two[row], gz_two[row])
        return carry

    lax.fori_loop(0, rows, each_row, 0)


def back_edge_kernel(shape, table, outer, inner, side, tiles, preds, m_turned, first_in, second, sums, local, slopes,
                     keep, one, parts):
    width = first_in.shape[1]
    gx = local[...] + rim_terms(table, tiles, outer, inner, side, shape)
    gz = (gx * slopes[...]).astype(BF16)
    first = first_in[...] + jnp.dot(m_turned[...], gz, preferred_element_type=F32)
    count, size, _ = parts.shape
    parts[:, : size // 2] = first.reshape(count, size // 2, width)
    parts[:, size // 2 :] = second[...].reshape(count, size // 2, width)
    spread_shares(parts, sums[...], lax.axis_index("narrow"), (keep, one))
    ride_preds(preds, one)


def spread_shares(parts, extra, digit, outs):
    size, radix = parts.shape[1], len(outs)
    groups = parts.shape[0] // radix
    for k, out in enumerate(outs):
        for group in range(groups):
            out[group * size : (group + 1) * size] = parts[radix * group + jnp.bitwise_xor(digit, k)]
        out[groups * size : groups * size + 8] = extra


def take_preds(preds, riding, pred_out):
    _, _, moved = place()
    start = riding.shape[0] - preds.shape[0] * preds.shape[1] // 2

    @pl.when(moved)
    def _():
        for row in range(preds.shape[0]):
            at = start + row // 2 * preds.shape[1]
            lane = row % 2 * preds.shape[2]
            pred_out[row] = riding[at : at + preds.shape[1], lane : lane + preds.shape[2]]

    @pl.when(jnp.logical_not(moved))
    def _():
        pred_out[...] = preds[...]


def ride_preds(preds, riding):
    start = riding.shape[0] - preds.shape[0] * preds.shape[1] // 2
    for row in range(preds.shape[0]):
        at = start + row // 2 * preds.shape[1]
        lane = row % 2 * preds.shape[2]
        riding[at : at + preds.shape[1], lane : lane + preds.shape[2]] = preds[row]


def fold_kernel(base, step, radix, keep, *refs):
    *got, preds = refs[: -1 - radix - (step == 2)]
    outs, parts = list(refs[len(got) + 1 : -1]), refs[-1]
    if step == 2:
        take_preds(preds, got[0], outs.pop())
    count, size, _ = parts.shape
    total = keep[...]
    for one in got:
        total = total + one[: keep.shape[0]]
    parts[...] = total[: count * size].reshape(parts.shape)
    spread_shares(parts, total[count * size :], lax.rem(lax.axis_index(AXES) // base, radix), outs)
    if step == 1:
        riding = got[0].shape[0] - keep.shape[0]
        outs[1][outs[1].shape[0] - riding :] = got[0][keep.shape[0] :]


def last_fold_kernel(keep, *refs):
    *got, first, second, readout = refs
    share = first.shape[0]
    total = keep[...]
    for one in got:
        total = total + one[...]
    first[...] = total[:share]
    second[...] = total[share : 2 * share]
    readout[...] = total[2 * share :].sum(axis=0, keepdims=True)


def shares_shape(groups, size, width, radix, riding=0):
    rows = [groups * size + 8] * radix
    rows[1] += riding
    return tuple(jax.ShapeDtypeStruct((number, width), F32) for number in rows)


def sum_shares(outs, preds, count, share, width, riding, params):
    radices, left = [2, 4], count // 8
    while left > 1:
        radices.append(min(4, left))
        left //= radices[-1]
    base, groups, pred_out = 1, count // 2, None
    for step, radix in enumerate(radices):
        got = [
            lax.ppermute(outs[k], AXES, [(i, i ^ (k * base)) for i in range(count)]) for k in range(1, radix)
        ]
        if step == len(radices) - 1:
            break
        base *= radix
        radix = radices[step + 1]
        more = (jax.ShapeDtypeStruct(preds.shape, F32),) if step == 1 else ()
        shapes = shares_shape(groups // radix, 2 * share, width, radix, riding if step == 0 else 0) + more
        folded = pl.pallas_call(
            functools.partial(fold_kernel, base, step + 1, radix),
            out_shape=shapes,
            in_specs=[VMEM] * (2 + len(got)),
            out_specs=(VMEM,) * len(shapes),
            scratch_shapes=[pltpu.VMEM((groups, 2 * share, width), F32)],
            compiler_params=params,
            name="fold",
        )(outs[0], *got, preds)
        outs = folded[:radix]
        if more:
            pred_out = folded[-1]
        groups //= radix
    small = jax.ShapeDtypeStruct((share, width), F32)
    sums = pl.pallas_call(
        last_fold_kernel,
        out_shape=(small, small, jax.ShapeDtypeStruct((1, width), F32)),
        in_specs=[VMEM] * (1 + len(got)),
        out_specs=(VMEM,) * 3,
        compiler_params=params,
        name="last_fold",
    )(outs[0], *got)
    return *sums, pred_out


def per_device(features, tile_ids, tiles, w_first, w_second, readout, target):
    rows, cols, nodes, width = features.shape
    wide, narrow = lax.axis_size("wide"), lax.axis_size("narrow")
    count = wide * narrow
    line, step = cols * nodes, rows * cols
    swap, first_side, inner_way, outer_way, side_way, above_way = routes(wide)
    scale = float(np.sqrt(np.float32(width) / np.float32(rows * line * count)))
    params = pltpu.CompilerParams(vmem_limit_bytes=VMEM_LIMIT)

    def send(value, way):
        return lax.ppermute(value, AXES, way)

    def edges(outer, inner, side):
        return send(outer, outer_way), send(inner, inner_way), send(side, side_way)

    def bf(*shape):
        return jax.ShapeDtypeStruct(shape, BF16)

    def sems(number):
        return pltpu.SemaphoreType.DMA((number,))

    features = features.reshape(rows, line, width)
    ends_s = features[0 :: rows - 1].reshape(2 * line, width)
    ends = send(ends_s, swap)
    side_s, numbers = pl.pallas_call(
        functools.partial(pack_kernel, nodes, cols),
        out_shape=(bf(rows * nodes + TAIL, width), bf(TAIL, width)),
        in_specs=[VMEM, ANY, ANY],
        out_specs=(VMEM,) * 2,
        scratch_shapes=[pltpu.VMEM((TAIL, width), F32), sems(rows)],
        compiler_params=params,
        name="pack",
    )(jnp.transpose(tile_ids, (2, 0, 1)).astype(F32), features, ends_s)
    side = send(side_s, first_side)
    middle_s = pl.pallas_call(
        middle_kernel,
        out_shape=bf((rows - 2) * line + TAIL, width),
        in_specs=[ANY, VMEM],
        out_specs=VMEM,
        scratch_shapes=[sems(rows - 2)],
        compiler_params=params,
        name="pack_middle",
    )(features, numbers)
    middle = send(middle_s, swap)
    tiles, w_first, w_second, _ = lax.optimization_barrier((tiles, w_first, w_second, middle_s))
    tiles, w_first, w_second, w_turned = pl.pallas_call(
        prepare_kernel,
        out_shape=(bf(2 * tiles.shape[0], nodes, nodes),) + (bf(width, width),) * 3,
        in_specs=[ANY] * 3,
        out_specs=(VMEM,) * 4,
        scratch_shapes=[sems(3)],
        compiler_params=params,
        name="prepare",
    )(tiles, w_first, w_second)
    spread = jnp.broadcast_to(readout[:, None], (width, 128))
    readout = readout[None]

    outer_s, inner_s = pl.pallas_call(
        pick_kernel,
        out_shape=(bf(line, width),) * 2,
        in_specs=[ANY, VMEM, ANY],
        out_specs=(VMEM,) * 2,
        scratch_shapes=[sems(4)],
        compiler_params=params,
        name="pick",
    )(features, ends, side)
    outer, inner = send(outer_s, outer_way), send(inner_s, inner_way)
    target_s, numbers_s, _ = lax.optimization_barrier((target, numbers, inner_s))
    goal_swap = send(target_s, swap)
    above = send(numbers_s, above_way)

    shape = (nodes, rows, cols)
    patch, padded = bf(rows, line, width), bf(rows + 2, line + 2 * nodes, width)
    edge_shapes = (bf(line, width), bf(line, width), bf(rows * nodes, width))
    square = jax.ShapeDtypeStruct((width, width), F32)
    sums_shape = jax.ShapeDtypeStruct((8, width), F32)
    goal_shape = jax.ShapeDtypeStruct(target.shape, F32)
    block = nodes * width
    edge, inside = 2 * cols + rows - 2, (rows - 2) * (cols - 1)

    def cost(products, denses):
        return pl.CostEstimate(
            flops=2 * block * (products * 6 * nodes + denses * width),
            bytes_accessed=4 * block * (products + denses),
            transcendentals=block * products,
        )

    table, f_field, x_field, m_one, outer_s, inner_s, side_s = pl.pallas_call(
        functools.partial(first_edge_kernel, shape),
        out_shape=(jax.ShapeDtypeStruct((5 * rows, 128), jnp.int32), padded, padded, patch) + edge_shapes,
        in_specs=[VMEM] * 8 + [ANY] + [VMEM] * 2,
        out_specs=(SMEM,) + (VMEM,) * 6,
        scratch_shapes=[
            pltpu.VMEM((TAIL, width), F32),
            pltpu.VMEM((TAIL, width), F32),
            pltpu.VMEM((5 * rows, 128), jnp.int32),
            sems(1),
        ],
        compiler_params=params,
        cost_estimate=cost(edge, edge),
        name="first_edge",
    )(numbers, above, features, ends, middle, outer, inner, side, goal_swap, tiles, w_first)

    outer, inner, side = edges(outer_s, inner_s, side_s)
    edge_terms = jax.ShapeDtypeStruct((edge * nodes, width), F32)
    x_field, m_one, m_two, gz_two, g_field, preds, goals, sums, local = pl.pallas_call(
        functools.partial(middle_compute_kernel, shape, scale),
        out_shape=(padded, patch, patch, patch, padded, goal_shape, goal_shape, sums_shape, edge_terms),
        in_specs=[SMEM] + [VMEM] * 11,
        out_specs=(VMEM,) * 9,
        input_output_aliases={10: 0, 11: 1},
        compiler_params=params,
        cost_estimate=cost(2 * inside + edge, 3 * inside),
        name="inner_forward",
    )(table, f_field, tiles, w_first, w_second, w_turned, readout, spread, target, goal_swap, x_field, m_one)

    m_two, gz_two, g_field, preds, sums, outer_s, inner_s, side_s = pl.pallas_call(
        functools.partial(second_edge_kernel, shape, scale),
        out_shape=(patch, patch, padded, goal_shape, sums_shape) + edge_shapes,
        in_specs=[SMEM] + [VMEM] * 16,
        out_specs=(VMEM,) * 8,
        input_output_aliases={12 + i: i for i in range(5)},
        compiler_params=params,
        cost_estimate=cost(edge // 4, 2 * edge),
        name="second_edge",
    )(table, outer, inner, side, tiles, w_second, w_turned, readout, spread, goals, x_field, local,
      m_two, gz_two, g_field, preds, sums)

    outer, inner, side = edges(outer_s, inner_s, side_s)
    first, second, local, slopes, m_turned = pl.pallas_call(
        functools.partial(back_inner_kernel, shape, scale),
        out_shape=(square, square, edge_terms, edge_terms, bf(width, edge * nodes)),
        in_specs=[SMEM] + [VMEM] * 9,
        out_specs=(VMEM,) * 5,
        compiler_params=params,
        cost_estimate=cost(rows * cols, 3 * rows * cols),
        name="back_inner",
    )(table, g_field, tiles, w_first, readout, goals, preds, m_one, m_two, gz_two)

    share, riding = width // count, step * nodes // width
    outs = pl.pallas_call(
        functools.partial(back_edge_kernel, shape),
        out_shape=shares_shape(count // 2, 2 * share, width, 2, riding),
        in_specs=[SMEM] + [VMEM] * 11,
        out_specs=(VMEM,) * 2,
        scratch_shapes=[pltpu.VMEM((count, 2 * share, width), F32)],
        compiler_params=params,
        cost_estimate=cost(edge // 4, edge),
        name="back_edge",
    )(table, outer, inner, side, tiles, preds, m_turned, first, second, sums, local, slopes)
    first, second, extra, pred_out = sum_shares(outs, preds, count, share, width, riding, params)
    return pred_out, first, second, extra[0]


def solution(mesh):
    in_specs = (
        P(("groups", "wide"), "narrow", None, None),
        P(("groups", "wide"), "narrow", None),
        P(),
        P(),
        P(),
        P(),
        P(("groups", "wide"), "narrow", None),
    )
    out_specs = (
        P(("groups", "wide"), "narrow", None),
        P(("groups", "wide", "narrow"), None),
        P(("groups", "wide", "narrow"), None),
        P("groups"),
    )
    return jax.shard_map(
        per_device, mesh=mesh, in_specs=in_specs, out_specs=out_specs, check_vma=False
    )
```

```python
import functools

import jax
import jax.numpy as jnp
import numpy as np
from jax import lax
from jax.experimental import pallas as pl
from jax.experimental.pallas import tpu as pltpu
from jax.sharding import PartitionSpec as P

F32 = jnp.float32
BF16 = jnp.bfloat16
AXES = ("wide", "narrow")
VMEM_LIMIT = 16 * 1024 * 1024
ANY = pl.BlockSpec(memory_space=pl.ANY)
VMEM = pl.BlockSpec(memory_space=pltpu.VMEM)
SMEM = pl.BlockSpec(memory_space=pltpu.SMEM)

SELF, EAST, WEST, NORTH, SOUTH = 0, 1, 2, 3, 4
TAIL = 16


def routes(wide):
    depth = wide // 2

    def at(z, y, c):
        return (2 * z + y) * 2 + c

    every = [(z, y, c) for z in range(depth) for y in range(2) for c in range(2)]
    swap = [(at(z, c, y), at(z, y, c)) for z, y, c in every if y != c]
    first_side = [(at(z, c, 1 - y), at(z, y, c)) for z, y, c in every]
    inner = [(at(z, y, 1 - c), at(z, y, c)) for z, y, c in every]
    outer = [(at(z - 1, y, 1), at(z, y, 0)) for z, y, c in every if c == 0 and z > 0]
    outer += [(at(z + 1, y, 0), at(z, y, 1)) for z, y, c in every if c == 1 and z + 1 < depth]
    side = [(at(z, 1 - y, c), at(z, y, c)) for z, y, c in every]
    above = [(at(z, 0, y), at(z, y, 1)) for z, y, c in every if c == 1]
    above += [(at(z - 1, 1, y), at(z, y, 0)) for z, y, c in every if c == 0 and z > 0]
    return swap, first_side, inner, outer, side, above


def place():
    half = lax.axis_index("narrow")
    side = lax.rem(lax.axis_index("wide"), 2)
    return half, side, half != side


def start_all(pairs, sems, first=0):
    copies = [pltpu.make_async_copy(a, b, sems.at[first + i]) for i, (a, b) in enumerate(pairs)]
    for copy in copies:
        copy.start()
    return copies


def wait_all(copies):
    for copy in copies:
        copy.wait()


def at_block(col, nodes):
    return pl.ds(col * nodes if isinstance(col, int) else pl.multiple_of(col * nodes, nodes), nodes)


def block_product(table, field, tiles, row, col, shape):
    nodes, rows, cols = shape

    def number(kind):
        return table[kind * rows + row, col]

    def block(r, c):
        return field[r, at_block(c, nodes)]

    half = tiles.shape[0] // 2
    lhs = jnp.concatenate(
        [
            tiles[number(SELF)],
            tiles[half + number(SELF)],
            tiles[number(EAST)],
            tiles[half + number(WEST)],
            tiles[number(NORTH)],
            tiles[half + number(SOUTH)],
        ],
        axis=1,
    )
    centre = block(row + 1, col + 1)
    rhs = jnp.concatenate(
        [
            centre,
            centre,
            block(row + 2, col + 1),
            block(row, col + 1),
            block(row + 1, col + 2),
            block(row + 1, col),
        ],
        axis=0,
    )
    return jnp.dot(lhs, rhs, preferred_element_type=F32)


def edge_blocks(shape):
    _, rows, cols = shape
    half, right, _ = place()
    outer, inner = jnp.where(half == 0, 0, rows - 1), jnp.where(half == 0, rows - 1, 0)
    beside = jnp.where(right == 0, cols - 1, 0)
    blocks = [(outer, col) for col in range(cols)] + [(inner, col) for col in range(cols)]
    return blocks + [(row, beside) for row in range(1, rows - 1)]


def inner_blocks(shape):
    _, rows, cols = shape
    _, right, _ = place()
    return [(row, right + col) for row in range(1, rows - 1) for col in range(cols - 1)]


def gather(read, blocks):
    return jnp.concatenate([read(row, col) for row, col in blocks], axis=0)


def scatter(ref, blocks, value, nodes, shift):
    for k, (row, col) in enumerate(blocks):
        ref[row + shift, at_block(col + shift, nodes)] = value[k * nodes : (k + 1) * nodes]


def messages(table, field, tiles, blocks, shape):
    return gather(
        lambda row, col: block_product(table, field, tiles, row, col, shape).astype(BF16), blocks
    )


def rim_terms(table, tiles, outer, inner, side, shape):
    nodes, rows, cols = shape
    half, right, _ = place()
    turned = tiles.shape[0] // 2

    def product(tile, block):
        return jnp.dot(tiles[tile], block, preferred_element_type=F32)

    def beside(row):
        tile = jnp.where(right == 0, table[NORTH * rows + row, cols - 1], turned + table[SOUTH * rows + row, 0])
        return product(tile, side[at_block(row, nodes)])

    terms = []
    first, last = jnp.where(half == 0, 0, rows - 1), jnp.where(half == 0, rows - 1, 0)
    for line, row, upward in ((outer, first, half == 0), (inner, last, half == 1)):
        corner = beside(row)
        for col in range(cols):
            tile = jnp.where(upward, turned + table[WEST * rows + row, col], table[EAST * rows + row, col])
            term = product(tile, line[at_block(col, nodes)])
            if col in (0, cols - 1):
                term = term + jnp.where((right == 0) == (col > 0), corner, 0.0)
            terms.append(term)
    return jnp.concatenate(terms + [beside(row) for row in range(1, rows - 1)], axis=0)


def products(table, field, tiles, blocks, shape):
    return gather(lambda row, col: block_product(table, field, tiles, row, col, shape), blocks)


def forward_one(shape, table, field, tiles, weight, x_field, m_all):
    nodes = shape[0]

    def body(blocks):
        m = messages(table, field, tiles, blocks, shape)
        scatter(m_all, blocks, m, nodes, 0)
        z = jnp.dot(m, weight[...], preferred_element_type=F32)
        base = gather(lambda row, col: field[row + 1, at_block(col + 1, nodes)], blocks)
        scatter(x_field, blocks, (base.astype(F32) + jnp.tanh(z)).astype(BF16), nodes, 1)

    return body


def residual_columns(seen, goal, scale):
    gp = (seen - goal) * scale
    column = jnp.broadcast_to(gp, (gp.shape[1], gp.shape[1])).T
    return jnp.concatenate([column, column], axis=1)


def columns_of(goals, blocks):
    rows = [goals[row, pl.ds(col, 1)] for row, col in blocks]
    nodes = rows[0].shape[1]
    turned = jnp.concatenate(rows + [jnp.zeros((nodes - len(rows), nodes), F32)], axis=0).T
    return jnp.concatenate(
        [jnp.broadcast_to(turned[:, k : k + 1], (nodes, nodes)) for k in range(len(rows))], axis=0
    )


def through_two(shape, scale, table, field, tiles, weight, weight_turned, readout, spread, m_all, gz_all, g_field, preds, sums):
    nodes = shape[0]
    readf = readout[...].astype(F32)

    def body(blocks, m, goal_columns):
        scatter(m_all, blocks, m, nodes, 0)
        t = jnp.tanh(jnp.dot(m, weight[...], preferred_element_type=F32))
        base = gather(lambda row, col: field[row + 1, at_block(col + 1, nodes)], blocks)
        x = (base.astype(F32) + t).astype(BF16)
        seen = jnp.dot(x, spread[...], preferred_element_type=F32)
        lanes = lax.broadcasted_iota(jnp.int32, (nodes, 128), 1)
        packed = jnp.zeros((nodes, 128), F32)
        for k in range(len(blocks)):
            packed = jnp.where(lanes == k, seen[k * nodes : (k + 1) * nodes], packed)
        packed = packed.T
        for k, (row, col) in enumerate(blocks):
            preds[row, pl.ds(col, 1)] = packed[k : k + 1]
        gp = (seen - goal_columns) * scale
        gp = jnp.concatenate([gp, gp], axis=1)
        sums[...] += (x.astype(F32) * gp).reshape(gp.shape[0] // 8, 8, gp.shape[1]).sum(axis=0)
        gz = (gp * readf * (1.0 - t * t)).astype(BF16)
        scatter(gz_all, blocks, gz, nodes, 0)
        g = jnp.dot(gz, weight_turned[...], preferred_element_type=F32).astype(BF16)
        scatter(g_field, blocks, g, nodes, 1)

    return body


def back_terms(scale, weight, readout, goals, preds, m_all, blocks, nodes):
    m = gather(lambda row, col: m_all[row, at_block(col, nodes)], blocks)
    t = jnp.tanh(jnp.dot(m, weight[...], preferred_element_type=F32))
    gp = gather(
        lambda row, col: residual_columns(preds[row, pl.ds(col, 1)], goals[row, pl.ds(col, 1)], scale), blocks
    )
    return gp * readout[...].astype(F32), 1.0 - t * t


def over_nodes(left, right):
    return lax.dot_general(left, right, (((0,), (0,)), ((), ())), preferred_element_type=F32)


def zero_rim(field, shape):
    nodes, rows, cols = shape
    field[0] = jnp.zeros(field.shape[1:], field.dtype)
    field[rows + 1] = jnp.zeros(field.shape[1:], field.dtype)
    for row in range(1, rows + 1):
        for col in (0, cols + 1):
            field[row, at_block(col, nodes)] = jnp.zeros((nodes, field.shape[2]), field.dtype)


def take_edges(field, outer, inner, side, shape):
    nodes, rows, cols = shape
    half, right, _ = place()
    inside = pl.ds(nodes, cols * nodes)
    outer[...] = field[jnp.where(half == 0, 1, rows), inside]
    inner[...] = field[jnp.where(half == 0, rows, 1), inside]
    column = at_block(jnp.where(right == 0, cols, 1), nodes)
    for row in range(rows):
        side[at_block(row, nodes)] = field[row + 1, column]


def fill_rim(field, outer, inner, side, shape):
    nodes, rows, cols = shape
    half, right, _ = place()
    inside = pl.ds(nodes, cols * nodes)
    line = pl.ds(0, cols * nodes)
    field[jnp.where(half == 0, 0, rows + 1), inside] = outer[line]
    field[jnp.where(half == 0, rows + 1, 0), inside] = inner[line]
    empty, column = jnp.where(right == 0, 0, cols + 1), jnp.where(right == 0, cols + 1, 0)
    for row in range(rows):
        field[row + 1, at_block(empty, nodes)] = jnp.zeros((nodes, field.shape[2]), field.dtype)
        field[row + 1, at_block(column, nodes)] = side[at_block(row, nodes)]


def pack_kernel(nodes, cols, ids, own, after, side, numbers, wide_ids, sems):
    rows = own.shape[0]
    half, _, _ = place()
    col = pl.multiple_of(jnp.where(half == 1, 0, (cols - 1) * nodes), nodes)
    copies = start_all(
        [(own.at[row, pl.ds(col, nodes)], side.at[pl.ds(row * nodes, nodes)]) for row in range(rows)], sems
    )
    wide_ids[...] = jnp.zeros_like(wide_ids)
    for kind in range(3):
        wide_ids[kind * rows : (kind + 1) * rows, 0:cols] = ids[kind]
    tail = wide_ids[...].astype(BF16)
    numbers[...] = tail
    side[rows * nodes :] = tail
    wait_all(copies)


def middle_kernel(own, numbers, middle, sems):
    rows, line = own.shape[0], own.shape[1]
    copies = start_all([(own.at[row + 1], middle.at[pl.ds(row * line, line)]) for row in range(rows - 2)], sems)
    middle[(rows - 2) * line :] = numbers[...]
    wait_all(copies)


def prepare_kernel(tiles, first, second, both, first_in, second_in, second_turned, sems):
    number = tiles.shape[0]
    wait_all(start_all([(tiles, both.at[pl.ds(0, number)]), (first, first_in), (second, second_in)], sems))

    second_turned[...] = second_in[...].T

    def one_tile(tile, carry):
        both[number + tile] = both[tile].T
        return carry

    lax.fori_loop(0, number, one_tile, 0)


def pick_kernel(own, ends, after, outer, inner, sems):
    rows, line = own.shape[0], own.shape[1]
    half, _, moved = place()

    @pl.when(moved)
    def _():
        outer[...] = ends[pl.ds(pl.multiple_of(half * line, line), line)]
        inner[...] = ends[pl.ds(pl.multiple_of((1 - half) * line, line), line)]

    @pl.when(jnp.logical_not(moved))
    def _():
        wait_all(start_all([
            (own.at[jnp.where(half == 0, 0, rows - 1)], outer),
            (own.at[jnp.where(half == 0, rows - 1, 0)], inner),
        ], sems))


def first_edge_kernel(shape, numbers, above, own, ends, middle, outer, inner, side, later, tiles, weight,
                      table, field, x_field, m_all, outer_out, inner_out, side_out, own_ids, above_ids, spots, sems):
    nodes, rows, cols = shape
    line = cols * nodes
    _, _, moved = place()
    inside = pl.ds(nodes, line)
    @pl.when(moved)
    def _():
        own_ids[...] = middle[pl.ds((rows - 2) * line, TAIL)].astype(F32)

    @pl.when(jnp.logical_not(moved))
    def _():
        own_ids[...] = numbers[...].astype(F32)

    above_ids[...] = above[...].astype(F32)
    left = side[pl.ds(rows * nodes, TAIL)].astype(F32)[2 * rows : 3 * rows, 0:128]
    north = own_ids[2 * rows : 3 * rows, 0:128]
    lanes = lax.broadcasted_iota(jnp.int32, north.shape, 1)
    beside = jnp.broadcast_to(left[:, cols - 1 : cols], left.shape)
    spots[0 : 2 * rows] = own_ids[0 : 2 * rows, 0:128].astype(jnp.int32)
    spots[WEST * rows : WEST * rows + 1] = above_ids[2 * rows - 1 : 2 * rows, 0:128].astype(jnp.int32)
    spots[WEST * rows + 1 : (WEST + 1) * rows] = own_ids[rows : 2 * rows - 1, 0:128].astype(jnp.int32)
    spots[NORTH * rows : (NORTH + 1) * rows] = north.astype(jnp.int32)
    spots[SOUTH * rows : (SOUTH + 1) * rows] = jnp.where(lanes == 0, beside, pltpu.roll(north, 1, 1)).astype(jnp.int32)
    copies = start_all([(spots, table)], sems)

    @pl.when(moved)
    def _():
        field[1, inside] = ends[pl.ds(0, line)]
        field[rows, inside] = ends[pl.ds(line, line)]
        for row in range(2, rows):
            field[row, inside] = middle[pl.ds((row - 2) * line, line)]

    @pl.when(jnp.logical_not(moved))
    def _():
        for row in range(rows):
            field[row + 1, inside] = own[row]

    fill_rim(field, outer, inner, side, shape)
    wait_all(copies)
    forward_one(shape, table, field, tiles, weight, x_field, m_all)(edge_blocks(shape))
    take_edges(x_field, outer_out, inner_out, side_out, shape)


def middle_compute_kernel(shape, scale, table, field, tiles, weight_one, weight_two, two_turned, readout, spread, target,
                          target_swap, x_in, m_in, x_field, m_one, m_two, gz_two, g_field, preds, goals, sums, local, goal_columns):
    _, _, moved = place()

    @pl.when(moved)
    def _():
        goals[...] = target_swap[...]

    @pl.when(jnp.logical_not(moved))
    def _():
        goals[...] = target[...]

    zero_rim(x_field, shape)
    zero_rim(g_field, shape)
    sums[...] = jnp.zeros_like(sums)
    blocks = inner_blocks(shape)
    forward_one(shape, table, field, tiles, weight_one, x_field, m_one)(blocks)
    through_two(
        shape, scale, table, x_field, tiles, weight_two, two_turned, readout, spread, m_two, gz_two,
        g_field, preds, sums,
    )(blocks, messages(table, x_field, tiles, blocks, shape), columns_of(goals, blocks))
    goal_columns[...] = columns_of(goals, edge_blocks(shape))
    local[...] = products(table, x_field, tiles, edge_blocks(shape), shape)


def second_edge_kernel(shape, scale, table, outer, inner, side, tiles, weight, weight_turned, readout, spread, goal_columns,
                       x_field, local, m_in, gz_in, g_in, preds_in, sums_in,
                       m_two, gz_two, g_field, preds, sums, outer_out, inner_out, side_out):
    m = (local[...] + rim_terms(table, tiles, outer, inner, side, shape)).astype(BF16)
    through_two(
        shape, scale, table, x_field, tiles, weight, weight_turned, readout, spread, m_two, gz_two,
        g_field, preds, sums,
    )(edge_blocks(shape), m, goal_columns[...])
    take_edges(g_field, outer_out, inner_out, side_out, shape)


def back_inner_kernel(shape, scale, table, g_field, tiles, weight, readout, goals, preds, m_one, m_two, gz_two,
                      first_out, second_out, local, slopes, m_turned):
    nodes, rows, cols = shape
    blocks = inner_blocks(shape)
    gx, slope = back_terms(scale, weight, readout, goals, preds, m_one, blocks, nodes)
    gz = ((gx + products(table, g_field, tiles, blocks, shape)) * slope).astype(BF16)
    first_out[...] = over_nodes(gather(lambda row, col: m_one[row, at_block(col, nodes)], blocks), gz)
    gx, slope = back_terms(scale, weight, readout, goals, preds, m_one, edge_blocks(shape), nodes)
    local[...] = gx + products(table, g_field, tiles, edge_blocks(shape), shape)
    slopes[...] = slope
    m_turned[...] = gather(lambda row, col: m_one[row, at_block(col, nodes)], edge_blocks(shape)).T
    second_out[...] = jnp.zeros_like(second_out)

    def each_row(row, carry):
        second_out[...] += over_nodes(m_two[row], gz_two[row])
        return carry

    lax.fori_loop(0, rows, each_row, 0)


def back_edge_kernel(shape, table, outer, inner, side, tiles, preds, m_turned, first_in, second, sums, local, slopes,
                     keep, one, parts):
    width = first_in.shape[1]
    gx = local[...] + rim_terms(table, tiles, outer, inner, side, shape)
    gz = (gx * slopes[...]).astype(BF16)
    first = first_in[...] + jnp.dot(m_turned[...], gz, preferred_element_type=F32)
    count, size, _ = parts.shape
    parts[:, : size // 2] = first.reshape(count, size // 2, width)
    parts[:, size // 2 :] = second[...].reshape(count, size // 2, width)
    spread_shares(parts, sums[...], lax.axis_index("narrow"), (keep, one))
    ride_preds(preds, one)


def spread_shares(parts, extra, digit, outs):
    size, radix = parts.shape[1], len(outs)
    groups = parts.shape[0] // radix
    for k, out in enumerate(outs):
        for group in range(groups):
            out[group * size : (group + 1) * size] = parts[radix * group + jnp.bitwise_xor(digit, k)]
        out[groups * size : groups * size + 8] = extra


def take_preds(preds, riding, pred_out):
    _, _, moved = place()
    start = riding.shape[0] - preds.shape[0] * preds.shape[1] // 2

    @pl.when(moved)
    def _():
        for row in range(preds.shape[0]):
            at = start + row // 2 * preds.shape[1]
            lane = row % 2 * preds.shape[2]
            pred_out[row] = riding[at : at + preds.shape[1], lane : lane + preds.shape[2]]

    @pl.when(jnp.logical_not(moved))
    def _():
        pred_out[...] = preds[...]


def ride_preds(preds, riding):
    start = riding.shape[0] - preds.shape[0] * preds.shape[1] // 2
    for row in range(preds.shape[0]):
        at = start + row // 2 * preds.shape[1]
        lane = row % 2 * preds.shape[2]
        riding[at : at + preds.shape[1], lane : lane + preds.shape[2]] = preds[row]


def fold_kernel(base, step, radix, keep, *refs):
    *got, preds = refs[: -1 - radix - (step == 2)]
    outs, parts = list(refs[len(got) + 1 : -1]), refs[-1]
    if step == 2:
        take_preds(preds, got[0], outs.pop())
    count, size, _ = parts.shape
    total = keep[...]
    for one in got:
        total = total + one[: keep.shape[0]]
    parts[...] = total[: count * size].reshape(parts.shape)
    spread_shares(parts, total[count * size :], lax.rem(lax.axis_index(AXES) // base, radix), outs)
    if step == 1:
        riding = got[0].shape[0] - keep.shape[0]
        outs[1][outs[1].shape[0] - riding :] = got[0][keep.shape[0] :]


def last_fold_kernel(keep, *refs):
    *got, first, second, readout = refs
    share = first.shape[0]
    total = keep[...]
    for one in got:
        total = total + one[...]
    first[...] = total[:share]
    second[...] = total[share : 2 * share]
    readout[...] = total[2 * share :].sum(axis=0, keepdims=True)


def shares_shape(groups, size, width, radix, riding=0):
    rows = [groups * size + 8] * radix
    rows[1] += riding
    return tuple(jax.ShapeDtypeStruct((number, width), F32) for number in rows)


def sum_shares(outs, preds, count, share, width, riding, params):
    radices, left = [2, 4], count // 8
    while left > 1:
        radices.append(min(4, left))
        left //= radices[-1]
    base, groups, pred_out = 1, count // 2, None
    for step, radix in enumerate(radices):
        got = [
            lax.ppermute(outs[k], AXES, [(i, i ^ (k * base)) for i in range(count)]) for k in range(1, radix)
        ]
        if step == len(radices) - 1:
            break
        base *= radix
        radix = radices[step + 1]
        more = (jax.ShapeDtypeStruct(preds.shape, F32),) if step == 1 else ()
        shapes = shares_shape(groups // radix, 2 * share, width, radix, riding if step == 0 else 0) + more
        folded = pl.pallas_call(
            functools.partial(fold_kernel, base, step + 1, radix),
            out_shape=shapes,
            in_specs=[VMEM] * (2 + len(got)),
            out_specs=(VMEM,) * len(shapes),
            scratch_shapes=[pltpu.VMEM((groups, 2 * share, width), F32)],
            compiler_params=params,
            name="fold",
        )(outs[0], *got, preds)
        outs = folded[:radix]
        if more:
            pred_out = folded[-1]
        groups //= radix
    small = jax.ShapeDtypeStruct((share, width), F32)
    sums = pl.pallas_call(
        last_fold_kernel,
        out_shape=(small, small, jax.ShapeDtypeStruct((1, width), F32)),
        in_specs=[VMEM] * (1 + len(got)),
        out_specs=(VMEM,) * 3,
        compiler_params=params,
        name="last_fold",
    )(outs[0], *got)
    return *sums, pred_out


def per_device(features, tile_ids, tiles, w_first, w_second, readout, target):
    rows, cols, nodes, width = features.shape
    wide, narrow = lax.axis_size("wide"), lax.axis_size("narrow")
    count = wide * narrow
    line, step = cols * nodes, rows * cols
    swap, first_side, inner_way, outer_way, side_way, above_way = routes(wide)
    scale = float(np.sqrt(np.float32(width) / np.float32(rows * line * count)))
    params = pltpu.CompilerParams(vmem_limit_bytes=VMEM_LIMIT)

    def send(value, way):
        return lax.ppermute(value, AXES, way)

    def edges(outer, inner, side):
        return send(outer, outer_way), send(inner, inner_way), send(side, side_way)

    def bf(*shape):
        return jax.ShapeDtypeStruct(shape, BF16)

    def sems(number):
        return pltpu.SemaphoreType.DMA((number,))

    features = features.reshape(rows, line, width)
    ends_s = features[0 :: rows - 1].reshape(2 * line, width)
    ends = send(ends_s, swap)
    side_s, numbers = pl.pallas_call(
        functools.partial(pack_kernel, nodes, cols),
        out_shape=(bf(rows * nodes + TAIL, width), bf(TAIL, width)),
        in_specs=[VMEM, ANY, ANY],
        out_specs=(VMEM,) * 2,
        scratch_shapes=[pltpu.VMEM((TAIL, width), F32), sems(rows)],
        compiler_params=params,
        name="pack",
    )(jnp.transpose(tile_ids, (2, 0, 1)).astype(F32), features, ends_s)
    side = send(side_s, first_side)
    middle_s = pl.pallas_call(
        middle_kernel,
        out_shape=bf((rows - 2) * line + TAIL, width),
        in_specs=[ANY, VMEM],
        out_specs=VMEM,
        scratch_shapes=[sems(rows - 2)],
        compiler_params=params,
        name="pack_middle",
    )(features, numbers)
    middle = send(middle_s, swap)
    tiles, w_first, w_second, _ = lax.optimization_barrier((tiles, w_first, w_second, middle_s))
    tiles, w_first, w_second, w_turned = pl.pallas_call(
        prepare_kernel,
        out_shape=(bf(2 * tiles.shape[0], nodes, nodes),) + (bf(width, width),) * 3,
        in_specs=[ANY] * 3,
        out_specs=(VMEM,) * 4,
        scratch_shapes=[sems(3)],
        compiler_params=params,
        name="prepare",
    )(tiles, w_first, w_second)
    spread = jnp.broadcast_to(readout[:, None], (width, 128))
    readout = readout[None]

    outer_s, inner_s = pl.pallas_call(
        pick_kernel,
        out_shape=(bf(line, width),) * 2,
        in_specs=[ANY, VMEM, ANY],
        out_specs=(VMEM,) * 2,
        scratch_shapes=[sems(4)],
        compiler_params=params,
        name="pick",
    )(features, ends, side)
    outer, inner = send(outer_s, outer_way), send(inner_s, inner_way)
    target_s, numbers_s, _ = lax.optimization_barrier((target, numbers, inner_s))
    goal_swap = send(target_s, swap)
    above = send(numbers_s, above_way)

    shape = (nodes, rows, cols)
    patch, padded = bf(rows, line, width), bf(rows + 2, line + 2 * nodes, width)
    edge_shapes = (bf(line, width), bf(line, width), bf(rows * nodes, width))
    square = jax.ShapeDtypeStruct((width, width), F32)
    sums_shape = jax.ShapeDtypeStruct((8, width), F32)
    goal_shape = jax.ShapeDtypeStruct(target.shape, F32)
    block = nodes * width
    edge, inside = 2 * cols + rows - 2, (rows - 2) * (cols - 1)

    def cost(products, denses):
        return pl.CostEstimate(
            flops=2 * block * (products * 6 * nodes + denses * width),
            bytes_accessed=4 * block * (products + denses),
            transcendentals=block * products,
        )

    table, f_field, x_field, m_one, outer_s, inner_s, side_s = pl.pallas_call(
        functools.partial(first_edge_kernel, shape),
        out_shape=(jax.ShapeDtypeStruct((5 * rows, 128), jnp.int32), padded, padded, patch) + edge_shapes,
        in_specs=[VMEM] * 8 + [ANY] + [VMEM] * 2,
        out_specs=(SMEM,) + (VMEM,) * 6,
        scratch_shapes=[
            pltpu.VMEM((TAIL, width), F32),
            pltpu.VMEM((TAIL, width), F32),
            pltpu.VMEM((5 * rows, 128), jnp.int32),
            sems(1),
        ],
        compiler_params=params,
        cost_estimate=cost(edge, edge),
        name="first_edge",
    )(numbers, above, features, ends, middle, outer, inner, side, goal_swap, tiles, w_first)

    outer, inner, side = edges(outer_s, inner_s, side_s)
    edge_terms = jax.ShapeDtypeStruct((edge * nodes, width), F32)
    x_field, m_one, m_two, gz_two, g_field, preds, goals, sums, local, goal_columns = pl.pallas_call(
        functools.partial(middle_compute_kernel, shape, scale),
        out_shape=(padded, patch, patch, patch, padded, goal_shape, goal_shape, sums_shape, edge_terms,
                   jax.ShapeDtypeStruct((edge * nodes, 128), F32)),
        in_specs=[SMEM] + [VMEM] * 11,
        out_specs=(VMEM,) * 10,
        input_output_aliases={10: 0, 11: 1},
        compiler_params=params,
        cost_estimate=cost(2 * inside + edge, 3 * inside),
        name="inner_forward",
    )(table, f_field, tiles, w_first, w_second, w_turned, readout, spread, target, goal_swap, x_field, m_one)

    m_two, gz_two, g_field, preds, sums, outer_s, inner_s, side_s = pl.pallas_call(
        functools.partial(second_edge_kernel, shape, scale),
        out_shape=(patch, patch, padded, goal_shape, sums_shape) + edge_shapes,
        in_specs=[SMEM] + [VMEM] * 16,
        out_specs=(VMEM,) * 8,
        input_output_aliases={12 + i: i for i in range(5)},
        compiler_params=params,
        cost_estimate=cost(edge // 4, 2 * edge),
        name="second_edge",
    )(table, outer, inner, side, tiles, w_second, w_turned, readout, spread, goal_columns, x_field, local,
      m_two, gz_two, g_field, preds, sums)

    outer, inner, side = edges(outer_s, inner_s, side_s)
    first, second, local, slopes, m_turned = pl.pallas_call(
        functools.partial(back_inner_kernel, shape, scale),
        out_shape=(square, square, edge_terms, edge_terms, bf(width, edge * nodes)),
        in_specs=[SMEM] + [VMEM] * 9,
        out_specs=(VMEM,) * 5,
        compiler_params=params,
        cost_estimate=cost(rows * cols, 3 * rows * cols),
        name="back_inner",
    )(table, g_field, tiles, w_first, readout, goals, preds, m_one, m_two, gz_two)

    share, riding = width // count, step * nodes // width
    outs = pl.pallas_call(
        functools.partial(back_edge_kernel, shape),
        out_shape=shares_shape(count // 2, 2 * share, width, 2, riding),
        in_specs=[SMEM] + [VMEM] * 11,
        out_specs=(VMEM,) * 2,
        scratch_shapes=[pltpu.VMEM((count, 2 * share, width), F32)],
        compiler_params=params,
        cost_estimate=cost(edge // 4, edge),
        name="back_edge",
    )(table, outer, inner, side, tiles, preds, m_turned, first, second, sums, local, slopes)
    first, second, extra, pred_out = sum_shares(outs, preds, count, share, width, riding, params)
    return pred_out, first, second, extra[0]


def solution(mesh):
    in_specs = (
        P(("groups", "wide"), "narrow", None, None),
        P(("groups", "wide"), "narrow", None),
        P(),
        P(),
        P(),
        P(),
        P(("groups", "wide"), "narrow", None),
    )
    out_specs = (
        P(("groups", "wide"), "narrow", None),
        P(("groups", "wide", "narrow"), None),
        P(("groups", "wide", "narrow"), None),
        P("groups"),
    )
    return jax.shard_map(
        per_device, mesh=mesh, in_specs=in_specs, out_specs=out_specs, check_vma=False
    )
```

```python
import functools

import jax
import jax.numpy as jnp
import numpy as np
from jax import lax
from jax.experimental import pallas as pl
from jax.experimental.pallas import tpu as pltpu
from jax.sharding import PartitionSpec as P

F32 = jnp.float32
BF16 = jnp.bfloat16
AXES = ("wide", "narrow")
VMEM_LIMIT = 16 * 1024 * 1024
ANY = pl.BlockSpec(memory_space=pl.ANY)
VMEM = pl.BlockSpec(memory_space=pltpu.VMEM)
SMEM = pl.BlockSpec(memory_space=pltpu.SMEM)

SELF, EAST, WEST, NORTH, SOUTH = 0, 1, 2, 3, 4
TAIL = 16


def routes(wide):
    depth = wide // 2

    def at(z, y, c):
        return (2 * z + y) * 2 + c

    every = [(z, y, c) for z in range(depth) for y in range(2) for c in range(2)]
    swap = [(at(z, c, y), at(z, y, c)) for z, y, c in every if y != c]
    first_side = [(at(z, c, 1 - y), at(z, y, c)) for z, y, c in every]
    inner = [(at(z, y, 1 - c), at(z, y, c)) for z, y, c in every]
    outer = [(at(z - 1, y, 1), at(z, y, 0)) for z, y, c in every if c == 0 and z > 0]
    outer += [(at(z + 1, y, 0), at(z, y, 1)) for z, y, c in every if c == 1 and z + 1 < depth]
    side = [(at(z, 1 - y, c), at(z, y, c)) for z, y, c in every]
    above = [(at(z, 0, y), at(z, y, 1)) for z, y, c in every if c == 1]
    above += [(at(z - 1, 1, y), at(z, y, 0)) for z, y, c in every if c == 0 and z > 0]
    return swap, first_side, inner, outer, side, above


def place():
    half = lax.axis_index("narrow")
    side = lax.rem(lax.axis_index("wide"), 2)
    return half, side, half != side


def start_all(pairs, sems, first=0):
    copies = [pltpu.make_async_copy(a, b, sems.at[first + i]) for i, (a, b) in enumerate(pairs)]
    for copy in copies:
        copy.start()
    return copies


def wait_all(copies):
    for copy in copies:
        copy.wait()


def at_block(col, nodes):
    return pl.ds(col * nodes if isinstance(col, int) else pl.multiple_of(col * nodes, nodes), nodes)


def block_product(table, field, tiles, row, col, shape):
    nodes, rows, cols = shape

    def number(kind):
        return table[kind * rows + row, col]

    def block(r, c):
        return field[r, at_block(c, nodes)]

    half = tiles.shape[0] // 2
    lhs = jnp.concatenate(
        [
            tiles[number(SELF)],
            tiles[half + number(SELF)],
            tiles[number(EAST)],
            tiles[half + number(WEST)],
            tiles[number(NORTH)],
            tiles[half + number(SOUTH)],
        ],
        axis=1,
    )
    centre = block(row + 1, col + 1)
    rhs = jnp.concatenate(
        [
            centre,
            centre,
            block(row + 2, col + 1),
            block(row, col + 1),
            block(row + 1, col + 2),
            block(row + 1, col),
        ],
        axis=0,
    )
    return jnp.dot(lhs, rhs, preferred_element_type=F32)


def edge_blocks(shape):
    _, rows, cols = shape
    half, right, _ = place()
    outer, inner = jnp.where(half == 0, 0, rows - 1), jnp.where(half == 0, rows - 1, 0)
    beside = jnp.where(right == 0, cols - 1, 0)
    blocks = [(outer, col) for col in range(cols)] + [(inner, col) for col in range(cols)]
    return blocks + [(row, beside) for row in range(1, rows - 1)]


def inner_blocks(shape):
    _, rows, cols = shape
    _, right, _ = place()
    return [(row, right + col) for row in range(1, rows - 1) for col in range(cols - 1)]


def gather(read, blocks):
    return jnp.concatenate([read(row, col) for row, col in blocks], axis=0)


def scatter(ref, blocks, value, nodes, shift):
    for k, (row, col) in enumerate(blocks):
        ref[row + shift, at_block(col + shift, nodes)] = value[k * nodes : (k + 1) * nodes]


def messages(table, field, tiles, blocks, shape):
    return gather(
        lambda row, col: block_product(table, field, tiles, row, col, shape).astype(BF16), blocks
    )


def rim_terms(table, tiles, outer, inner, side, shape):
    nodes, rows, cols = shape
    half, right, _ = place()
    turned = tiles.shape[0] // 2

    def product(tile, block):
        return jnp.dot(tiles[tile], block, preferred_element_type=F32)

    def beside(row):
        tile = jnp.where(right == 0, table[NORTH * rows + row, cols - 1], turned + table[SOUTH * rows + row, 0])
        return product(tile, side[at_block(row, nodes)])

    terms = []
    first, last = jnp.where(half == 0, 0, rows - 1), jnp.where(half == 0, rows - 1, 0)
    for line, row, upward in ((outer, first, half == 0), (inner, last, half == 1)):
        corner = beside(row)
        for col in range(cols):
            tile = jnp.where(upward, turned + table[WEST * rows + row, col], table[EAST * rows + row, col])
            term = product(tile, line[at_block(col, nodes)])
            if col in (0, cols - 1):
                term = term + jnp.where((right == 0) == (col > 0), corner, 0.0)
            terms.append(term)
    return jnp.concatenate(terms + [beside(row) for row in range(1, rows - 1)], axis=0)


def products(table, field, tiles, blocks, shape):
    return gather(lambda row, col: block_product(table, field, tiles, row, col, shape), blocks)


def forward_one(shape, table, field, tiles, weight, x_field, m_all):
    nodes = shape[0]

    def body(blocks):
        m = messages(table, field, tiles, blocks, shape)
        scatter(m_all, blocks, m, nodes, 0)
        z = jnp.dot(m, weight[...], preferred_element_type=F32)
        base = gather(lambda row, col: field[row + 1, at_block(col + 1, nodes)], blocks)
        scatter(x_field, blocks, (base.astype(F32) + jnp.tanh(z)).astype(BF16), nodes, 1)

    return body


def residual_columns(seen, goal, scale):
    gp = (seen - goal) * scale
    column = jnp.broadcast_to(gp, (gp.shape[1], gp.shape[1])).T
    return jnp.concatenate([column, column], axis=1)


def columns_of(goals, blocks):
    rows = [goals[row, pl.ds(col, 1)] for row, col in blocks]
    nodes = rows[0].shape[1]
    turned = jnp.concatenate(rows + [jnp.zeros((nodes - len(rows), nodes), F32)], axis=0).T
    return jnp.concatenate(
        [jnp.broadcast_to(turned[:, k : k + 1], (nodes, nodes)) for k in range(len(rows))], axis=0
    )


def through_two(shape, scale, table, field, tiles, weight, weight_turned, readout, spread, m_all, gz_all, g_field, preds, sums):
    nodes = shape[0]
    readf = readout[...].astype(F32)

    def body(blocks, m, goal_columns):
        scatter(m_all, blocks, m, nodes, 0)
        t = jnp.tanh(jnp.dot(m, weight[...], preferred_element_type=F32))
        base = gather(lambda row, col: field[row + 1, at_block(col + 1, nodes)], blocks)
        x = (base.astype(F32) + t).astype(BF16)
        seen = jnp.dot(x, spread[...], preferred_element_type=F32)
        lanes = lax.broadcasted_iota(jnp.int32, (nodes, 128), 1)
        packed = jnp.zeros((nodes, 128), F32)
        for k in range(len(blocks)):
            packed = jnp.where(lanes == k, seen[k * nodes : (k + 1) * nodes], packed)
        packed = packed.T
        for k, (row, col) in enumerate(blocks):
            preds[row, pl.ds(col, 1)] = packed[k : k + 1]
        gp = (seen - goal_columns) * scale
        gp = jnp.concatenate([gp, gp], axis=1)
        sums[...] += (x.astype(F32) * gp).reshape(gp.shape[0] // 8, 8, gp.shape[1]).sum(axis=0)
        gz = (gp * readf * (1.0 - t * t)).astype(BF16)
        scatter(gz_all, blocks, gz, nodes, 0)
        g = jnp.dot(gz, weight_turned[...], preferred_element_type=F32).astype(BF16)
        scatter(g_field, blocks, g, nodes, 1)

    return body


def back_terms(scale, weight, readout, goals, preds, m_all, blocks, nodes):
    m = gather(lambda row, col: m_all[row, at_block(col, nodes)], blocks)
    t = jnp.tanh(jnp.dot(m, weight[...], preferred_element_type=F32))
    gp = gather(
        lambda row, col: residual_columns(preds[row, pl.ds(col, 1)], goals[row, pl.ds(col, 1)], scale), blocks
    )
    return gp * readout[...].astype(F32), 1.0 - t * t


def over_nodes(left, right):
    return lax.dot_general(left, right, (((0,), (0,)), ((), ())), preferred_element_type=F32)


def zero_rim(field, shape):
    nodes, rows, cols = shape
    field[0] = jnp.zeros(field.shape[1:], field.dtype)
    field[rows + 1] = jnp.zeros(field.shape[1:], field.dtype)
    for row in range(1, rows + 1):
        for col in (0, cols + 1):
            field[row, at_block(col, nodes)] = jnp.zeros((nodes, field.shape[2]), field.dtype)


def take_edges(field, outer, inner, side, shape):
    nodes, rows, cols = shape
    half, right, _ = place()
    inside = pl.ds(nodes, cols * nodes)
    outer[...] = field[jnp.where(half == 0, 1, rows), inside]
    inner[...] = field[jnp.where(half == 0, rows, 1), inside]
    column = at_block(jnp.where(right == 0, cols, 1), nodes)
    for row in range(rows):
        side[at_block(row, nodes)] = field[row + 1, column]


def fill_rim(field, outer, inner, side, shape):
    nodes, rows, cols = shape
    half, right, _ = place()
    inside = pl.ds(nodes, cols * nodes)
    line = pl.ds(0, cols * nodes)
    field[jnp.where(half == 0, 0, rows + 1), inside] = outer[line]
    field[jnp.where(half == 0, rows + 1, 0), inside] = inner[line]
    empty, column = jnp.where(right == 0, 0, cols + 1), jnp.where(right == 0, cols + 1, 0)
    for row in range(rows):
        field[row + 1, at_block(empty, nodes)] = jnp.zeros((nodes, field.shape[2]), field.dtype)
        field[row + 1, at_block(column, nodes)] = side[at_block(row, nodes)]


def pack_kernel(nodes, cols, ids, own, after, side, numbers, wide_ids, sems):
    rows = own.shape[0]
    half, _, _ = place()
    col = pl.multiple_of(jnp.where(half == 1, 0, (cols - 1) * nodes), nodes)
    copies = start_all(
        [(own.at[row, pl.ds(col, nodes)], side.at[pl.ds(row * nodes, nodes)]) for row in range(rows)], sems
    )
    wide_ids[...] = jnp.zeros_like(wide_ids)
    for kind in range(3):
        wide_ids[kind * rows : (kind + 1) * rows, 0:cols] = ids[kind]
    tail = wide_ids[...].astype(BF16)
    numbers[...] = tail
    side[rows * nodes :] = tail
    wait_all(copies)


def middle_kernel(own, numbers, middle, sems):
    rows, line = own.shape[0], own.shape[1]
    copies = start_all([(own.at[row + 1], middle.at[pl.ds(row * line, line)]) for row in range(rows - 2)], sems)
    middle[(rows - 2) * line :] = numbers[...]
    wait_all(copies)


def prepare_kernel(tiles, first, second, both, first_in, second_in, second_turned, sems):
    number = tiles.shape[0]
    wait_all(start_all([(tiles, both.at[pl.ds(0, number)]), (first, first_in), (second, second_in)], sems))

    second_turned[...] = second_in[...].T

    def one_tile(tile, carry):
        both[number + tile] = both[tile].T
        return carry

    lax.fori_loop(0, number, one_tile, 0)


def pick_kernel(own, ends, after, outer, inner, sems):
    rows, line = own.shape[0], own.shape[1]
    half, _, moved = place()

    @pl.when(moved)
    def _():
        outer[...] = ends[pl.ds(pl.multiple_of(half * line, line), line)]
        inner[...] = ends[pl.ds(pl.multiple_of((1 - half) * line, line), line)]

    @pl.when(jnp.logical_not(moved))
    def _():
        wait_all(start_all([
            (own.at[jnp.where(half == 0, 0, rows - 1)], outer),
            (own.at[jnp.where(half == 0, rows - 1, 0)], inner),
        ], sems))


def first_edge_kernel(shape, numbers, above, own, ends, middle, outer, inner, side, later, tiles, weight,
                      spots, field, x_field, m_all, outer_out, inner_out, side_out, own_ids, above_ids, table, sems):
    nodes, rows, cols = shape
    line = cols * nodes
    _, _, moved = place()
    inside = pl.ds(nodes, line)
    @pl.when(moved)
    def _():
        own_ids[...] = middle[pl.ds((rows - 2) * line, TAIL)].astype(F32)

    @pl.when(jnp.logical_not(moved))
    def _():
        own_ids[...] = numbers[...].astype(F32)

    above_ids[...] = above[...].astype(F32)
    left = side[pl.ds(rows * nodes, TAIL)].astype(F32)[2 * rows : 3 * rows, 0:128]
    north = own_ids[2 * rows : 3 * rows, 0:128]
    lanes = lax.broadcasted_iota(jnp.int32, north.shape, 1)
    beside = jnp.broadcast_to(left[:, cols - 1 : cols], left.shape)
    spots[0 : 2 * rows] = own_ids[0 : 2 * rows, 0:128].astype(jnp.int32)
    spots[WEST * rows : WEST * rows + 1] = above_ids[2 * rows - 1 : 2 * rows, 0:128].astype(jnp.int32)
    spots[WEST * rows + 1 : (WEST + 1) * rows] = own_ids[rows : 2 * rows - 1, 0:128].astype(jnp.int32)
    spots[NORTH * rows : (NORTH + 1) * rows] = north.astype(jnp.int32)
    spots[SOUTH * rows : (SOUTH + 1) * rows] = jnp.where(lanes == 0, beside, pltpu.roll(north, 1, 1)).astype(jnp.int32)
    copies = start_all([(spots, table)], sems)

    @pl.when(moved)
    def _():
        field[1, inside] = ends[pl.ds(0, line)]
        field[rows, inside] = ends[pl.ds(line, line)]
        for row in range(2, rows):
            field[row, inside] = middle[pl.ds((row - 2) * line, line)]

    @pl.when(jnp.logical_not(moved))
    def _():
        for row in range(rows):
            field[row + 1, inside] = own[row]

    fill_rim(field, outer, inner, side, shape)
    wait_all(copies)
    forward_one(shape, table, field, tiles, weight, x_field, m_all)(edge_blocks(shape))
    take_edges(x_field, outer_out, inner_out, side_out, shape)


def middle_compute_kernel(shape, scale, table, field, tiles, weight_one, weight_two, two_turned, readout, spread, target,
                          target_swap, x_in, m_in, x_field, m_one, m_two, gz_two, g_field, preds, goals, sums, local, goal_columns):
    _, _, moved = place()

    @pl.when(moved)
    def _():
        goals[...] = target_swap[...]

    @pl.when(jnp.logical_not(moved))
    def _():
        goals[...] = target[...]

    zero_rim(x_field, shape)
    zero_rim(g_field, shape)
    sums[...] = jnp.zeros_like(sums)
    blocks = inner_blocks(shape)
    forward_one(shape, table, field, tiles, weight_one, x_field, m_one)(blocks)
    through_two(
        shape, scale, table, x_field, tiles, weight_two, two_turned, readout, spread, m_two, gz_two,
        g_field, preds, sums,
    )(blocks, messages(table, x_field, tiles, blocks, shape), columns_of(goals, blocks))
    goal_columns[...] = columns_of(goals, edge_blocks(shape))
    local[...] = products(table, x_field, tiles, edge_blocks(shape), shape)


def second_edge_kernel(shape, scale, table, outer, inner, side, tiles, weight, weight_turned, readout, spread, goal_columns,
                       x_field, local, m_in, gz_in, g_in, preds_in, sums_in,
                       m_two, gz_two, g_field, preds, sums, outer_out, inner_out, side_out):
    m = (local[...] + rim_terms(table, tiles, outer, inner, side, shape)).astype(BF16)
    through_two(
        shape, scale, table, x_field, tiles, weight, weight_turned, readout, spread, m_two, gz_two,
        g_field, preds, sums,
    )(edge_blocks(shape), m, goal_columns[...])
    take_edges(g_field, outer_out, inner_out, side_out, shape)


def back_inner_kernel(shape, scale, table, g_field, tiles, weight, readout, goals, preds, m_one, m_two, gz_two,
                      first_out, second_out, local, slopes, m_turned):
    nodes, rows, cols = shape
    blocks = inner_blocks(shape)
    gx, slope = back_terms(scale, weight, readout, goals, preds, m_one, blocks, nodes)
    gz = ((gx + products(table, g_field, tiles, blocks, shape)) * slope).astype(BF16)
    first_out[...] = over_nodes(gather(lambda row, col: m_one[row, at_block(col, nodes)], blocks), gz)
    gx, slope = back_terms(scale, weight, readout, goals, preds, m_one, edge_blocks(shape), nodes)
    local[...] = gx + products(table, g_field, tiles, edge_blocks(shape), shape)
    slopes[...] = slope
    m_turned[...] = gather(lambda row, col: m_one[row, at_block(col, nodes)], edge_blocks(shape)).T
    second_out[...] = jnp.zeros_like(second_out)

    def each_row(row, carry):
        second_out[...] += over_nodes(m_two[row], gz_two[row])
        return carry

    lax.fori_loop(0, rows, each_row, 0)


def back_edge_kernel(shape, table, outer, inner, side, tiles, preds, m_turned, first_in, second, sums, local, slopes,
                     keep, one, parts):
    width = first_in.shape[1]
    gx = local[...] + rim_terms(table, tiles, outer, inner, side, shape)
    gz = (gx * slopes[...]).astype(BF16)
    first = first_in[...] + jnp.dot(m_turned[...], gz, preferred_element_type=F32)
    count, size, _ = parts.shape
    parts[:, : size // 2] = first.reshape(count, size // 2, width)
    parts[:, size // 2 :] = second[...].reshape(count, size // 2, width)
    spread_shares(parts, sums[...], lax.axis_index("narrow"), (keep, one))
    ride_preds(preds, one)


def spread_shares(parts, extra, digit, outs):
    size, radix = parts.shape[1], len(outs)
    groups = parts.shape[0] // radix
    for k, out in enumerate(outs):
        for group in range(groups):
            out[group * size : (group + 1) * size] = parts[radix * group + jnp.bitwise_xor(digit, k)]
        out[groups * size : groups * size + 8] = extra


def take_preds(preds, riding, pred_out):
    _, _, moved = place()
    start = riding.shape[0] - preds.shape[0] * preds.shape[1] // 2

    @pl.when(moved)
    def _():
        for row in range(preds.shape[0]):
            at = start + row // 2 * preds.shape[1]
            lane = row % 2 * preds.shape[2]
            pred_out[row] = riding[at : at + preds.shape[1], lane : lane + preds.shape[2]]

    @pl.when(jnp.logical_not(moved))
    def _():
        pred_out[...] = preds[...]


def ride_preds(preds, riding):
    start = riding.shape[0] - preds.shape[0] * preds.shape[1] // 2
    for row in range(preds.shape[0]):
        at = start + row // 2 * preds.shape[1]
        lane = row % 2 * preds.shape[2]
        riding[at : at + preds.shape[1], lane : lane + preds.shape[2]] = preds[row]


def fold_kernel(base, step, radix, keep, *refs):
    *got, preds = refs[: -1 - radix - (step == 2)]
    outs, parts = list(refs[len(got) + 1 : -1]), refs[-1]
    if step == 2:
        take_preds(preds, got[0], outs.pop())
    count, size, _ = parts.shape
    total = keep[...]
    for one in got:
        total = total + one[: keep.shape[0]]
    parts[...] = total[: count * size].reshape(parts.shape)
    spread_shares(parts, total[count * size :], lax.rem(lax.axis_index(AXES) // base, radix), outs)
    if step == 1:
        riding = got[0].shape[0] - keep.shape[0]
        outs[1][outs[1].shape[0] - riding :] = got[0][keep.shape[0] :]


def last_fold_kernel(keep, *refs):
    *got, first, second, readout = refs
    share = first.shape[0]
    total = keep[...]
    for one in got:
        total = total + one[...]
    first[...] = total[:share]
    second[...] = total[share : 2 * share]
    readout[...] = total[2 * share :].sum(axis=0, keepdims=True)


def shares_shape(groups, size, width, radix, riding=0):
    rows = [groups * size + 8] * radix
    rows[1] += riding
    return tuple(jax.ShapeDtypeStruct((number, width), F32) for number in rows)


def sum_shares(outs, preds, count, share, width, riding, params):
    radices, left = [2, 4], count // 8
    while left > 1:
        radices.append(min(4, left))
        left //= radices[-1]
    base, groups, pred_out = 1, count // 2, None
    for step, radix in enumerate(radices):
        got = [
            lax.ppermute(outs[k], AXES, [(i, i ^ (k * base)) for i in range(count)]) for k in range(1, radix)
        ]
        if step == len(radices) - 1:
            break
        base *= radix
        radix = radices[step + 1]
        more = (jax.ShapeDtypeStruct(preds.shape, F32),) if step == 1 else ()
        shapes = shares_shape(groups // radix, 2 * share, width, radix, riding if step == 0 else 0) + more
        folded = pl.pallas_call(
            functools.partial(fold_kernel, base, step + 1, radix),
            out_shape=shapes,
            in_specs=[VMEM] * (2 + len(got)),
            out_specs=(VMEM,) * len(shapes),
            scratch_shapes=[pltpu.VMEM((groups, 2 * share, width), F32)],
            compiler_params=params,
            name="fold",
        )(outs[0], *got, preds)
        outs = folded[:radix]
        if more:
            pred_out = folded[-1]
        groups //= radix
    small = jax.ShapeDtypeStruct((share, width), F32)
    sums = pl.pallas_call(
        last_fold_kernel,
        out_shape=(small, small, jax.ShapeDtypeStruct((1, width), F32)),
        in_specs=[VMEM] * (1 + len(got)),
        out_specs=(VMEM,) * 3,
        compiler_params=params,
        name="last_fold",
    )(outs[0], *got)
    return *sums, pred_out


def per_device(features, tile_ids, tiles, w_first, w_second, readout, target):
    rows, cols, nodes, width = features.shape
    wide, narrow = lax.axis_size("wide"), lax.axis_size("narrow")
    count = wide * narrow
    line, step = cols * nodes, rows * cols
    swap, first_side, inner_way, outer_way, side_way, above_way = routes(wide)
    scale = float(np.sqrt(np.float32(width) / np.float32(rows * line * count)))
    params = pltpu.CompilerParams(vmem_limit_bytes=VMEM_LIMIT)

    def send(value, way):
        return lax.ppermute(value, AXES, way)

    def edges(outer, inner, side):
        return send(outer, outer_way), send(inner, inner_way), send(side, side_way)

    def bf(*shape):
        return jax.ShapeDtypeStruct(shape, BF16)

    def sems(number):
        return pltpu.SemaphoreType.DMA((number,))

    features = features.reshape(rows, line, width)
    ends_s = features[0 :: rows - 1].reshape(2 * line, width)
    ends = send(ends_s, swap)
    side_s, numbers = pl.pallas_call(
        functools.partial(pack_kernel, nodes, cols),
        out_shape=(bf(rows * nodes + TAIL, width), bf(TAIL, width)),
        in_specs=[VMEM, ANY, ANY],
        out_specs=(VMEM,) * 2,
        scratch_shapes=[pltpu.VMEM((TAIL, width), F32), sems(rows)],
        compiler_params=params,
        name="pack",
    )(jnp.transpose(tile_ids, (2, 0, 1)).astype(F32), features, ends_s)
    side = send(side_s, first_side)
    middle_s = pl.pallas_call(
        middle_kernel,
        out_shape=bf((rows - 2) * line + TAIL, width),
        in_specs=[ANY, VMEM],
        out_specs=VMEM,
        scratch_shapes=[sems(rows - 2)],
        compiler_params=params,
        name="pack_middle",
    )(features, numbers)
    middle = send(middle_s, swap)
    tiles, w_first, w_second, _ = lax.optimization_barrier((tiles, w_first, w_second, middle_s))
    tiles, w_first, w_second, w_turned = pl.pallas_call(
        prepare_kernel,
        out_shape=(bf(2 * tiles.shape[0], nodes, nodes),) + (bf(width, width),) * 3,
        in_specs=[ANY] * 3,
        out_specs=(VMEM,) * 4,
        scratch_shapes=[sems(3)],
        compiler_params=params,
        name="prepare",
    )(tiles, w_first, w_second)
    spread = jnp.broadcast_to(readout[:, None], (width, 128))
    readout = readout[None]

    outer_s, inner_s = pl.pallas_call(
        pick_kernel,
        out_shape=(bf(line, width),) * 2,
        in_specs=[ANY, VMEM, ANY],
        out_specs=(VMEM,) * 2,
        scratch_shapes=[sems(4)],
        compiler_params=params,
        name="pick",
    )(features, ends, side)
    outer, inner = send(outer_s, outer_way), send(inner_s, inner_way)
    target_s, numbers_s, _ = lax.optimization_barrier((target, numbers, inner_s))
    goal_swap = send(target_s, swap)
    above = send(numbers_s, above_way)

    shape = (nodes, rows, cols)
    patch, padded = bf(rows, line, width), bf(rows + 2, line + 2 * nodes, width)
    edge_shapes = (bf(line, width), bf(line, width), bf(rows * nodes, width))
    square = jax.ShapeDtypeStruct((width, width), F32)
    sums_shape = jax.ShapeDtypeStruct((8, width), F32)
    goal_shape = jax.ShapeDtypeStruct(target.shape, F32)
    block = nodes * width
    edge, inside = 2 * cols + rows - 2, (rows - 2) * (cols - 1)

    def cost(products, denses):
        return pl.CostEstimate(
            flops=2 * block * (products * 6 * nodes + denses * width),
            bytes_accessed=4 * block * (products + denses),
            transcendentals=block * products,
        )

    table, f_field, x_field, m_one, outer_s, inner_s, side_s = pl.pallas_call(
        functools.partial(first_edge_kernel, shape),
        out_shape=(jax.ShapeDtypeStruct((5 * rows, 128), jnp.int32), padded, padded, patch) + edge_shapes,
        in_specs=[VMEM] * 8 + [ANY] + [VMEM] * 2,
        out_specs=(VMEM,) * 7,
        scratch_shapes=[
            pltpu.VMEM((TAIL, width), F32),
            pltpu.VMEM((TAIL, width), F32),
            pltpu.SMEM((5 * rows, 128), jnp.int32),
            sems(1),
        ],
        compiler_params=params,
        cost_estimate=cost(edge, edge),
        name="first_edge",
    )(numbers, above, features, ends, middle, outer, inner, side, goal_swap, tiles, w_first)

    outer, inner, side = edges(outer_s, inner_s, side_s)
    edge_terms = jax.ShapeDtypeStruct((edge * nodes, width), F32)
    x_field, m_one, m_two, gz_two, g_field, preds, goals, sums, local, goal_columns = pl.pallas_call(
        functools.partial(middle_compute_kernel, shape, scale),
        out_shape=(padded, patch, patch, patch, padded, goal_shape, goal_shape, sums_shape, edge_terms,
                   jax.ShapeDtypeStruct((edge * nodes, 128), F32)),
        in_specs=[SMEM] + [VMEM] * 11,
        out_specs=(VMEM,) * 10,
        input_output_aliases={10: 0, 11: 1},
        compiler_params=params,
        cost_estimate=cost(2 * inside + edge, 3 * inside),
        name="inner_forward",
    )(table, f_field, tiles, w_first, w_second, w_turned, readout, spread, target, goal_swap, x_field, m_one)

    m_two, gz_two, g_field, preds, sums, outer_s, inner_s, side_s = pl.pallas_call(
        functools.partial(second_edge_kernel, shape, scale),
        out_shape=(patch, patch, padded, goal_shape, sums_shape) + edge_shapes,
        in_specs=[SMEM] + [VMEM] * 16,
        out_specs=(VMEM,) * 8,
        input_output_aliases={12 + i: i for i in range(5)},
        compiler_params=params,
        cost_estimate=cost(edge // 4, 2 * edge),
        name="second_edge",
    )(table, outer, inner, side, tiles, w_second, w_turned, readout, spread, goal_columns, x_field, local,
      m_two, gz_two, g_field, preds, sums)

    outer, inner, side = edges(outer_s, inner_s, side_s)
    first, second, local, slopes, m_turned = pl.pallas_call(
        functools.partial(back_inner_kernel, shape, scale),
        out_shape=(square, square, edge_terms, edge_terms, bf(width, edge * nodes)),
        in_specs=[SMEM] + [VMEM] * 9,
        out_specs=(VMEM,) * 5,
        compiler_params=params,
        cost_estimate=cost(rows * cols, 3 * rows * cols),
        name="back_inner",
    )(table, g_field, tiles, w_first, readout, goals, preds, m_one, m_two, gz_two)

    share, riding = width // count, step * nodes // width
    outs = pl.pallas_call(
        functools.partial(back_edge_kernel, shape),
        out_shape=shares_shape(count // 2, 2 * share, width, 2, riding),
        in_specs=[SMEM] + [VMEM] * 11,
        out_specs=(VMEM,) * 2,
        scratch_shapes=[pltpu.VMEM((count, 2 * share, width), F32)],
        compiler_params=params,
        cost_estimate=cost(edge // 4, edge),
        name="back_edge",
    )(table, outer, inner, side, tiles, preds, m_turned, first, second, sums, local, slopes)
    first, second, extra, pred_out = sum_shares(outs, preds, count, share, width, riding, params)
    return pred_out, first, second, extra[0]


def solution(mesh):
    in_specs = (
        P(("groups", "wide"), "narrow", None, None),
        P(("groups", "wide"), "narrow", None),
        P(),
        P(),
        P(),
        P(),
        P(("groups", "wide"), "narrow", None),
    )
    out_specs = (
        P(("groups", "wide"), "narrow", None),
        P(("groups", "wide", "narrow"), None),
        P(("groups", "wide", "narrow"), None),
        P("groups"),
    )
    return jax.shard_map(
        per_device, mesh=mesh, in_specs=in_specs, out_specs=out_specs, check_vma=False
    )
```
